32 devices in a mesh: seq: 4 (over y, x), wshard: 8 (over z, core).
Axes of the slice: x: 2, y: 2, z: 4, core: 2. Of those that a mesh axis runs over, the one named last changes fastest.
Arguments:
- tokens: bfloat16 [8, 3072, 768], P('wshard', 'seq'), may hold values from -6 to 6
- teacher: bfloat16 [8, 3072, 768], P('wshard', 'seq'), may hold values from -6 to 6
- lengths: int32 [8, 4], P('wshard'), may hold values from 128 to 512, as said below
- w_query: bfloat16 [768, 768], P('wshard'), may hold values from -0.0546875 to 0.0546875
- w_key: bfloat16 [768, 768], P('wshard'), may hold values from -0.21875 to 0.21875
- w_value: bfloat16 [768, 768], P('wshard'), may hold values from -0.21875 to 0.21875
- w_out: bfloat16 [768, 768], P('wshard'), may hold values from -0.625 to 0.625
- w_in: bfloat16 [768, 3072], P('wshard'), may hold values from -0.21875 to 0.21875
- w_ff: bfloat16 [3072, 768], P('wshard'), may hold values from -0.15625 to 0.15625
- gain_attn: bfloat16 [768], P('wshard'), may hold values from 0.5 to 1.5
- gain_ff: bfloat16 [768], P('wshard'), may hold values from 0.5 to 1.5
- bias_table: bfloat16 [32, 12], replicated, may hold values from -4 to 4
Outputs:
- output: bfloat16 [8, 3072, 768], P('wshard', 'seq')
- tokens_grad: float32 [8, 3072, 768], P('wshard', 'seq')
- w_query_grad: float32 [768, 768], P('wshard')
- w_key_grad: float32 [768, 768], P('wshard')
- w_value_grad: float32 [768, 768], P('wshard')
- w_out_grad: float32 [768, 768], P('wshard')
- w_in_grad: float32 [768, 3072], P('wshard')
- w_ff_grad: float32 [3072, 768], P('wshard')
- gain_attn_grad: float32 [768], P('wshard')
- gain_ff_grad: float32 [768], P('wshard')
- bias_table_grad: float32 [32, 12], replicated
The draws below stay inside these ranges and needn't reach their ends.
Inputs may be any that keep to these rules, and one draw needn't show every extreme that they name: `lengths`: in every group one of the 4 continuations, drawn at random, has exactly 512 valid tokens; the others have 512 // 4 or more.
All inputs are finite; a program needn't handle non-finite values.
Results may differ from the reference program's by a relative error of at most 0.025.
The reference program's roundings to bfloat16 on the way count: a program that leaves them out, or rounds other values in their place, can miss the bound.
Values may be sent and summed in bfloat16 or wider, within the bound.
No kernel may reach another device: no remote copies, remote signals or barrier semaphores. Data moves between devices by JAX's collectives and lax.ppermute only.
A program may use at most 192 MiB of HBM per device.

```python
import jax
import jax.numpy as jnp
from jax import lax

D = 768
H = 12
DH = 64
FF = 3072
NB = 32
PLEN = 1024
CLEN = 512
CONT = 4
NGROUP = 8
GTOK = 3072


def draw_lengths(key, part):
    spread_key = jax.random.fold_in(key, 11)
    choose_key = jax.random.fold_in(key, 23)
    drawn_lengths = jax.random.randint(spread_key, (NGROUP, CONT), CLEN // 4, CLEN + 1)
    chosen_slot = jax.random.randint(choose_key, (NGROUP, 1), 0, CONT)
    filled_slot = jnp.arange(CONT, dtype=jnp.int32)[None, :] == chosen_slot
    return jnp.where(filled_slot, CLEN, drawn_lengths).astype(jnp.int32)


def block_scale(stream_key, shape, pieces, least, largest):
    def one(axis_at, parts):
        draws = jax.random.uniform(jax.random.fold_in(jax.random.fold_in(stream_key, 6), axis_at), (parts,), jnp.float32, least / len(pieces), largest / len(pieces))
        return jnp.repeat(jnp.exp(draws), shape[axis_at] // parts).reshape((-1,) + (1,) * (len(shape) - axis_at - 1))

    factor_of = one(*pieces[0])
    for cut in pieces[1:]:
        factor_of = factor_of * one(*cut)
    return factor_of


def scatter_about(own_key, extent, spread, limit, split=(), held_as=jnp.bfloat16):
    factor_of = block_scale(own_key, extent, split, -0.22, 0.18) if split else 1.0
    array = jax.random.normal(own_key, extent, jnp.float32) * spread * factor_of
    return jnp.minimum(jnp.maximum(array, -limit), limit).astype(held_as)


def setup_inputs(seed: int = 0) -> dict:
    key_list = jax.random.split(jax.random.key(seed), 13)
    return {
        "tokens": scatter_about(key_list[0], (NGROUP, GTOK, D), 1.0, 6.0, ((0, 8), (1, 4))),
        "teacher": scatter_about(key_list[1], (NGROUP, GTOK, D), 1.0, 6.0, ((0, 8), (1, 4))),
        "lengths": draw_lengths(jax.random.fold_in(key_list[12], 71), 0),
        "w_query": scatter_about(key_list[3], (D, D), (16 * D) ** -0.5, 0.0546875, ((0, 8),)),
        "w_key": scatter_about(key_list[4], (D, D), D ** -0.5, 0.21875, ((0, 8),)),
        "w_value": scatter_about(key_list[5], (D, D), D ** -0.5, 0.21875, ((0, 8),)),
        "w_out": scatter_about(key_list[6], (D, D), (D // 8) ** -0.5, 0.625, ((0, 8),)),
        "w_in": scatter_about(key_list[7], (D, FF), D ** -0.5, 0.21875, ((0, 8),)),
        "w_ff": scatter_about(key_list[8], (FF, D), (FF // 2) ** -0.5, 0.15625, ((0, 8),)),
        "gain_attn": jnp.clip(1.0 + 0.1 * jax.random.normal(key_list[9], (D,), jnp.float32), 0.5, 1.5).astype(jnp.bfloat16),
        "gain_ff": jnp.clip(1.0 + 0.1 * jax.random.normal(key_list[10], (D,), jnp.float32), 0.5, 1.5).astype(jnp.bfloat16),
        "bias_table": scatter_about(key_list[11], (NB, H), 1.0, 4.0),
    }


EPSILON = 1e-06
NEGATIVE = -1e+30
THRESHOLDS = (12, 16, 23, 32, 46, 64, 91)
HIGHEST = lax.Precision.HIGHEST

@jax.custom_vjp
def low(v):
    return lax.optimization_barrier(v.astype(jnp.bfloat16)).astype(jnp.float32)

@jax.custom_vjp
def low_back(v):
    return v

def low_keep(v):
    return (low(v), None)

def low_pass(kept, grad):
    return (grad,)

def back_keep(v):
    return (v, None)

def back_low(kept, grad):
    return (low(grad),)
low.defvjp(low_keep, low_pass)
low_back.defvjp(back_keep, back_low)

def bucket_of(offset):
    magnitude = jnp.abs(offset)
    coarse = 8 + sum(((magnitude >= edge_value).astype(jnp.int32) for edge_value in THRESHOLDS))
    return jnp.where(offset > 0, NB // 2, 0) + jnp.where(magnitude < 8, magnitude, coarse)

def matmul(left, right):
    return jnp.dot(left, right, precision=HIGHEST)

def rms_scale(inputs, gain):
    return inputs * lax.rsqrt(lax.optimization_barrier(jnp.mean(inputs * inputs, axis=1, keepdims=True)) + EPSILON) * gain

def attend(queries, key_rows, value_rows, bias_table, first_pos, live_keys):
    height, breadth = (queries.shape[0], key_rows.shape[0])
    offsets = lax.iota(jnp.int32, breadth)[None, :] - (first_pos + lax.iota(jnp.int32, height))[:, None]
    bias_values = jnp.transpose(bias_table[bucket_of(offsets)], (2, 0, 1))
    scores = jnp.einsum('qhd,khd->hqk', queries, key_rows, precision=HIGHEST) + bias_values
    scores = low_back(scores)
    scores = jnp.where(live_keys[None, None, :], scores, NEGATIVE)
    shifted = jnp.exp(scores - lax.optimization_barrier(jnp.max(scores, axis=2, keepdims=True)))
    probs_low = low(shifted / lax.optimization_barrier(jnp.sum(shifted, axis=2, keepdims=True)))
    return jnp.einsum('hqk,khd->qhd', probs_low, value_rows, precision=HIGHEST)

def group_loss(params, inputs, targets, spans):
    w_query, w_key, w_value, w_out, w_in, w_ff, gain_attn, gain_ff, bias_table = params
    total_rows = inputs.shape[0]
    normed_one = low(rms_scale(inputs, gain_attn))
    queries = low(low_back(matmul(normed_one, w_query))).reshape(total_rows, H, DH)
    key_rows = low(low_back(matmul(normed_one, w_key))).reshape(total_rows, H, DH)
    value_rows = low(low_back(matmul(normed_one, w_value))).reshape(total_rows, H, DH)
    prompt_live = jnp.ones((PLEN,), jnp.bool_)
    prompt_out = attend(queries[:PLEN], key_rows[:PLEN], value_rows[:PLEN], bias_table, 0, prompt_live)

    def continuation(items):
        cont_queries, cont_keys, cont_values, cont_span = items
        live_keys = lax.iota(jnp.int32, PLEN + CLEN) < PLEN + cont_span
        joined_keys = jnp.concatenate([key_rows[:PLEN], cont_keys], axis=0)
        joined_values = jnp.concatenate([value_rows[:PLEN], cont_values], axis=0)
        return attend(cont_queries, joined_keys, joined_values, bias_table, PLEN, live_keys)
    cont_out = lax.map(jax.checkpoint(continuation), (queries[PLEN:].reshape(CONT, CLEN, H, DH), key_rows[PLEN:].reshape(CONT, CLEN, H, DH), value_rows[PLEN:].reshape(CONT, CLEN, H, DH), spans))
    context = jnp.concatenate([prompt_out, cont_out.reshape(CONT * CLEN, H, DH)], axis=0).reshape(total_rows, H * DH)
    context = low(low_back(context))
    middle = inputs + low_back(matmul(context, w_out))
    normed_two = low(rms_scale(middle, gain_ff))
    hidden_pre = low_back(matmul(normed_two, w_in))
    hidden_act = low(jnp.where(hidden_pre > 0, hidden_pre, 0.0))
    final_rows = middle + low_back(matmul(hidden_act, w_ff))
    row_index = lax.iota(jnp.int32, total_rows)
    slot_index = jnp.maximum(row_index - PLEN, 0)
    row_limit = spans[jnp.minimum(slot_index // CLEN, CONT - 1)]
    valid_rows = (row_index < PLEN) | (slot_index % CLEN < row_limit)
    row_count = PLEN + jnp.sum(spans).astype(jnp.float32)
    weights_row = jnp.where(valid_rows, total_rows / row_count, 0.0)
    diff_rows = final_rows - targets
    loss_value = 0.5 * jnp.sum(weights_row[:, None] * diff_rows * diff_rows)
    return (loss_value, final_rows)

def reference(tokens, teacher, lengths, w_query, w_key, w_value, w_out, w_in, w_ff, gain_attn, gain_ff, bias_table):
    params = tuple((weight.astype(jnp.float32) for weight in (w_query, w_key, w_value, w_out, w_in, w_ff, gain_attn, gain_ff, bias_table)))

    def one_group(totals, items):
        group_tokens, group_teacher, group_spans = items
        targets = group_teacher.astype(jnp.float32)

        def loss_of(param_set, inputs):
            return group_loss(param_set, inputs, targets, group_spans)
        loss_value, pull_back, final_rows = jax.vjp(loss_of, params, group_tokens.astype(jnp.float32), has_aux=True)
        param_grads, input_grads = pull_back(jnp.ones_like(loss_value))
        totals = jax.tree.map(jnp.add, totals, param_grads)
        return (totals, (final_rows.astype(jnp.bfloat16), input_grads))
    initial = jax.tree.map(jnp.zeros_like, params)
    totals, (outputs, input_grads) = lax.scan(one_group, initial, (tokens, teacher, lengths))
    return (outputs, input_grads, totals[0], totals[1], totals[2], totals[3], totals[4], totals[5], totals[6], totals[7], totals[8])
```

```python
import jax
import jax.numpy as jnp
import numpy as np
from jax import lax
from jax.experimental import pallas as pl
from jax.experimental.pallas import tpu as pltpu
from jax.sharding import PartitionSpec as P

DH = 64
NB = 32
PLEN = 1024
CLEN = 512
CONT = 4
QB = 256
NQ = 3
ROWS = QB * NQ
KROWS = PLEN + 2 * CLEN
TILE = 128
NEGATIVE = -1e30
f32 = jnp.float32
bf16 = jnp.bfloat16


def dot_nt(a, b):
    return lax.dot_general(a, b, (((1,), (1,)), ((), ())), preferred_element_type=f32)


def dot_nn(a, b):
    return lax.dot_general(a, b, (((1,), (0,)), ((), ())), preferred_element_type=f32)


def low_lanes(shape):
    return lax.broadcasted_iota(jnp.int32, shape, 1) < DH


def add_bias(s, bias_ref, head, kc, qc):
    rows = []
    for a in range(s.shape[0] // TILE):
        cols = []
        for b in range(s.shape[1] // TILE):
            d = jnp.clip(kc + a - qc[b], -2, 2) + 2
            cols.append(bias_ref[head, pl.ds(pl.multiple_of(d * TILE, TILE), TILE), :])
        rows.append(jnp.concatenate(cols, axis=1))
    return s + jnp.concatenate(rows, axis=0)


def forward_kernel(meta, q_ref, k_ref, v_ref, qaug_ref, kaug_ref, bias_ref, ctx_ref, rest_ref, lse_ref,
                   k_scr, vt_scr, s_scr):
    low_k = low_lanes((KROWS, TILE))
    low_q = low_lanes((QB, TILE))
    k_scr[0] = jnp.where(low_k, k_ref[...], kaug_ref[...])
    k_scr[1] = jnp.where(low_k, kaug_ref[...], k_ref[...])
    vt_scr[...] = v_ref[...].T
    KC = 512
    for qb in range(NQ):
        qc = meta[qb]
        slot = pl.multiple_of(PLEN + meta[NQ + qb] * CLEN, CLEN)
        q = q_ref[qb * QB:(qb + 1) * QB, :]
        qa = qaug_ref[qb * QB:(qb + 1) * QB, :]
        outs = []
        for h in range(2):
            qh = jnp.where(low_q, q, qa) if h == 0 else jnp.where(low_q, qa, q)
            m = None
            for c in range(3):
                kk = k_scr[h, c * KC:(c + 1) * KC, :] if c < 2 else k_scr[h, pl.ds(slot, KC), :]
                s = dot_nt(kk, qh)
                s = add_bias(s, bias_ref, h, 4 * c, (qc, qc + 1))
                s_scr[h, c * KC:(c + 1) * KC, :] = s
                mc = jnp.max(s, axis=0, keepdims=True)
                m = mc if m is None else jnp.maximum(m, mc)
            l = None
            acc = None
            for c in range(3):
                p = jnp.exp(s_scr[h, c * KC:(c + 1) * KC, :] - m)
                lc = jnp.sum(p, axis=0, keepdims=True)
                l = lc if l is None else l + lc
                vv = (vt_scr[h * DH:(h + 1) * DH, c * KC:(c + 1) * KC] if c < 2
                      else vt_scr[h * DH:(h + 1) * DH, pl.ds(slot, KC)])
                o = dot_nn(vv, p.astype(bf16))
                acc = o if acc is None else acc + o
            outs.append(acc / l)
            lse_ref[0, h:h + 1, qb * QB:(qb + 1) * QB] = m + jnp.log(l)
        ctx = jnp.concatenate(outs, axis=0).T
        ctx_low = ctx.astype(bf16)
        ctx_ref[qb * QB:(qb + 1) * QB, :] = ctx_low
        rest_ref[qb * QB:(qb + 1) * QB, :] = (ctx - ctx_low.astype(f32)).astype(bf16)


def attention_forward(meta, q, kv, qaug, kaug, bias):
    pairs = q.shape[1] // TILE
    spec = lambda rows, first=0: pl.BlockSpec((rows, TILE), lambda i, meta: (0, first + i))
    fixed = lambda rows: pl.BlockSpec((rows, TILE), lambda i, meta: (0, 0))
    return pl.pallas_call(
        forward_kernel,
        grid_spec=pltpu.PrefetchScalarGridSpec(
            num_scalar_prefetch=1,
            grid=(pairs,),
            in_specs=[spec(ROWS), spec(KROWS), spec(KROWS, pairs), fixed(ROWS), fixed(KROWS),
                      pl.BlockSpec((2, 5 * TILE, TILE), lambda i, meta: (i, 0, 0))],
            out_specs=[spec(ROWS), spec(ROWS), pl.BlockSpec((1, 2, ROWS), lambda i, meta: (i, 0, 0))],
            scratch_shapes=[
                pltpu.VMEM((2, KROWS, TILE), bf16),
                pltpu.VMEM((TILE, KROWS), bf16),
                pltpu.VMEM((2, PLEN + CLEN, QB), f32),
            ],
        ),
        out_shape=[jax.ShapeDtypeStruct((ROWS, pairs * TILE), bf16),
                   jax.ShapeDtypeStruct((ROWS, pairs * TILE), bf16),
                   jax.ShapeDtypeStruct((pairs, 2, ROWS), f32)],
        compiler_params=pltpu.CompilerParams(dimension_semantics=("arbitrary",),
                                             vmem_limit_bytes=56 << 20),
        name="attention_forward",
    )(meta, q, kv, kv, qaug, kaug, bias)


PAD = TILE


def fold_rows(rows):
    return jnp.sum(rows.reshape(rows.shape[0] // 8, 8, rows.shape[1]), axis=0)


def backward_kernel(meta, q_ref, k_ref, v_ref, do_ref, ctx_ref, rest_ref, lse_ref, qaug_ref, kaug_ref,
                    bias_ref, pick_ref, dq_ref, dk_ref, dv_ref, near_ref,
                    k_scr, kt_scr, q_scr, do_scr, delta_scr, ds_scr, dks_scr, dvs_scr, far_scr):
    low_k = low_lanes((KROWS, TILE))
    low_q = low_lanes((ROWS, TILE))
    k_scr[0] = jnp.where(low_k, k_ref[...], kaug_ref[...])
    k_scr[1] = jnp.where(low_k, kaug_ref[...], k_ref[...])
    kt_scr[...] = k_ref[...].T
    q_scr[0] = jnp.where(low_q, q_ref[...], qaug_ref[...])
    q_scr[1] = jnp.where(low_q, qaug_ref[...], q_ref[...])
    zero = jnp.zeros((ROWS, TILE), bf16)
    do_scr[0] = jnp.where(low_q, do_ref[...], zero)
    do_scr[1] = jnp.where(low_q, zero, do_ref[...])
    prod = do_ref[...].astype(f32) * (ctx_ref[...].astype(f32) + rest_ref[...].astype(f32))
    hi = prod.astype(bf16)
    lo = (prod - hi.astype(f32)).astype(bf16)
    pick_row = lax.broadcasted_iota(jnp.int32, (8, TILE), 0)
    pick_low = low_lanes((8, TILE))
    pick = jnp.where((pick_row == 0) & pick_low | (pick_row == 1) & ~pick_low, 1.0, 0.0).astype(bf16)
    delta_scr[...] = dot_nt(pick, hi) + dot_nt(pick, lo)
    for h in range(2):
        ds_scr[h, 0:PAD, :] = jnp.zeros((PAD, ROWS), bf16)
        ds_scr[h, PAD + PLEN + CLEN:, :] = jnp.zeros((PAD, ROWS), bf16)

    def piece(h, kk, vv, kc, qb):
        cols = slice(qb * QB, (qb + 1) * QB)
        s = dot_nt(kk, q_scr[h, cols, :])
        qc = meta[qb]
        s = add_bias(s, bias_ref, h, kc, (qc, qc + 1))
        p = jnp.exp(s - lse_ref[0, h:h + 1, cols])
        dp = dot_nt(vv, do_scr[h, cols, :])
        ds = (p * (dp - delta_scr[h:h + 1, cols])).astype(bf16)
        return p.astype(bf16), ds

    low_c = low_lanes((QB, TILE))

    def prompt_chunk(c, carry):
        start = pl.multiple_of(c * QB, QB)
        dv = None
        dks = []
        for h in range(2):
            kk = k_scr[h, pl.ds(start, QB), :]
            vv = v_ref[pl.ds(start, QB), :]
            dk = None
            for qb in range(NQ):
                cols = slice(qb * QB, (qb + 1) * QB)
                p, ds = piece(h, kk, vv, 2 * c, qb)
                ds_scr[h, pl.ds(PAD + start, QB), cols] = ds
                a = dot_nn(p, do_scr[h, cols, :])
                b = dot_nn(ds, q_scr[h, cols, :])
                dv = a if dv is None else dv + a
                dk = b if dk is None else dk + b
            dks.append(dk)
        dv_ref[pl.ds(start, QB), :] = dv.astype(bf16)
        dk_ref[pl.ds(start, QB), :] = jnp.where(low_c, dks[0], dks[1]).astype(bf16)
        sums = jnp.where(low_c, dks[1], dks[0])
        far_scr[2 * c] = fold_rows(sums[:TILE])
        far_scr[2 * c + 1] = fold_rows(sums[TILE:])
        return carry

    lax.fori_loop(0, PLEN // QB, prompt_chunk, 0)
    dvs_scr[...] = jnp.zeros_like(dvs_scr)
    dks_scr[...] = jnp.zeros_like(dks_scr)
    for qb in range(NQ):
        cols = slice(qb * QB, (qb + 1) * QB)
        slot = pl.multiple_of(meta[NQ + qb] * CLEN, CLEN)
        for half in range(CLEN // QB):
            start = pl.multiple_of(slot + half * QB, QB)
            dv = None
            for h in range(2):
                kk = k_scr[h, pl.ds(PLEN + start, QB), :]
                vv = v_ref[pl.ds(PLEN + start, QB), :]
                p, ds = piece(h, kk, vv, 8 + 2 * half, qb)
                ds_scr[h, PAD + PLEN + half * QB:PAD + PLEN + (half + 1) * QB, cols] = ds
                a = dot_nn(p, do_scr[h, cols, :])
                dv = a if dv is None else dv + a
                dks_scr[h, pl.ds(start, QB), :] += dot_nn(ds, q_scr[h, cols, :])
            dvs_scr[pl.ds(start, QB), :] += dv
    dv_ref[PLEN:, :] = dvs_scr[...].astype(bf16)
    low_s = low_lanes((2 * CLEN, TILE))
    dk_ref[PLEN:, :] = jnp.where(low_s, dks_scr[0], dks_scr[1]).astype(bf16)
    sums = jnp.where(low_s, dks_scr[1], dks_scr[0])
    for t in range(2 * CLEN // TILE):
        far_scr[8 + t] = fold_rows(sums[t * TILE:(t + 1) * TILE])

    dqt = []
    for h in range(2):
        parts = []
        for qb in range(NQ):
            cols = slice(qb * QB, (qb + 1) * QB)
            slot = pl.multiple_of(PLEN + meta[NQ + qb] * CLEN, CLEN)
            rows = slice(h * DH, (h + 1) * DH)
            a = dot_nn(kt_scr[rows, 0:PLEN], ds_scr[h, PAD:PAD + PLEN, cols])
            b = dot_nn(kt_scr[rows, pl.ds(slot, CLEN)], ds_scr[h, PAD + PLEN:PAD + PLEN + CLEN, cols])
            parts.append(a + b)
        dqt.append(jnp.concatenate(parts, axis=1))
    dq_ref[...] = jnp.concatenate(dqt, axis=0).T.astype(bf16)

    row_id = lax.broadcasted_iota(jnp.int32, (TILE, TILE), 0)
    lane_id = lax.broadcasted_iota(jnp.int32, (TILE, TILE), 1)
    flip = jnp.where(row_id + lane_id == TILE - 1, 1.0, 0.0).astype(bf16)
    for h in range(2):
        acc = None
        for sub in range(2 * NQ):
            qc = meta[sub // 2] + sub % 2
            start = pl.multiple_of(qc * TILE, TILE)
            part = ds_scr[h, pl.ds(start, 3 * TILE), sub * TILE:(sub + 1) * TILE].astype(f32)
            acc = part if acc is None else acc + part
        top = acc.astype(bf16)
        acc = dot_nn(top, flip) + dot_nn((acc - top.astype(f32)).astype(bf16), flip)
        sums = []
        for d in range(3):
            rolled = pltpu.roll(acc[d * TILE:(d + 1) * TILE], 0, 1, stride=1, stride_axis=0)
            wrapped = jnp.where(lane_id < row_id, rolled, 0.0)
            sums += [fold_rows(rolled), fold_rows(wrapped)]
        for side in range(2):
            total = None
            for t in range(16):
                term = far_scr[t] * pick_ref[h, side, t]
                total = term if total is None else total + term
            sums.append(total)
        for i, eight in enumerate(sums):
            near_ref[0, h, i] = eight


def attention_backward(meta, q, kv, do, ctx, rest, lse, qaug, kaug, bias, pick):
    pairs = q.shape[1] // TILE
    spec = lambda rows, first=0: pl.BlockSpec((rows, TILE), lambda i, meta: (0, first + i))
    fixed = lambda rows: pl.BlockSpec((rows, TILE), lambda i, meta: (0, 0))
    width = pairs * TILE
    return pl.pallas_call(
        backward_kernel,
        grid_spec=pltpu.PrefetchScalarGridSpec(
            num_scalar_prefetch=1,
            grid=(pairs,),
            in_specs=[spec(ROWS), spec(KROWS), spec(KROWS, pairs), spec(ROWS), spec(ROWS), spec(ROWS),
                      pl.BlockSpec((1, 2, ROWS), lambda i, meta: (i, 0, 0)),
                      fixed(ROWS), fixed(KROWS),
                      pl.BlockSpec((2, 5 * TILE, TILE), lambda i, meta: (i, 0, 0)),
                      pl.BlockSpec((2, 2, 16, 8, TILE), lambda i, meta: (0, 0, 0, 0, 0))],
            out_specs=[spec(ROWS), spec(KROWS), spec(KROWS),
                       pl.BlockSpec((1, 2, 8, 8, TILE), lambda i, meta: (i, 0, 0, 0, 0))],
            scratch_shapes=[
                pltpu.VMEM((2, KROWS, TILE), bf16),
                pltpu.VMEM((TILE, KROWS), bf16),
                pltpu.VMEM((2, ROWS, TILE), bf16),
                pltpu.VMEM((2, ROWS, TILE), bf16),
                pltpu.VMEM((8, ROWS), f32),
                pltpu.VMEM((2, PLEN + CLEN + 2 * PAD, ROWS), bf16),
                pltpu.VMEM((2, 2 * CLEN, TILE), f32),
                pltpu.VMEM((2 * CLEN, TILE), f32),
                pltpu.VMEM((16, 8, TILE), f32),
            ],
        ),
        out_shape=[jax.ShapeDtypeStruct((ROWS, width), bf16),
                   jax.ShapeDtypeStruct((KROWS, width), bf16),
                   jax.ShapeDtypeStruct((KROWS, width), bf16),
                   jax.ShapeDtypeStruct((pairs, 2, 8, 8, TILE), f32)],
        compiler_params=pltpu.CompilerParams(dimension_semantics=("arbitrary",),
                                             vmem_limit_bytes=60 << 20),
        name="attention_backward",
    )(meta, q, kv, kv, do, ctx, rest, lse, qaug, kaug, bias, pick)


EPSILON = 1e-06
THRESHOLDS = (12, 16, 23, 32, 46, 64, 91)
OWNER_BLOCK = (0, 3, 1, 2)


def python_bucket(offset):
    magnitude = abs(offset)
    base = NB // 2 if offset > 0 else 0
    if magnitude < 8:
        return base + magnitude
    return base + 8 + sum(1 for edge in THRESHOLDS if magnitude >= edge)


def bias_tiles(table):
    shape = (5, TILE, TILE)
    offset = (TILE * (lax.broadcasted_iota(jnp.int32, shape, 0) - 2)
              + lax.broadcasted_iota(jnp.int32, shape, 1) - lax.broadcasted_iota(jnp.int32, shape, 2))
    columns = table.astype(f32).T[:, :, None, None, None]
    previous = python_bucket(-200)
    tiles = jnp.broadcast_to(columns[:, previous], (table.shape[1],) + shape)
    for n in range(-199, 201):
        current = python_bucket(n)
        if current != previous:
            tiles = jnp.where(offset >= n, columns[:, current], tiles)
            previous = current
    return tiles.reshape(table.shape[1], 5 * TILE, TILE)


def bias_spread():
    spread = np.zeros((8, TILE, NB), np.float32)
    for lane in range(TILE):
        for d in range(3):
            inside = python_bucket(TILE * (d - 1) + lane - (TILE - 1))
            passed = python_bucket(TILE * d + lane - (TILE - 1))
            spread[2 * d, lane, inside] += 1
            spread[2 * d + 1, lane, passed] += 1
            spread[2 * d + 1, lane, inside] -= 1
    spread[6, :, python_bucket(-200)] = 1
    spread[7, :, python_bucket(200)] = 1
    return spread.reshape(8 * TILE, NB)


def placement(me, spans):
    block = NQ * me + jnp.arange(NQ, dtype=jnp.int32)
    prompt = block < PLEN // QB
    cont = jnp.maximum(block - PLEN // QB, 0) // 2
    half = jnp.maximum(block - PLEN // QB, 0) % 2
    tile = jnp.where(prompt, 2 * block, PLEN // TILE + 2 * half)
    slot = jnp.where(prompt, 0, cont - (me - 1))
    chosen = cont[:, None] == jnp.arange(CONT, dtype=jnp.int32)[None, :]
    limit = jnp.where(prompt, 0, jnp.sum(jnp.where(chosen, spans[None, :], 0), axis=1))
    meta = jnp.concatenate([tile, slot]).astype(jnp.int32)
    shape = (KROWS, TILE)
    key = lax.broadcasted_iota(jnp.int32, shape, 0)
    sub = lax.broadcasted_iota(jnp.int32, shape, 1) % DH
    kaug = jnp.zeros(shape, f32)
    for q in range(NQ):
        first = PLEN + CLEN * slot[q]
        seen = (key < PLEN) | ((key >= first) & (key < first + limit[q]))
        kaug = jnp.where((sub // 2 == q) & ~seen, NEGATIVE, kaug)
    shape = (ROWS, TILE)
    qaug = lax.broadcasted_iota(jnp.int32, shape, 1) % DH == lax.broadcasted_iota(jnp.int32, shape, 0) // TILE
    shape = (2, 2, 16, 8, TILE)
    head, side, row, lane = (lax.broadcasted_iota(jnp.int32, shape, a) for a in (0, 1, 2, 4))
    sub = lane - jnp.where(head == 0, DH, 0)
    key_tile = jnp.where(row < 8, row, 8 + (row - 8) % 4)
    query_tile = jnp.full(shape, -1000, jnp.int32)
    for q in range(2 * NQ):
        query_tile = jnp.where(sub == q, tile[q // 2] + q % 2, query_tile)
    apart = key_tile - query_tile
    far = jnp.where(side == 0, apart <= -2, (apart >= 2) & (apart < 100))
    return meta, qaug.astype(bf16), kaug.astype(bf16), far.astype(f32)


def rms(rows):
    return lax.rsqrt(jnp.mean(rows * rows, axis=1, keepdims=True) + EPSILON)


def normed_rows(rows, gain):
    rows = rows.astype(f32)
    return (rows * rms(rows) * gain).astype(bf16)


def norm_backward(inputs, inverse, gain, d_normed):
    scaled = inputs * inverse
    d_gain = jnp.sum(d_normed * scaled, axis=0)
    d_scaled = d_normed * gain
    return (inverse * (d_scaled - scaled * jnp.mean(d_scaled * scaled, axis=1, keepdims=True)), d_gain)


def contract_rows(left, right):
    return lax.dot_general(left, right, (((0,), (0,)), ((), ())), preferred_element_type=f32)


def block_of(rows, i):
    return rows[i * QB:(i + 1) * QB]


def send(rows, pairs):
    return lax.ppermute(rows, "seq", pairs)


def pick_by(me, *choices):
    out = choices[-1]
    for i in range(len(choices) - 2, -1, -1):
        out = jnp.where(me == i, choices[i], out)
    return out


def gather_rows(me, own):
    mine = [block_of(own, i) for i in range(NQ)]
    pair = pick_by(me, mine[0], mine[0], mine[2], mine[0])
    cross = send(pair, [(1, 0), (2, 3), (3, 2)])
    down = [send(mine[i], [(0, 1)]) for i in range(NQ)]
    side = [send(pick_by(me, mine[i], mine[0], mine[i], mine[i]), [(0, 2)] + ([(1, 3)] if i == 0 else []))
            for i in range(NQ)]
    last = side[0]
    prompt = []
    first_relay = send(down[0], [(1, 3)])
    second_relay = send(side[1], [(2, 3)])
    half = QB // 2
    third_a = send(down[2][:half], [(1, 3)])
    third_b = send(side[2][half:], [(2, 3)])
    fourth = send(last, [(3, 2)])
    relays = [first_relay, second_relay, jnp.concatenate([third_a, third_b], axis=0)]
    for i in range(NQ):
        prompt.append(pick_by(me, mine[i], down[i], side[i], relays[i]))
    prompt.append(pick_by(me, cross, mine[0], fourth, last))
    slots = [
        pick_by(me, mine[0], mine[1], mine[0], cross),
        pick_by(me, mine[1], mine[2], mine[1], mine[0]),
        pick_by(me, mine[1], mine[1], mine[2], mine[1]),
        pick_by(me, mine[2], mine[2], cross, mine[2]),
    ]
    return jnp.concatenate(prompt + slots, axis=0)


def sum_prompt(me, partial):
    owner = jnp.array(OWNER_BLOCK, jnp.int32)

    def take(device):
        start = owner[device] * QB
        return lax.dynamic_slice_in_dim(partial, start, QB, 0)

    total = take(me).astype(f32)
    for flip in (1, 2, 3):
        total = total + send(take(me ^ flip), [(i, i ^ flip) for i in range(4)]).astype(f32)
    parts = [block_of(partial, i) for i in range(8)]
    crossed = send(jnp.where(me == 2, parts[7], parts[4]), [(2, 3), (3, 2)])
    zero = jnp.zeros_like(parts[0])
    joined = (jnp.where(me == 2, parts[6], parts[5]).astype(f32) + crossed.astype(f32)).astype(bf16)
    rows = [
        total.astype(bf16),
        pick_by(me, zero, zero, parts[4], joined),
        pick_by(me, zero, parts[4], parts[5], parts[6]),
        pick_by(me, zero, parts[5], joined, parts[7]),
    ]
    return jnp.concatenate(rows, axis=0)


def local(tokens, teacher, lengths, w_query, w_key, w_value, w_out, w_in, w_ff, gain_attn, gain_ff, bias_table):
    me = lax.axis_index("seq")
    own = tokens[0]
    inputs = own.astype(f32)
    targets = teacher[0].astype(f32)
    spans = lengths[0]
    width = own.shape[1]
    pairs = width // TILE

    def gather(w):
        return lax.all_gather(w, "wshard", axis=0, tiled=True)

    full_qkv = gather(jnp.concatenate([w_query, w_key, w_value], axis=1))
    full_out, full_in, full_ff = gather(w_out), gather(w_in), gather(w_ff)
    gains = gather(jnp.stack([gain_attn, gain_ff], axis=1)).astype(f32).T
    gain_one, gain_two = gains[0], gains[1]
    meta, qaug, kaug, far = placement(me, spans)
    bias = bias_tiles(bias_table)
    seen = gather_rows(me, own)
    inverse_one = rms(inputs)
    normed_own = (inputs * inverse_one * gain_one).astype(bf16)
    normed_seen = normed_rows(seen, gain_one)
    queries = jnp.dot(normed_own, full_qkv[:, :width], preferred_element_type=f32).astype(bf16)
    keys_values = jnp.dot(normed_seen, full_qkv[:, width:], preferred_element_type=f32).astype(bf16)
    context, rest, lse = attention_forward(meta, queries, keys_values, qaug, kaug, bias)
    middle = inputs + jnp.dot(context, full_out, preferred_element_type=f32)
    inverse_two = rms(middle)
    normed_two = (middle * inverse_two * gain_two).astype(bf16)
    hidden_act = jnp.maximum(jnp.dot(normed_two, full_in, preferred_element_type=f32), 0.0).astype(bf16)
    final_rows = middle + jnp.dot(hidden_act, full_ff, preferred_element_type=f32)
    local_rows = inputs.shape[0]
    row_index = me * local_rows + lax.iota(jnp.int32, local_rows)
    slot_index = jnp.maximum(row_index - PLEN, 0)
    owner_match = (slot_index // CLEN)[:, None] == lax.iota(jnp.int32, CONT)[None, :]
    row_limit = jnp.sum(jnp.where(owner_match, spans[None, :], 0), axis=1)
    valid_rows = (row_index < PLEN) | (slot_index % CLEN < row_limit)
    row_count = PLEN + jnp.sum(spans).astype(f32)
    factor = (PLEN + CONT * CLEN) / row_count
    d_final = jnp.where(valid_rows[:, None], factor * (final_rows - targets), 0.0)
    d_branch_two = d_final.astype(bf16)
    grad_ff = contract_rows(hidden_act, d_branch_two)
    d_pre = jnp.where(hidden_act > 0, dot_nt(d_branch_two, full_ff), 0.0).astype(bf16)
    grad_in = contract_rows(normed_two, d_pre)
    d_middle, grad_gain2 = norm_backward(middle, inverse_two, gain_two, dot_nt(d_pre, full_in))
    d_middle = d_final + d_middle
    d_branch_one = d_middle.astype(bf16)
    grad_out = contract_rows(context, d_branch_one)
    d_context = dot_nt(d_branch_one, full_out).astype(bf16)
    d_queries, d_keys, d_values, near = attention_backward(
        meta, queries, keys_values, d_context, context, rest, lse, qaug, kaug, bias, far)
    d_kv = sum_prompt(me, jnp.concatenate([d_keys, d_values], axis=1))
    prompt_start = jnp.array(OWNER_BLOCK, jnp.int32)[me] * QB
    normed_sum = jnp.concatenate([lax.dynamic_slice_in_dim(normed_seen, prompt_start, QB, 0), normed_own], axis=0)
    d_qkv = jnp.concatenate([
        jnp.concatenate([jnp.zeros((QB, width), bf16), d_queries], axis=0), d_kv], axis=1)
    grad_qkv = contract_rows(normed_sum, d_qkv)
    f_rows = dot_nt(d_qkv, full_qkv)
    f_first = f_rows[:QB]
    f_sent = f_first.astype(bf16)
    from_two = send(f_sent, [(2, 0)]).astype(f32)
    from_three = send(f_sent, [(3, 0)]).astype(f32)
    f_own = f_rows[QB:] + jnp.concatenate([jnp.where(me < 2, f_first, 0.0), from_two, from_three], axis=0)
    d_inputs, grad_gain1 = norm_backward(inputs, inverse_one, gain_one, f_own)
    d_tokens = d_middle + d_inputs

    def reduce(g):
        share = lax.psum_scatter(g.astype(bf16), "wshard", scatter_dimension=0, tiled=True)
        return lax.psum(share, "seq").astype(f32)

    share_ff, share_in, share_out, share_qkv = reduce(grad_ff), reduce(grad_in), reduce(grad_out), reduce(grad_qkv)
    heads = bias_table.shape[1]
    bias_local = jnp.dot(jnp.sum(near, axis=3).reshape(heads, 8 * TILE), jnp.asarray(bias_spread()),
                         precision=lax.Precision.HIGHEST)
    small = jnp.concatenate([grad_gain1, grad_gain2, bias_local.reshape(-1)])
    small = lax.psum(small, ("seq", "wshard"))
    mine = lax.axis_index("wshard")
    part = gain_attn.shape[0]
    gain_share = [lax.dynamic_slice_in_dim(small, i * width + mine * part, part) for i in range(2)]
    bias_grad = small[2 * width:].reshape(heads, NB).T
    return (
        final_rows.astype(bf16)[None],
        d_tokens[None],
        share_qkv[:, :width],
        share_qkv[:, width:2 * width],
        share_qkv[:, 2 * width:],
        share_out,
        share_in,
        share_ff,
        gain_share[0],
        gain_share[1],
        bias_grad,
    )


def solution(mesh):
    rows = P("wshard", "seq", None)
    weight = P("wshard", None)
    placed = (rows, rows) + (weight,) * 7 + (P("wshard"), P("wshard"), P())
    return jax.shard_map(
        local,
        mesh=mesh,
        in_specs=placed,
        out_specs=(rows, rows) + (weight,) * 6 + (P("wshard"), P("wshard"), P()),
        check_vma=False,
    )
```

```python
import jax
import jax.numpy as jnp
import numpy as np
from jax import lax
from jax.experimental import pallas as pl
from jax.experimental.pallas import tpu as pltpu
from jax.experimental.layout import Layout, with_layout_constraint
from jax.sharding import PartitionSpec as P

DH = 64
NB = 32
PLEN = 1024
CLEN = 512
CONT = 4
QB = 256
NQ = 3
ROWS = QB * NQ
KROWS = PLEN + 2 * CLEN
TILE = 128
NEGATIVE = -1e30
f32 = jnp.float32
bf16 = jnp.bfloat16


def dot_nt(a, b):
    return lax.dot_general(a, b, (((1,), (1,)), ((), ())), preferred_element_type=f32)


def dot_nn(a, b):
    return lax.dot_general(a, b, (((1,), (0,)), ((), ())), preferred_element_type=f32)


def low_lanes(shape):
    return lax.broadcasted_iota(jnp.int32, shape, 1) < DH


def add_bias(s, bias_ref, head, kc, qc):
    rows = []
    for a in range(s.shape[0] // TILE):
        cols = []
        for b in range(s.shape[1] // TILE):
            d = jnp.clip(kc + a - qc[b], -2, 2) + 2
            cols.append(bias_ref[head, pl.ds(pl.multiple_of(d * TILE, TILE), TILE), :])
        rows.append(jnp.concatenate(cols, axis=1))
    return s + jnp.concatenate(rows, axis=0)


def forward_kernel(meta, q_ref, k_ref, v_ref, qaug_ref, kaug_ref, bias_ref, ctx_ref, rest_ref, lse_ref,
                   k_scr, vt_scr, s_scr):
    low_k = low_lanes((KROWS, TILE))
    low_q = low_lanes((QB, TILE))
    k_scr[0] = jnp.where(low_k, k_ref[...], kaug_ref[...])
    k_scr[1] = jnp.where(low_k, kaug_ref[...], k_ref[...])
    vt_scr[...] = v_ref[...].T
    KC = 512
    for qb in range(NQ):
        qc = meta[qb]
        slot = pl.multiple_of(PLEN + meta[NQ + qb] * CLEN, CLEN)
        q = q_ref[qb * QB:(qb + 1) * QB, :]
        qa = qaug_ref[qb * QB:(qb + 1) * QB, :]
        outs = []
        for h in range(2):
            qh = jnp.where(low_q, q, qa) if h == 0 else jnp.where(low_q, qa, q)
            m = None
            for c in range(3):
                kk = k_scr[h, c * KC:(c + 1) * KC, :] if c < 2 else k_scr[h, pl.ds(slot, KC), :]
                s = dot_nt(kk, qh)
                s = add_bias(s, bias_ref, h, 4 * c, (qc, qc + 1))
                s_scr[h, c * KC:(c + 1) * KC, :] = s
                mc = jnp.max(s, axis=0, keepdims=True)
                m = mc if m is None else jnp.maximum(m, mc)
            l = None
            acc = None
            for c in range(3):
                p = jnp.exp(s_scr[h, c * KC:(c + 1) * KC, :] - m)
                lc = jnp.sum(p, axis=0, keepdims=True)
                l = lc if l is None else l + lc
                vv = (vt_scr[h * DH:(h + 1) * DH, c * KC:(c + 1) * KC] if c < 2
                      else vt_scr[h * DH:(h + 1) * DH, pl.ds(slot, KC)])
                o = dot_nn(vv, p.astype(bf16))
                acc = o if acc is None else acc + o
            outs.append(acc / l)
            lse_ref[0, h:h + 1, qb * QB:(qb + 1) * QB] = m + jnp.log(l)
        ctx = jnp.concatenate(outs, axis=0).T
        ctx_low = ctx.astype(bf16)
        ctx_ref[qb * QB:(qb + 1) * QB, :] = ctx_low
        rest_ref[qb * QB:(qb + 1) * QB, :] = (ctx - ctx_low.astype(f32)).astype(bf16)


def attention_forward(meta, q, kv, qaug, kaug, bias, first, pairs):
    own = pl.BlockSpec((ROWS, TILE), lambda i, meta: (0, first + i))
    out = pl.BlockSpec((ROWS, TILE), lambda i, meta: (0, i))
    keys = pl.BlockSpec((KROWS, TILE), lambda i, meta: (0, 2 * (first + i)))
    values = pl.BlockSpec((KROWS, TILE), lambda i, meta: (0, 2 * (first + i) + 1))
    fixed = lambda rows: pl.BlockSpec((rows, TILE), lambda i, meta: (0, 0))
    return pl.pallas_call(
        forward_kernel,
        grid_spec=pltpu.PrefetchScalarGridSpec(
            num_scalar_prefetch=1,
            grid=(pairs,),
            in_specs=[own, keys, values, fixed(ROWS), fixed(KROWS),
                      pl.BlockSpec((2, 5 * TILE, TILE), lambda i, meta: (first + i, 0, 0))],
            out_specs=[out, out, pl.BlockSpec((1, 2, ROWS), lambda i, meta: (i, 0, 0))],
            scratch_shapes=[
                pltpu.VMEM((2, KROWS, TILE), bf16),
                pltpu.VMEM((TILE, KROWS), bf16),
                pltpu.VMEM((2, PLEN + CLEN, QB), f32),
            ],
        ),
        out_shape=[jax.ShapeDtypeStruct((ROWS, pairs * TILE), bf16),
                   jax.ShapeDtypeStruct((ROWS, pairs * TILE), bf16),
                   jax.ShapeDtypeStruct((pairs, 2, ROWS), f32)],
        compiler_params=pltpu.CompilerParams(dimension_semantics=("arbitrary",),
                                             vmem_limit_bytes=56 << 20),
        cost_estimate=pl.CostEstimate(flops=pairs * 5_000_000_000, bytes_accessed=pairs * 2_000_000,
                                      transcendentals=pairs * 2 * ROWS * (PLEN + CLEN)),
        name="attention_forward",
    )(meta, q, kv, kv, qaug, kaug, bias)


PAD = TILE


def fold_rows(rows):
    return jnp.sum(rows.reshape(rows.shape[0] // 8, 8, rows.shape[1]), axis=0)


def backward_kernel(meta, q_ref, k_ref, v_ref, do_ref, ctx_ref, rest_ref, lse_ref, qaug_ref, kaug_ref,
                    bias_ref, pick_ref, dq_ref, dkv_ref, near_ref,
                    k_scr, kt_scr, q_scr, do_scr, delta_scr, ds_scr, dks_scr, dvs_scr, far_scr):
    low_k = low_lanes((KROWS, TILE))
    low_q = low_lanes((ROWS, TILE))
    k_scr[0] = jnp.where(low_k, k_ref[...], kaug_ref[...])
    k_scr[1] = jnp.where(low_k, kaug_ref[...], k_ref[...])
    kt_scr[...] = k_ref[...].T
    q_scr[0] = jnp.where(low_q, q_ref[...], qaug_ref[...])
    q_scr[1] = jnp.where(low_q, qaug_ref[...], q_ref[...])
    zero = jnp.zeros((ROWS, TILE), bf16)
    do_scr[0] = jnp.where(low_q, do_ref[...], zero)
    do_scr[1] = jnp.where(low_q, zero, do_ref[...])
    prod = do_ref[...].astype(f32) * (ctx_ref[...].astype(f32) + rest_ref[...].astype(f32))
    hi = prod.astype(bf16)
    lo = (prod - hi.astype(f32)).astype(bf16)
    pick_row = lax.broadcasted_iota(jnp.int32, (8, TILE), 0)
    pick_low = low_lanes((8, TILE))
    pick = jnp.where((pick_row == 0) & pick_low | (pick_row == 1) & ~pick_low, 1.0, 0.0).astype(bf16)
    delta_scr[...] = dot_nt(pick, hi) + dot_nt(pick, lo)
    for h in range(2):
        ds_scr[h, 0:PAD, :] = jnp.zeros((PAD, ROWS), bf16)
        ds_scr[h, PAD + PLEN + CLEN:, :] = jnp.zeros((PAD, ROWS), bf16)

    def piece(h, kk, vv, kc, qb):
        cols = slice(qb * QB, (qb + 1) * QB)
        s = dot_nt(kk, q_scr[h, cols, :])
        qc = meta[qb]
        s = add_bias(s, bias_ref, h, kc, (qc, qc + 1))
        p = jnp.exp(s - lse_ref[0, h:h + 1, cols])
        dp = dot_nt(vv, do_scr[h, cols, :])
        ds = (p * (dp - delta_scr[h:h + 1, cols])).astype(bf16)
        return p.astype(bf16), ds

    low_c = low_lanes((QB, TILE))

    def prompt_chunk(c, carry):
        start = pl.multiple_of(c * QB, QB)
        dv = None
        dks = []
        for h in range(2):
            kk = k_scr[h, pl.ds(start, QB), :]
            vv = v_ref[pl.ds(start, QB), :]
            dk = None
            for qb in range(NQ):
                cols = slice(qb * QB, (qb + 1) * QB)
                p, ds = piece(h, kk, vv, 2 * c, qb)
                ds_scr[h, pl.ds(PAD + start, QB), cols] = ds
                a = dot_nn(p, do_scr[h, cols, :])
                b = dot_nn(ds, q_scr[h, cols, :])
                dv = a if dv is None else dv + a
                dk = b if dk is None else dk + b
            dks.append(dk)
        dkv_ref[pl.ds(start, QB), TILE:] = dv.astype(bf16)
        dkv_ref[pl.ds(start, QB), :TILE] = jnp.where(low_c, dks[0], dks[1]).astype(bf16)
        sums = jnp.where(low_c, dks[1], dks[0])
        far_scr[2 * c] = fold_rows(sums[:TILE])
        far_scr[2 * c + 1] = fold_rows(sums[TILE:])
        return carry

    lax.fori_loop(0, PLEN // QB, prompt_chunk, 0)
    dvs_scr[...] = jnp.zeros_like(dvs_scr)
    dks_scr[...] = jnp.zeros_like(dks_scr)
    for qb in range(NQ):
        cols = slice(qb * QB, (qb + 1) * QB)
        slot = pl.multiple_of(meta[NQ + qb] * CLEN, CLEN)
        for half in range(CLEN // QB):
            start = pl.multiple_of(slot + half * QB, QB)
            dv = None
            for h in range(2):
                kk = k_scr[h, pl.ds(PLEN + start, QB), :]
                vv = v_ref[pl.ds(PLEN + start, QB), :]
                p, ds = piece(h, kk, vv, 8 + 2 * half, qb)
                ds_scr[h, PAD + PLEN + half * QB:PAD + PLEN + (half + 1) * QB, cols] = ds
                a = dot_nn(p, do_scr[h, cols, :])
                dv = a if dv is None else dv + a
                dks_scr[h, pl.ds(start, QB), :] += dot_nn(ds, q_scr[h, cols, :])
            dvs_scr[pl.ds(start, QB), :] += dv
    dkv_ref[PLEN:, TILE:] = dvs_scr[...].astype(bf16)
    low_s = low_lanes((2 * CLEN, TILE))
    dkv_ref[PLEN:, :TILE] = jnp.where(low_s, dks_scr[0], dks_scr[1]).astype(bf16)
    sums = jnp.where(low_s, dks_scr[1], dks_scr[0])
    for t in range(2 * CLEN // TILE):
        far_scr[8 + t] = fold_rows(sums[t * TILE:(t + 1) * TILE])

    dqt = []
    for h in range(2):
        parts = []
        for qb in range(NQ):
            cols = slice(qb * QB, (qb + 1) * QB)
            slot = pl.multiple_of(PLEN + meta[NQ + qb] * CLEN, CLEN)
            rows = slice(h * DH, (h + 1) * DH)
            a = dot_nn(kt_scr[rows, 0:PLEN], ds_scr[h, PAD:PAD + PLEN, cols])
            b = dot_nn(kt_scr[rows, pl.ds(slot, CLEN)], ds_scr[h, PAD + PLEN:PAD + PLEN + CLEN, cols])
            parts.append(a + b)
        dqt.append(jnp.concatenate(parts, axis=1))
    dq_ref[...] = jnp.concatenate(dqt, axis=0).T.astype(bf16)

    row_id = lax.broadcasted_iota(jnp.int32, (TILE, TILE), 0)
    lane_id = lax.broadcasted_iota(jnp.int32, (TILE, TILE), 1)
    flip = jnp.where(row_id + lane_id == TILE - 1, 1.0, 0.0).astype(bf16)
    for h in range(2):
        acc = None
        for sub in range(2 * NQ):
            qc = meta[sub // 2] + sub % 2
            start = pl.multiple_of(qc * TILE, TILE)
            part = ds_scr[h, pl.ds(start, 3 * TILE), sub * TILE:(sub + 1) * TILE].astype(f32)
            acc = part if acc is None else acc + part
        top = acc.astype(bf16)
        acc = dot_nn(top, flip) + dot_nn((acc - top.astype(f32)).astype(bf16), flip)
        sums = []
        for d in range(3):
            rolled = pltpu.roll(acc[d * TILE:(d + 1) * TILE], 0, 1, stride=1, stride_axis=0)
            wrapped = jnp.where(lane_id < row_id, rolled, 0.0)
            sums += [fold_rows(rolled), fold_rows(wrapped)]
        for side in range(2):
            total = None
            for t in range(16):
                term = far_scr[t] * pick_ref[h, side, t]
                total = term if total is None else total + term
            sums.append(total)
        for i, eight in enumerate(sums):
            near_ref[0, h, i] = eight


def attention_backward(meta, q, kv, do, ctx, rest, lse, qaug, kaug, bias, pick, first, pairs):
    own = pl.BlockSpec((ROWS, TILE), lambda i, meta: (0, first + i))
    keys = pl.BlockSpec((KROWS, TILE), lambda i, meta: (0, 2 * (first + i)))
    values = pl.BlockSpec((KROWS, TILE), lambda i, meta: (0, 2 * (first + i) + 1))
    fixed = lambda rows: pl.BlockSpec((rows, TILE), lambda i, meta: (0, 0))
    return pl.pallas_call(
        backward_kernel,
        grid_spec=pltpu.PrefetchScalarGridSpec(
            num_scalar_prefetch=1,
            grid=(pairs,),
            in_specs=[own, keys, values, own, own, own,
                      pl.BlockSpec((1, 2, ROWS), lambda i, meta: (first + i, 0, 0)),
                      fixed(ROWS), fixed(KROWS),
                      pl.BlockSpec((2, 5 * TILE, TILE), lambda i, meta: (first + i, 0, 0)),
                      pl.BlockSpec((2, 2, 16, 8, TILE), lambda i, meta: (0, 0, 0, 0, 0))],
            out_specs=[pl.BlockSpec((ROWS, TILE), lambda i, meta: (0, i)),
                       pl.BlockSpec((KROWS, 2 * TILE), lambda i, meta: (0, i)),
                       pl.BlockSpec((1, 2, 8, 8, TILE), lambda i, meta: (i, 0, 0, 0, 0))],
            scratch_shapes=[
                pltpu.VMEM((2, KROWS, TILE), bf16),
                pltpu.VMEM((TILE, KROWS), bf16),
                pltpu.VMEM((2, ROWS, TILE), bf16),
                pltpu.VMEM((2, ROWS, TILE), bf16),
                pltpu.VMEM((8, ROWS), f32),
                pltpu.VMEM((2, PLEN + CLEN + 2 * PAD, ROWS), bf16),
                pltpu.VMEM((2, 2 * CLEN, TILE), f32),
                pltpu.VMEM((2 * CLEN, TILE), f32),
                pltpu.VMEM((16, 8, TILE), f32),
            ],
        ),
        out_shape=[jax.ShapeDtypeStruct((ROWS, pairs * TILE), bf16),
                   jax.ShapeDtypeStruct((KROWS, 2 * pairs * TILE), bf16),
                   jax.ShapeDtypeStruct((pairs, 2, 8, 8, TILE), f32)],
        compiler_params=pltpu.CompilerParams(dimension_semantics=("arbitrary",),
                                             vmem_limit_bytes=56 << 20),
        cost_estimate=pl.CostEstimate(flops=pairs * 10_000_000_000, bytes_accessed=pairs * 3_000_000,
                                      transcendentals=pairs * 2 * ROWS * (PLEN + CLEN)),
        name="attention_backward",
    )(meta, q, kv, kv, do, ctx, rest, lse, qaug, kaug, bias, pick)


EPSILON = 1e-06
THRESHOLDS = (12, 16, 23, 32, 46, 64, 91)
OWNER_BLOCK = (0, 3, 1, 2)


def python_bucket(offset):
    magnitude = abs(offset)
    base = NB // 2 if offset > 0 else 0
    if magnitude < 8:
        return base + magnitude
    return base + 8 + sum(1 for edge in THRESHOLDS if magnitude >= edge)


def bias_spread():
    spread = np.zeros((8, TILE, NB), np.float32)
    for lane in range(TILE):
        for d in range(3):
            inside = python_bucket(TILE * (d - 1) + lane - (TILE - 1))
            passed = python_bucket(TILE * d + lane - (TILE - 1))
            spread[2 * d, lane, inside] += 1
            spread[2 * d + 1, lane, passed] += 1
            spread[2 * d + 1, lane, inside] -= 1
    spread[6, :, python_bucket(-200)] = 1
    spread[7, :, python_bucket(200)] = 1
    return spread.reshape(8 * TILE, NB)


def setup_kernel(meta, limit, table, bias_ref, qaug_ref, kaug_ref, far_ref):
    head = pl.program_id(0)
    heads = pl.num_programs(0)
    near = (lax.broadcasted_iota(jnp.int32, (TILE, TILE), 0)
            - lax.broadcasted_iota(jnp.int32, (TILE, TILE), 1))
    for d in range(-2, 3):
        first, last = TILE * d - TILE + 1, TILE * d + TILE - 1
        previous = python_bucket(first)
        tile = jnp.full((TILE, TILE), table[previous * heads + head], f32)
        for n in range(first + 1, last + 1):
            current = python_bucket(n)
            if current != previous:
                tile = jnp.where(near >= n - TILE * d, table[current * heads + head], tile)
                previous = current
        bias_ref[0, (d + 2) * TILE:(d + 3) * TILE, :] = tile

    @pl.when(head == 0)
    def _():
        shape = (ROWS, TILE)
        sub = lax.broadcasted_iota(jnp.int32, shape, 1) & (DH - 1)
        qaug_ref[...] = jnp.where(sub == lax.broadcasted_iota(jnp.int32, shape, 0) // TILE, 1.0, 0.0).astype(bf16)
        shape = (KROWS, TILE)
        key = lax.broadcasted_iota(jnp.int32, shape, 0)
        sub = lax.broadcasted_iota(jnp.int32, shape, 1) & (DH - 1)
        kaug = jnp.zeros(shape, f32)
        for q in range(NQ):
            first = PLEN + CLEN * meta[NQ + q]
            hidden = (key >= PLEN) & ((key < first) | (key >= first + limit[q]))
            kaug = jnp.where(((sub == 2 * q) | (sub == 2 * q + 1)) & hidden, NEGATIVE, kaug)
        kaug_ref[...] = kaug.astype(bf16)
        lane = lax.broadcasted_iota(jnp.int32, (8, TILE), 1)
        for h in range(2):
            for row in range(16):
                key_tile = row if row < 8 else 8 + (row - 8) % 4
                for side in range(2):
                    out = jnp.zeros((8, TILE), f32)
                    for q in range(2 * NQ):
                        apart = key_tile - (meta[q // 2] + q % 2)
                        is_far = (apart <= -2) if side == 0 else (apart >= 2)
                        out = jnp.where(lane == q + (DH if h == 0 else 0), jnp.where(is_far, 1.0, 0.0), out)
                    far_ref[h, side, row] = out


def setup(me, spans, table):
    block = NQ * me + jnp.arange(NQ, dtype=jnp.int32)
    prompt = block < PLEN // QB
    cont = jnp.maximum(block - PLEN // QB, 0) // 2
    half = jnp.maximum(block - PLEN // QB, 0) % 2
    tile = jnp.where(prompt, 2 * block, PLEN // TILE + 2 * half)
    slot = jnp.where(prompt, 0, cont - (me - 1))
    chosen = cont[:, None] == jnp.arange(CONT, dtype=jnp.int32)[None, :]
    limit = jnp.where(prompt, 0, jnp.sum(jnp.where(chosen, spans[None, :], 0), axis=1)).astype(jnp.int32)
    meta = jnp.concatenate([tile, slot]).astype(jnp.int32)
    heads = table.shape[1]
    whole = lambda *shape: pl.BlockSpec(shape, lambda i, *_: (0,) * len(shape))
    bias, qaug, kaug, far = pl.pallas_call(
        setup_kernel,
        grid_spec=pltpu.PrefetchScalarGridSpec(
            num_scalar_prefetch=3,
            grid=(heads,),
            in_specs=[],
            out_specs=[pl.BlockSpec((1, 5 * TILE, TILE), lambda i, *_: (i, 0, 0)),
                       whole(ROWS, TILE), whole(KROWS, TILE), whole(2, 2, 16, 8, TILE)],
        ),
        out_shape=[jax.ShapeDtypeStruct((heads, 5 * TILE, TILE), f32),
                   jax.ShapeDtypeStruct((ROWS, TILE), bf16),
                   jax.ShapeDtypeStruct((KROWS, TILE), bf16),
                   jax.ShapeDtypeStruct((2, 2, 16, 8, TILE), f32)],
        compiler_params=pltpu.CompilerParams(dimension_semantics=("arbitrary",)),
        cost_estimate=pl.CostEstimate(flops=30_000_000, bytes_accessed=5_000_000, transcendentals=0),
        name="setup",
    )(meta, limit, table.astype(f32).reshape(-1))
    return meta, bias, qaug, kaug, far


def by_rows(x):
    return with_layout_constraint(x, Layout(tuple(range(x.ndim))))


def rms(rows):
    return lax.rsqrt(jnp.mean(rows * rows, axis=1, keepdims=True) + EPSILON)


def normed_rows(rows, gain):
    rows = rows.astype(f32)
    return (rows * rms(rows) * gain).astype(bf16)


def contract_rows(left, right):
    return lax.dot_general(left, right, (((0,), (0,)), ((), ())), preferred_element_type=f32)


def block_of(rows, i):
    return rows[i * QB:(i + 1) * QB]


def send(rows, pairs):
    return lax.ppermute(rows, "seq", pairs)


def pick_by(me, *choices):
    out = choices[-1]
    for i in range(len(choices) - 2, -1, -1):
        out = jnp.where(me == i, choices[i], out)
    return out


def exchange_rows(me, own):
    low, high = own[:ROWS // 2], own[ROWS // 2:]
    return (send(jnp.where(me == 2, high, low), [(0, 1), (1, 0), (2, 3), (3, 2)]),
            send(jnp.where(me == 0, high, low), [(0, 2), (1, 3)]))


def exchange_again(me, own, across, down):
    low, high = own[:ROWS // 2], own[ROWS // 2:]
    return (send(jnp.where(me == 0, high, down), [(0, 1), (2, 3), (3, 2)]),
            send(jnp.where(me == 0, low, across), [(0, 2), (1, 3)]))


def seen_rows(me, own, got):
    across, down, across_again, down_again = got
    mine = [block_of(own, i) for i in range(NQ)]
    low, high = own[:ROWS // 2], own[ROWS // 2:]
    prompt = [
        pick_by(me, low, across, down_again, down_again),
        pick_by(me, high, across_again, down, across_again),
        pick_by(me, across[:QB], mine[0], across_again[:QB], down[:QB]),
    ]
    slots = [
        pick_by(me, mine[0], mine[1], mine[0], across[ROWS // 2 - QB:]),
        pick_by(me, mine[1], mine[2], mine[1], mine[0]),
        pick_by(me, mine[1], mine[1], mine[2], mine[1]),
        pick_by(me, mine[2], mine[2], across[:QB], mine[2]),
    ]
    return jnp.concatenate(prompt + slots, axis=0)


def halve(rows, bit, axis, pairs):
    n, r, c = rows.shape
    parts = rows.reshape(n, 2, r // 2, c)
    away = lax.dynamic_index_in_dim(parts, 1 - bit, 1, keepdims=False)
    kept = lax.dynamic_index_in_dim(parts, bit, 1, keepdims=False)
    got = lax.ppermute(away, axis, pairs)
    return (kept.astype(f32) + got.astype(f32)).astype(bf16)


def join(rows, bit, axis, pairs):
    got = lax.ppermute(rows, axis, pairs)
    return jnp.concatenate([jnp.where(bit == 0, rows, got), jnp.where(bit == 0, got, rows)], axis=-2)


def seq_bits(me, order):
    steps = {"x": (me % 2, [(i, i ^ 1) for i in range(4)]), "y": (me // 2, [(i, i ^ 2) for i in range(4)])}
    return [steps[name] for name in order]


class Owned:
    def __init__(self, grad, me, order):
        self.step, self.steps = 0, seq_bits(me, order)
        self.rows = grad
        if lax.axis_size("wshard") != 8:
            self.rows = quarter_sum(lax.psum_scatter(grad, "wshard", scatter_dimension=0, tiled=True))
            self.step = 5

    def advance(self):
        place = lax.axis_index("wshard")
        flip = lambda bit: [(i, i ^ bit) for i in range(8)]
        step, rows = self.step, self.rows
        if step == 0:
            rows = halve(rows.reshape(4, -1, rows.shape[1]), place % 2, "wshard", flip(1))
        elif step in (1, 2):
            rows = halve(rows, self.steps[step - 1][0], "seq", self.steps[step - 1][1])
        elif step == 3:
            rows = halve(rows.reshape(1, -1, rows.shape[2]), place // 4, "wshard", flip(4))
        elif step == 4:
            rows = halve(rows, place // 2 % 2, "wshard", flip(2))[0]
        self.step, self.rows = step + 1, rows

    def finish(self):
        while self.step < 5:
            self.advance()
        return self.rows


def beside(rows, bit, axis, pairs, dim):
    got = lax.ppermute(rows, axis, pairs)
    return jnp.stack([jnp.where(bit == 0, rows, got), jnp.where(bit == 0, got, rows)], axis=dim)


class Gathered:
    def __init__(self, me, w_ff, w_out):
        self.plain = lax.axis_size("wshard") != 8
        if self.plain:
            self.state = [lax.all_gather(w, "wshard", axis=0, tiled=True) for w in (w_ff, w_out)]
            return
        place = lax.axis_index("wshard")
        self.core, self.depth = place % 2, place // 2
        self.n, self.m = w_ff.shape[0] // 4, w_out.shape[0] // 4
        self.cut = 2 * self.n // 3
        quarter = jnp.concatenate([lax.dynamic_slice_in_dim(w_ff, me * self.n, self.n, 0),
                                   lax.dynamic_slice_in_dim(w_out, me * self.m, self.m, 0)], axis=0)
        self.state = [quarter] + [
            lax.ppermute(quarter, "wshard", [(i, ((i // 2 + k) % 4) * 2 + i % 2) for i in range(8)])
            for k in range(1, 4)]
        self.steps = [seq_bits(me, "xy"), seq_bits(me, "yx")]

    def exchange(self, i):
        if self.plain:
            return
        if i == 0:
            rows = jnp.stack([pick_by((self.depth - d) % 4, *self.state) for d in range(4)])
            self.state = [rows[:, :self.cut], rows[:, self.cut:]]
        self.state = [beside(rows, steps[i][0], "seq", steps[i][1], dim)
                      for rows, steps, dim in zip(self.state, self.steps, (1, 1 + i))]

    def cores(self):
        if not self.plain:
            self.state = [beside(rows, self.core, "wshard", [(i, i ^ 1) for i in range(8)], 1)
                          for rows in self.state]

    def tie(self, others):
        others, self.state = lax.optimization_barrier((others, self.state))
        return others

    def whole(self):
        if self.plain:
            return self.state
        first, last = self.state
        c = first.shape[-1]
        keep = self.n - self.cut
        w_ff = jnp.concatenate([first, last[..., :keep, :]], axis=-2).reshape(32 * self.n, c)
        return w_ff, last[..., keep:, :].reshape(32 * self.m, c)


def quarter_sum(rows):
    parts = lax.all_to_all(rows.reshape(4, -1, rows.shape[1]), "seq", split_axis=0, concat_axis=0, tiled=True)
    return jnp.sum(parts.astype(f32), axis=0).astype(bf16)


def join_quarters(rows, me):
    steps = seq_bits(me, "xy")
    rows = beside(rows, *steps[0][:1], "seq", steps[0][1], 0)
    return beside(rows, steps[1][0], "seq", steps[1][1], 0).reshape((4,) + rows.shape[1:])


def sum_prompt(me, partial):
    owner = jnp.array(OWNER_BLOCK, jnp.int32)

    def take(device):
        start = owner[device] * QB
        return lax.dynamic_slice_in_dim(partial, start, QB, 0)

    total = take(me).astype(f32)
    for flip in (1, 2, 3):
        total = total + send(take(me ^ flip), [(i, i ^ flip) for i in range(4)]).astype(f32)
    parts = [block_of(partial, i) for i in range(8)]
    crossed = send(jnp.where(me == 2, parts[7], parts[4]), [(2, 3), (3, 2)])
    zero = jnp.zeros_like(parts[0])
    joined = (jnp.where(me == 2, parts[6], parts[5]).astype(f32) + crossed.astype(f32)).astype(bf16)
    rows = [
        total.astype(bf16),
        pick_by(me, zero, zero, parts[4], joined),
        pick_by(me, zero, parts[4], parts[5], parts[6]),
        pick_by(me, zero, parts[5], joined, parts[7]),
    ]
    return jnp.concatenate(rows, axis=0)


CHUNKS = (4, 2)


def interleave(key_part, value_part):
    r, w = key_part.shape
    both = jnp.stack([key_part.reshape(r, w // TILE, TILE), value_part.reshape(r, w // TILE, TILE)], axis=2)
    return both.reshape(r, 2 * w)


def local(tokens, teacher, lengths, w_query, w_key, w_value, w_out, w_in, w_ff, gain_attn, gain_ff, bias_table):
    me = lax.axis_index("seq")
    own = by_rows(tokens[0])
    inputs = own.astype(f32)
    targets = teacher[0].astype(f32)
    spans = lengths[0]
    width = own.shape[1]
    pairs = width // TILE

    def gather(w):
        return lax.all_gather(w, "wshard", axis=0, tiled=True)

    w_kv = interleave(w_key, w_value)
    gain_columns = jnp.pad(jnp.stack([gain_attn, gain_ff], axis=1), ((0, 0), (0, TILE - 2)))
    first = gather(jnp.concatenate([w_query, w_kv, gain_columns], axis=1))
    full_query, full_kv = first[:, :width], first[:, width:3 * width]
    gains = first[:, 3 * width:3 * width + 2].astype(f32).T
    gain_one, gain_two = gains[0], gains[1]
    gathered = Gathered(me, w_ff, w_out)
    full_in = gather(w_in)
    got = exchange_rows(me, own)
    got, spans, table = gathered.tie((got, spans, bias_table))
    got = got + exchange_again(me, own, *got)
    gathered.exchange(0)
    prepared = setup(me, spans, table)
    inverse_one = rms(inputs)
    got, prepared, inverse_one = gathered.tie((got, prepared, inverse_one))
    meta, bias, qaug, kaug, far = prepared
    gathered.exchange(1)
    normed_own = by_rows((inputs * inverse_one * gain_one).astype(bf16))
    normed_seen = by_rows(normed_rows(by_rows(seen_rows(me, own, got)), gain_one))
    queries = jnp.dot(normed_own, full_query, preferred_element_type=f32).astype(bf16)
    keys_values = jnp.dot(normed_seen, full_kv, preferred_element_type=f32).astype(bf16)
    queries, keys_values = gathered.tie((queries, keys_values))
    gathered.cores()
    context, rest, lse = gathered.tie(attention_forward(meta, queries, keys_values, qaug, kaug, bias, 0, pairs))
    full_ff, full_out = gathered.whole()
    middle = by_rows(inputs + jnp.dot(context, full_out, preferred_element_type=f32))
    inverse_two = rms(middle)
    normed_two = by_rows((middle * inverse_two * gain_two).astype(bf16))
    hidden_act = jnp.maximum(jnp.dot(normed_two, full_in, preferred_element_type=f32), 0.0).astype(bf16)
    final_rows = middle + jnp.dot(hidden_act, full_ff, preferred_element_type=f32)
    local_rows = inputs.shape[0]
    row_index = me * local_rows + lax.iota(jnp.int32, local_rows)
    slot_index = jnp.maximum(row_index - PLEN, 0)
    owner_match = (slot_index // CLEN)[:, None] == lax.iota(jnp.int32, CONT)[None, :]
    row_limit = jnp.sum(jnp.where(owner_match, spans[None, :], 0), axis=1)
    valid_rows = (row_index < PLEN) | (slot_index % CLEN < row_limit)
    row_count = PLEN + jnp.sum(spans).astype(f32)
    factor = (PLEN + CONT * CLEN) / row_count
    d_final = jnp.where(valid_rows[:, None], factor * (final_rows - targets), 0.0)
    d_final = by_rows(d_final)
    d_branch_two = by_rows(d_final.astype(bf16))

    def owners(g):
        return lax.psum_scatter(g, "wshard", scatter_dimension=0, tiled=True)

    size = gain_attn.shape[0]
    owned_ff = Owned(contract_rows(hidden_act, d_branch_two).astype(bf16), me, "yx")
    owned_ff.advance()
    d_pre = jnp.where(hidden_act > 0, dot_nt(d_branch_two, full_ff), 0.0).astype(bf16)
    grad_in = contract_rows(normed_two, d_pre).astype(bf16)
    d_normed_two = by_rows(dot_nt(d_pre, full_in))
    d_normed_two, owned_ff.rows = lax.optimization_barrier((d_normed_two, owned_ff.rows))
    owned_ff.advance()
    scaled_two = middle * inverse_two
    d_scaled_two = d_normed_two * gain_two
    d_middle = d_final + inverse_two * (
        d_scaled_two - scaled_two * jnp.mean(d_scaled_two * scaled_two, axis=1, keepdims=True))
    d_middle = by_rows(d_middle)
    d_branch_one = by_rows(d_middle.astype(bf16))
    grad_out = contract_rows(context, d_branch_one).astype(bf16)
    d_context = dot_nt(d_branch_one, full_out).astype(bf16)
    share_in = owners(grad_in)
    d_context, grad_out = lax.optimization_barrier((d_context, grad_out))

    starts = [sum(CHUNKS[:i]) for i in range(len(CHUNKS))]
    cuts = [(starts[i] * TILE, (starts[i] + CHUNKS[i]) * TILE) for i in range(len(CHUNKS))]

    def backward(meta, i):
        return attention_backward(meta, queries, keys_values, d_context, context, rest, lse, qaug, kaug, bias, far,
                                  starts[i], CHUNKS[i])

    def weight_grad(d_q, d_kv):
        return jnp.concatenate([by_rows(contract_rows(normed_own, d_q).astype(bf16)),
                                by_rows(contract_rows(normed_seen, d_kv).astype(bf16))], axis=1)

    def back_to_rows(i, d_q, d_kv):
        lo, hi = cuts[i]
        return by_rows(dot_nt(d_q, full_query[:, lo:hi])), by_rows(dot_nt(d_kv, full_kv[:, 2 * lo:2 * hi]))

    first = backward(meta, 0)
    meta, first, owned_ff.rows, share_in = lax.optimization_barrier((meta, first, owned_ff.rows, share_in))
    owned_ff.advance()
    grad_first = jnp.concatenate([weight_grad(*first[:2]), grad_out], axis=1)
    f_first = back_to_rows(0, *first[:2])
    meta, grad_first, f_first = lax.optimization_barrier((meta, grad_first, f_first))
    share_first = owners(grad_first)
    second = backward(meta, 1)
    second, owned_ff.rows, share_first = lax.optimization_barrier((second, owned_ff.rows, share_first))
    grad_second = weight_grad(*second[:2])
    heads = bias_table.shape[1]
    near = jnp.sum(jnp.concatenate([first[2], second[2]], axis=0), axis=3).reshape(heads, 8 * TILE)
    bias_local = jnp.dot(near, jnp.asarray(bias_spread()), precision=lax.Precision.HIGHEST).reshape(1, -1)
    bias_top = bias_local.astype(bf16)
    bias_rest = (bias_local - bias_top.astype(f32)).astype(bf16)
    n_bias = bias_local.shape[1]
    n_last = grad_second.shape[1]
    bias_rows = jnp.pad(jnp.concatenate([bias_top, bias_rest], axis=1), ((0, 7), (0, n_last - 2 * n_bias)))
    blocks = grad_second.reshape(-1, size, n_last)
    bias_rows = jnp.broadcast_to(bias_rows[None], (blocks.shape[0],) + bias_rows.shape)
    last = jnp.concatenate([blocks, bias_rows], axis=1).reshape(-1, n_last)
    share_last = owners(last)
    f_second = back_to_rows(1, *second[:2])
    f_query = f_first[0] + f_second[0]
    f_summed = by_rows(sum_prompt(me, by_rows((f_first[1] + f_second[1]).astype(bf16))))
    quarter_ff = owned_ff.finish()
    shares_out = jnp.concatenate([share.reshape(-1, width) for share in (share_in, share_first)], axis=0)
    quarter_out = quarter_sum(shares_out)
    share_last, f_summed, quarter_ff, quarter_out = lax.optimization_barrier(
        (share_last, f_summed, quarter_ff, quarter_out))
    quarters = [quarter_ff, quarter_out]
    f_block = f_summed[:QB]
    from_two = send(f_block, [(2, 0)])
    from_three = send(f_block, [(3, 0)])
    f_own = f_query + (f_summed[QB:] + jnp.concatenate(
        [jnp.where(me < 2, f_block, jnp.zeros_like(f_block)), from_two, from_three], axis=0)).astype(f32)
    scaled_one = inputs * inverse_one
    d_scaled_one = f_own * gain_one
    d_tokens = d_middle + inverse_one * (
        d_scaled_one - scaled_one * jnp.mean(d_scaled_one * scaled_one, axis=1, keepdims=True))

    size = gain_attn.shape[0]
    n_quarter = quarter_ff.shape[0]
    early = join_quarters(jnp.concatenate(quarters, axis=0), me)
    share_ff = early[:, :n_quarter].reshape(-1, width).astype(f32)
    others = early[:, n_quarter:].reshape(-1, width).astype(f32)
    n_in = share_in.shape[0] * share_in.shape[1] // width
    share_in = others[:n_in].reshape(size, -1)
    share_first = others[n_in:].reshape(size, -1)
    share_out = share_first[:, -width:]
    late = join_quarters(quarter_sum(share_last.reshape(-1, width)), me).reshape(-1, n_last).astype(f32)
    shares = [share_first[:, :-width], late[:size]]
    bias_grad = (late[size, :n_bias] + late[size, n_bias:2 * n_bias]).reshape(heads, NB).T
    share_query = jnp.concatenate(
        [share[:, :count * TILE] for share, count in zip(shares, CHUNKS)], axis=1)
    share_kv = jnp.concatenate(
        [share[:, count * TILE:] for share, count in zip(shares, CHUNKS)], axis=1)
    share_kv = share_kv.reshape(share_kv.shape[0], pairs, 2, TILE)
    share_key = share_kv[:, :, 0].reshape(-1, width)
    share_value = share_kv[:, :, 1].reshape(-1, width)
    gain_grad_one = (jnp.sum(share_query * w_query.astype(f32), axis=1)
                     + jnp.sum(share_key * w_key.astype(f32), axis=1)
                     + jnp.sum(share_value * w_value.astype(f32), axis=1)) / gain_attn.astype(f32)
    gain_grad_two = jnp.sum(share_in * w_in.astype(f32), axis=1) / gain_ff.astype(f32)
    return (
        final_rows.astype(bf16)[None],
        d_tokens[None],
        share_query,
        share_key,
        share_value,
        share_out,
        share_in,
        share_ff,
        gain_grad_one,
        gain_grad_two,
        bias_grad,
    )


def solution(mesh):
    rows = P("wshard", "seq", None)
    weight = P("wshard", None)
    placed = (rows, rows) + (weight,) * 7 + (P("wshard"), P("wshard"), P())
    return jax.shard_map(
        local,
        mesh=mesh,
        in_specs=placed,
        out_specs=(rows, rows) + (weight,) * 6 + (P("wshard"), P("wshard"), P()),
        check_vma=False,
    )
```

```python
import jax
import jax.numpy as jnp
import numpy as np
from jax import lax
from jax.experimental import pallas as pl
from jax.experimental.pallas import tpu as pltpu
from jax.experimental.layout import Layout, with_layout_constraint
from jax.sharding import PartitionSpec as P

DH = 64
NB = 32
PLEN = 1024
CLEN = 512
CONT = 4
QB = 256
NQ = 3
ROWS = QB * NQ
KROWS = PLEN + 2 * CLEN
TILE = 128
NEGATIVE = -1e30
f32 = jnp.float32
bf16 = jnp.bfloat16


def dot_nt(a, b):
    return lax.dot_general(a, b, (((1,), (1,)), ((), ())), preferred_element_type=f32)


def dot_nn(a, b):
    return lax.dot_general(a, b, (((1,), (0,)), ((), ())), preferred_element_type=f32)


def low_lanes(shape):
    return lax.broadcasted_iota(jnp.int32, shape, 1) < DH


def add_bias(s, bias_ref, head, kc, qc):
    rows = []
    for a in range(s.shape[0] // TILE):
        cols = []
        for b in range(s.shape[1] // TILE):
            d = jnp.clip(kc + a - qc[b], -2, 2) + 2
            cols.append(bias_ref[head, pl.ds(pl.multiple_of(d * TILE, TILE), TILE), :])
        rows.append(jnp.concatenate(cols, axis=1))
    return s + jnp.concatenate(rows, axis=0)


def forward_kernel(meta, q_ref, k_ref, v_ref, qaug_ref, kaug_ref, bias_ref, ctx_ref, rest_ref, lse_ref,
                   k_scr, vt_scr, s_scr):
    low_k = low_lanes((KROWS, TILE))
    low_q = low_lanes((QB, TILE))
    k_scr[0] = jnp.where(low_k, k_ref[...], kaug_ref[...])
    k_scr[1] = jnp.where(low_k, kaug_ref[...], k_ref[...])
    vt_scr[...] = v_ref[...].T
    KC = 512
    for qb in range(NQ):
        qc = meta[qb]
        slot = pl.multiple_of(PLEN + meta[NQ + qb] * CLEN, CLEN)
        q = q_ref[qb * QB:(qb + 1) * QB, :]
        qa = qaug_ref[qb * QB:(qb + 1) * QB, :]
        outs = []
        for h in range(2):
            qh = jnp.where(low_q, q, qa) if h == 0 else jnp.where(low_q, qa, q)
            m = None
            for c in range(3):
                kk = k_scr[h, c * KC:(c + 1) * KC, :] if c < 2 else k_scr[h, pl.ds(slot, KC), :]
                s = dot_nt(kk, qh)
                s = add_bias(s, bias_ref, h, 4 * c, (qc, qc + 1))
                s_scr[h, c * KC:(c + 1) * KC, :] = s
                mc = jnp.max(s, axis=0, keepdims=True)
                m = mc if m is None else jnp.maximum(m, mc)
            l = None
            acc = None
            for c in range(3):
                p = jnp.exp(s_scr[h, c * KC:(c + 1) * KC, :] - m)
                lc = jnp.sum(p, axis=0, keepdims=True)
                l = lc if l is None else l + lc
                vv = (vt_scr[h * DH:(h + 1) * DH, c * KC:(c + 1) * KC] if c < 2
                      else vt_scr[h * DH:(h + 1) * DH, pl.ds(slot, KC)])
                o = dot_nn(vv, p.astype(bf16))
                acc = o if acc is None else acc + o
            outs.append(acc / l)
            lse_ref[0, h:h + 1, qb * QB:(qb + 1) * QB] = m + jnp.log(l)
        ctx = jnp.concatenate(outs, axis=0).T
        ctx_low = ctx.astype(bf16)
        ctx_ref[qb * QB:(qb + 1) * QB, :] = ctx_low
        rest_ref[qb * QB:(qb + 1) * QB, :] = (ctx - ctx_low.astype(f32)).astype(bf16)


def attention_forward(meta, q, kv, qaug, kaug, bias, first, pairs):
    own = pl.BlockSpec((ROWS, TILE), lambda i, meta: (0, first + i))
    out = pl.BlockSpec((ROWS, TILE), lambda i, meta: (0, i))
    keys = pl.BlockSpec((KROWS, TILE), lambda i, meta: (0, 2 * (first + i)))
    values = pl.BlockSpec((KROWS, TILE), lambda i, meta: (0, 2 * (first + i) + 1))
    fixed = lambda rows: pl.BlockSpec((rows, TILE), lambda i, meta: (0, 0))
    return pl.pallas_call(
        forward_kernel,
        grid_spec=pltpu.PrefetchScalarGridSpec(
            num_scalar_prefetch=1,
            grid=(pairs,),
            in_specs=[own, keys, values, fixed(ROWS), fixed(KROWS),
                      pl.BlockSpec((2, 5 * TILE, TILE), lambda i, meta: (first + i, 0, 0))],
            out_specs=[out, out, pl.BlockSpec((1, 2, ROWS), lambda i, meta: (i, 0, 0))],
            scratch_shapes=[
                pltpu.VMEM((2, KROWS, TILE), bf16),
                pltpu.VMEM((TILE, KROWS), bf16),
                pltpu.VMEM((2, PLEN + CLEN, QB), f32),
            ],
        ),
        out_shape=[jax.ShapeDtypeStruct((ROWS, pairs * TILE), bf16),
                   jax.ShapeDtypeStruct((ROWS, pairs * TILE), bf16),
                   jax.ShapeDtypeStruct((pairs, 2, ROWS), f32)],
        compiler_params=pltpu.CompilerParams(dimension_semantics=("arbitrary",),
                                             vmem_limit_bytes=56 << 20),
        cost_estimate=pl.CostEstimate(flops=pairs * 5_000_000_000, bytes_accessed=pairs * 2_000_000,
                                      transcendentals=pairs * 2 * ROWS * (PLEN + CLEN)),
        name="attention_forward",
    )(meta, q, kv, kv, qaug, kaug, bias)


PAD = TILE


def fold_rows(rows):
    return jnp.sum(rows.reshape(rows.shape[0] // 8, 8, rows.shape[1]), axis=0)


def backward_kernel(meta, q_ref, k_ref, v_ref, do_ref, ctx_ref, rest_ref, lse_ref, qaug_ref, kaug_ref,
                    bias_ref, pick_ref, dq_ref, dkv_ref, near_ref,
                    k_scr, kt_scr, q_scr, do_scr, delta_scr, ds_scr, dks_scr, dvs_scr, far_scr):
    low_k = low_lanes((KROWS, TILE))
    low_q = low_lanes((ROWS, TILE))
    k_scr[0] = jnp.where(low_k, k_ref[...], kaug_ref[...])
    k_scr[1] = jnp.where(low_k, kaug_ref[...], k_ref[...])
    kt_scr[...] = k_ref[...].T
    q_scr[0] = jnp.where(low_q, q_ref[...], qaug_ref[...])
    q_scr[1] = jnp.where(low_q, qaug_ref[...], q_ref[...])
    zero = jnp.zeros((ROWS, TILE), bf16)
    do_scr[0] = jnp.where(low_q, do_ref[...], zero)
    do_scr[1] = jnp.where(low_q, zero, do_ref[...])
    prod = do_ref[...].astype(f32) * (ctx_ref[...].astype(f32) + rest_ref[...].astype(f32))
    hi = prod.astype(bf16)
    lo = (prod - hi.astype(f32)).astype(bf16)
    pick_row = lax.broadcasted_iota(jnp.int32, (8, TILE), 0)
    pick_low = low_lanes((8, TILE))
    pick = jnp.where((pick_row == 0) & pick_low | (pick_row == 1) & ~pick_low, 1.0, 0.0).astype(bf16)
    delta_scr[...] = dot_nt(pick, hi) + dot_nt(pick, lo)
    for h in range(2):
        ds_scr[h, 0:PAD, :] = jnp.zeros((PAD, ROWS), bf16)
        ds_scr[h, PAD + PLEN + CLEN:, :] = jnp.zeros((PAD, ROWS), bf16)

    def piece(h, kk, vv, kc, qb):
        cols = slice(qb * QB, (qb + 1) * QB)
        s = dot_nt(kk, q_scr[h, cols, :])
        qc = meta[qb]
        s = add_bias(s, bias_ref, h, kc, (qc, qc + 1))
        p = jnp.exp(s - lse_ref[0, h:h + 1, cols])
        dp = dot_nt(vv, do_scr[h, cols, :])
        ds = (p * (dp - delta_scr[h:h + 1, cols])).astype(bf16)
        return p.astype(bf16), ds

    low_c = low_lanes((QB, TILE))

    def prompt_chunk(c, carry):
        start = pl.multiple_of(c * QB, QB)
        dv = None
        dks = []
        for h in range(2):
            kk = k_scr[h, pl.ds(start, QB), :]
            vv = v_ref[pl.ds(start, QB), :]
            dk = None
            for qb in range(NQ):
                cols = slice(qb * QB, (qb + 1) * QB)
                p, ds = piece(h, kk, vv, 2 * c, qb)
                ds_scr[h, pl.ds(PAD + start, QB), cols] = ds
                a = dot_nn(p, do_scr[h, cols, :])
                b = dot_nn(ds, q_scr[h, cols, :])
                dv = a if dv is None else dv + a
                dk = b if dk is None else dk + b
            dks.append(dk)
        dkv_ref[pl.ds(start, QB), TILE:] = dv.astype(bf16)
        dkv_ref[pl.ds(start, QB), :TILE] = jnp.where(low_c, dks[0], dks[1]).astype(bf16)
        sums = jnp.where(low_c, dks[1], dks[0])
        far_scr[2 * c] = fold_rows(sums[:TILE])
        far_scr[2 * c + 1] = fold_rows(sums[TILE:])
        return carry

    lax.fori_loop(0, PLEN // QB, prompt_chunk, 0)
    dvs_scr[...] = jnp.zeros_like(dvs_scr)
    dks_scr[...] = jnp.zeros_like(dks_scr)
    for qb in range(NQ):
        cols = slice(qb * QB, (qb + 1) * QB)
        slot = pl.multiple_of(meta[NQ + qb] * CLEN, CLEN)
        for half in range(CLEN // QB):
            start = pl.multiple_of(slot + half * QB, QB)
            dv = None
            for h in range(2):
                kk = k_scr[h, pl.ds(PLEN + start, QB), :]
                vv = v_ref[pl.ds(PLEN + start, QB), :]
                p, ds = piece(h, kk, vv, 8 + 2 * half, qb)
                ds_scr[h, PAD + PLEN + half * QB:PAD + PLEN + (half + 1) * QB, cols] = ds
                a = dot_nn(p, do_scr[h, cols, :])
                dv = a if dv is None else dv + a
                dks_scr[h, pl.ds(start, QB), :] += dot_nn(ds, q_scr[h, cols, :])
            dvs_scr[pl.ds(start, QB), :] += dv
    dkv_ref[PLEN:, TILE:] = dvs_scr[...].astype(bf16)
    low_s = low_lanes((2 * CLEN, TILE))
    dkv_ref[PLEN:, :TILE] = jnp.where(low_s, dks_scr[0], dks_scr[1]).astype(bf16)
    sums = jnp.where(low_s, dks_scr[1], dks_scr[0])
    for t in range(2 * CLEN // TILE):
        far_scr[8 + t] = fold_rows(sums[t * TILE:(t + 1) * TILE])

    dqt = []
    for h in range(2):
        parts = []
        for qb in range(NQ):
            cols = slice(qb * QB, (qb + 1) * QB)
            slot = pl.multiple_of(PLEN + meta[NQ + qb] * CLEN, CLEN)
            rows = slice(h * DH, (h + 1) * DH)
            a = dot_nn(kt_scr[rows, 0:PLEN], ds_scr[h, PAD:PAD + PLEN, cols])
            b = dot_nn(kt_scr[rows, pl.ds(slot, CLEN)], ds_scr[h, PAD + PLEN:PAD + PLEN + CLEN, cols])
            parts.append(a + b)
        dqt.append(jnp.concatenate(parts, axis=1))
    dq_ref[...] = jnp.concatenate(dqt, axis=0).T.astype(bf16)

    row_id = lax.broadcasted_iota(jnp.int32, (TILE, TILE), 0)
    lane_id = lax.broadcasted_iota(jnp.int32, (TILE, TILE), 1)
    flip = jnp.where(row_id + lane_id == TILE - 1, 1.0, 0.0).astype(bf16)
    for h in range(2):
        acc = None
        for sub in range(2 * NQ):
            qc = meta[sub // 2] + sub % 2
            start = pl.multiple_of(qc * TILE, TILE)
            part = ds_scr[h, pl.ds(start, 3 * TILE), sub * TILE:(sub + 1) * TILE].astype(f32)
            acc = part if acc is None else acc + part
        top = acc.astype(bf16)
        acc = dot_nn(top, flip) + dot_nn((acc - top.astype(f32)).astype(bf16), flip)
        sums = []
        for d in range(3):
            rolled = pltpu.roll(acc[d * TILE:(d + 1) * TILE], 0, 1, stride=1, stride_axis=0)
            wrapped = jnp.where(lane_id < row_id, rolled, 0.0)
            sums += [fold_rows(rolled), fold_rows(wrapped)]
        for side in range(2):
            total = None
            for t in range(16):
                term = far_scr[t] * pick_ref[h, side, t]
                total = term if total is None else total + term
            sums.append(total)
        for i, eight in enumerate(sums):
            near_ref[0, h, i] = eight


def attention_backward(meta, q, kv, do, ctx, rest, lse, qaug, kaug, bias, pick, first, pairs):
    own = pl.BlockSpec((ROWS, TILE), lambda i, meta: (0, first + i))
    keys = pl.BlockSpec((KROWS, TILE), lambda i, meta: (0, 2 * (first + i)))
    values = pl.BlockSpec((KROWS, TILE), lambda i, meta: (0, 2 * (first + i) + 1))
    fixed = lambda rows: pl.BlockSpec((rows, TILE), lambda i, meta: (0, 0))
    return pl.pallas_call(
        backward_kernel,
        grid_spec=pltpu.PrefetchScalarGridSpec(
            num_scalar_prefetch=1,
            grid=(pairs,),
            in_specs=[own, keys, values, own, own, own,
                      pl.BlockSpec((1, 2, ROWS), lambda i, meta: (first + i, 0, 0)),
                      fixed(ROWS), fixed(KROWS),
                      pl.BlockSpec((2, 5 * TILE, TILE), lambda i, meta: (first + i, 0, 0)),
                      pl.BlockSpec((2, 2, 16, 8, TILE), lambda i, meta: (0, 0, 0, 0, 0))],
            out_specs=[pl.BlockSpec((ROWS, TILE), lambda i, meta: (0, i)),
                       pl.BlockSpec((KROWS, 2 * TILE), lambda i, meta: (0, i)),
                       pl.BlockSpec((1, 2, 8, 8, TILE), lambda i, meta: (i, 0, 0, 0, 0))],
            scratch_shapes=[
                pltpu.VMEM((2, KROWS, TILE), bf16),
                pltpu.VMEM((TILE, KROWS), bf16),
                pltpu.VMEM((2, ROWS, TILE), bf16),
                pltpu.VMEM((2, ROWS, TILE), bf16),
                pltpu.VMEM((8, ROWS), f32),
                pltpu.VMEM((2, PLEN + CLEN + 2 * PAD, ROWS), bf16),
                pltpu.VMEM((2, 2 * CLEN, TILE), f32),
                pltpu.VMEM((2 * CLEN, TILE), f32),
                pltpu.VMEM((16, 8, TILE), f32),
            ],
        ),
        out_shape=[jax.ShapeDtypeStruct((ROWS, pairs * TILE), bf16),
                   jax.ShapeDtypeStruct((KROWS, 2 * pairs * TILE), bf16),
                   jax.ShapeDtypeStruct((pairs, 2, 8, 8, TILE), f32)],
        compiler_params=pltpu.CompilerParams(dimension_semantics=("arbitrary",),
                                             vmem_limit_bytes=56 << 20),
        cost_estimate=pl.CostEstimate(flops=pairs * 10_000_000_000, bytes_accessed=pairs * 3_000_000,
                                      transcendentals=pairs * 2 * ROWS * (PLEN + CLEN)),
        name="attention_backward",
    )(meta, q, kv, kv, do, ctx, rest, lse, qaug, kaug, bias, pick)


EPSILON = 1e-06
THRESHOLDS = (12, 16, 23, 32, 46, 64, 91)
OWNER_BLOCK = (0, 3, 1, 2)


def python_bucket(offset):
    magnitude = abs(offset)
    base = NB // 2 if offset > 0 else 0
    if magnitude < 8:
        return base + magnitude
    return base + 8 + sum(1 for edge in THRESHOLDS if magnitude >= edge)


def bias_spread():
    spread = np.zeros((8, TILE, NB), np.float32)
    for lane in range(TILE):
        for d in range(3):
            inside = python_bucket(TILE * (d - 1) + lane - (TILE - 1))
            passed = python_bucket(TILE * d + lane - (TILE - 1))
            spread[2 * d, lane, inside] += 1
            spread[2 * d + 1, lane, passed] += 1
            spread[2 * d + 1, lane, inside] -= 1
    spread[6, :, python_bucket(-200)] = 1
    spread[7, :, python_bucket(200)] = 1
    return spread.reshape(8 * TILE, NB)


def setup_kernel(meta, limit, table, bias_ref, qaug_ref, kaug_ref, far_ref):
    head = pl.program_id(0)
    heads = pl.num_programs(0)
    near = (lax.broadcasted_iota(jnp.int32, (TILE, TILE), 0)
            - lax.broadcasted_iota(jnp.int32, (TILE, TILE), 1))
    for d in range(-2, 3):
        first, last = TILE * d - TILE + 1, TILE * d + TILE - 1
        previous = python_bucket(first)
        tile = jnp.full((TILE, TILE), table[previous * heads + head], f32)
        for n in range(first + 1, last + 1):
            current = python_bucket(n)
            if current != previous:
                tile = jnp.where(near >= n - TILE * d, table[current * heads + head], tile)
                previous = current
        bias_ref[0, (d + 2) * TILE:(d + 3) * TILE, :] = tile

    @pl.when(head == 0)
    def _():
        shape = (ROWS, TILE)
        sub = lax.broadcasted_iota(jnp.int32, shape, 1) & (DH - 1)
        qaug_ref[...] = jnp.where(sub == lax.broadcasted_iota(jnp.int32, shape, 0) // TILE, 1.0, 0.0).astype(bf16)
        shape = (KROWS, TILE)
        key = lax.broadcasted_iota(jnp.int32, shape, 0)
        sub = lax.broadcasted_iota(jnp.int32, shape, 1) & (DH - 1)
        kaug = jnp.zeros(shape, f32)
        for q in range(NQ):
            first = PLEN + CLEN * meta[NQ + q]
            hidden = (key >= PLEN) & ((key < first) | (key >= first + limit[q]))
            kaug = jnp.where(((sub == 2 * q) | (sub == 2 * q + 1)) & hidden, NEGATIVE, kaug)
        kaug_ref[...] = kaug.astype(bf16)
        lane = lax.broadcasted_iota(jnp.int32, (8, TILE), 1)
        for h in range(2):
            for row in range(16):
                key_tile = row if row < 8 else 8 + (row - 8) % 4
                for side in range(2):
                    out = jnp.zeros((8, TILE), f32)
                    for q in range(2 * NQ):
                        apart = key_tile - (meta[q // 2] + q % 2)
                        is_far = (apart <= -2) if side == 0 else (apart >= 2)
                        out = jnp.where(lane == q + (DH if h == 0 else 0), jnp.where(is_far, 1.0, 0.0), out)
                    far_ref[h, side, row] = out


def setup(me, spans, table):
    block = NQ * me + jnp.arange(NQ, dtype=jnp.int32)
    prompt = block < PLEN // QB
    cont = jnp.maximum(block - PLEN // QB, 0) // 2
    half = jnp.maximum(block - PLEN // QB, 0) % 2
    tile = jnp.where(prompt, 2 * block, PLEN // TILE + 2 * half)
    slot = jnp.where(prompt, 0, cont - (me - 1))
    chosen = cont[:, None] == jnp.arange(CONT, dtype=jnp.int32)[None, :]
    limit = jnp.where(prompt, 0, jnp.sum(jnp.where(chosen, spans[None, :], 0), axis=1)).astype(jnp.int32)
    meta = jnp.concatenate([tile, slot]).astype(jnp.int32)
    heads = table.shape[1]
    whole = lambda *shape: pl.BlockSpec(shape, lambda i, *_: (0,) * len(shape))
    bias, qaug, kaug, far = pl.pallas_call(
        setup_kernel,
        grid_spec=pltpu.PrefetchScalarGridSpec(
            num_scalar_prefetch=3,
            grid=(heads,),
            in_specs=[],
            out_specs=[pl.BlockSpec((1, 5 * TILE, TILE), lambda i, *_: (i, 0, 0)),
                       whole(ROWS, TILE), whole(KROWS, TILE), whole(2, 2, 16, 8, TILE)],
        ),
        out_shape=[jax.ShapeDtypeStruct((heads, 5 * TILE, TILE), f32),
                   jax.ShapeDtypeStruct((ROWS, TILE), bf16),
                   jax.ShapeDtypeStruct((KROWS, TILE), bf16),
                   jax.ShapeDtypeStruct((2, 2, 16, 8, TILE), f32)],
        compiler_params=pltpu.CompilerParams(dimension_semantics=("arbitrary",)),
        cost_estimate=pl.CostEstimate(flops=30_000_000, bytes_accessed=5_000_000, transcendentals=0),
        name="setup",
    )(meta, limit, table.astype(f32).reshape(-1))
    return meta, bias, qaug, kaug, far


def by_rows(x):
    return with_layout_constraint(x, Layout(tuple(range(x.ndim))))


def rms(rows):
    return lax.rsqrt(jnp.mean(rows * rows, axis=1, keepdims=True) + EPSILON)


def normed_rows(rows, gain):
    rows = rows.astype(f32)
    return (rows * rms(rows) * gain).astype(bf16)


def contract_rows(left, right):
    return lax.dot_general(left, right, (((0,), (0,)), ((), ())), preferred_element_type=f32)


def block_of(rows, i):
    return rows[i * QB:(i + 1) * QB]


def send(rows, pairs):
    return lax.ppermute(rows, "seq", pairs)


def pick_by(me, *choices):
    out = choices[-1]
    for i in range(len(choices) - 2, -1, -1):
        out = jnp.where(me == i, choices[i], out)
    return out


def exchange_rows(me, own):
    low, high = own[:ROWS // 2], own[ROWS // 2:]
    return (send(jnp.where(me == 2, high, low), [(0, 1), (1, 0), (2, 3), (3, 2)]),
            send(jnp.where(me == 0, high, low), [(0, 2), (1, 3)]))


def exchange_again(me, own, across, down):
    low, high = own[:ROWS // 2], own[ROWS // 2:]
    return (send(jnp.where(me == 0, high, down), [(0, 1), (2, 3), (3, 2)]),
            send(jnp.where(me == 0, low, across), [(0, 2), (1, 3)]))


def seen_rows(me, own, got):
    across, down, across_again, down_again = got
    mine = [block_of(own, i) for i in range(NQ)]
    low, high = own[:ROWS // 2], own[ROWS // 2:]
    prompt = [
        pick_by(me, low, across, down_again, down_again),
        pick_by(me, high, across_again, down, across_again),
        pick_by(me, across[:QB], mine[0], across_again[:QB], down[:QB]),
    ]
    slots = [
        pick_by(me, mine[0], mine[1], mine[0], across[ROWS // 2 - QB:]),
        pick_by(me, mine[1], mine[2], mine[1], mine[0]),
        pick_by(me, mine[1], mine[1], mine[2], mine[1]),
        pick_by(me, mine[2], mine[2], across[:QB], mine[2]),
    ]
    return jnp.concatenate(prompt + slots, axis=0)


def halve(rows, bit, axis, pairs):
    n, r, c = rows.shape
    parts = rows.reshape(n, 2, r // 2, c)
    away = lax.dynamic_index_in_dim(parts, 1 - bit, 1, keepdims=False)
    kept = lax.dynamic_index_in_dim(parts, bit, 1, keepdims=False)
    got = lax.ppermute(away, axis, pairs)
    return (kept.astype(f32) + got.astype(f32)).astype(bf16)


def join(rows, bit, axis, pairs):
    got = lax.ppermute(rows, axis, pairs)
    return jnp.concatenate([jnp.where(bit == 0, rows, got), jnp.where(bit == 0, got, rows)], axis=-2)


def seq_bits(me, order):
    steps = {"x": (me % 2, [(i, i ^ 1) for i in range(4)]), "y": (me // 2, [(i, i ^ 2) for i in range(4)])}
    return [steps[name] for name in order]


class Owned:
    def __init__(self, grad, me, order):
        self.step, self.steps = 0, seq_bits(me, order)
        self.rows = grad
        if lax.axis_size("wshard") != 8:
            self.rows = quarter_sum(lax.psum_scatter(grad, "wshard", scatter_dimension=0, tiled=True))
            self.step = 5

    def advance(self):
        place = lax.axis_index("wshard")
        flip = lambda bit: [(i, i ^ bit) for i in range(8)]
        step, rows = self.step, self.rows
        if step == 0:
            rows = halve(rows.reshape(4, -1, rows.shape[1]), place % 2, "wshard", flip(1))
        elif step in (1, 2):
            rows = halve(rows, self.steps[step - 1][0], "seq", self.steps[step - 1][1])
        elif step == 3:
            rows = halve(rows.reshape(1, -1, rows.shape[2]), place // 4, "wshard", flip(4))
        elif step == 4:
            rows = halve(rows, place // 2 % 2, "wshard", flip(2))[0]
        self.step, self.rows = step + 1, rows

    def finish(self):
        while self.step < 5:
            self.advance()
        return self.rows


def beside(rows, bit, axis, pairs, dim):
    got = lax.ppermute(rows, axis, pairs)
    return jnp.stack([jnp.where(bit == 0, rows, got), jnp.where(bit == 0, got, rows)], axis=dim)


class Gathered:
    def __init__(self, me, w_ff, w_out):
        self.plain = lax.axis_size("wshard") != 8
        if self.plain:
            self.state = [lax.all_gather(w, "wshard", axis=0, tiled=True) for w in (w_ff, w_out)]
            return
        place = lax.axis_index("wshard")
        self.core, self.depth = place % 2, place // 2
        self.n, self.m = w_ff.shape[0] // 4, w_out.shape[0] // 4
        self.cut = 2 * self.n // 3
        quarter = jnp.concatenate([lax.dynamic_slice_in_dim(w_ff, me * self.n, self.n, 0),
                                   lax.dynamic_slice_in_dim(w_out, me * self.m, self.m, 0)], axis=0)
        self.state = [quarter] + [
            lax.ppermute(quarter, "wshard", [(i, ((i // 2 + k) % 4) * 2 + i % 2) for i in range(8)])
            for k in range(1, 4)]
        self.steps = [seq_bits(me, "xy"), seq_bits(me, "yx")]

    def exchange(self, i):
        if self.plain:
            return
        if i == 0:
            rows = jnp.stack([pick_by((self.depth - d) % 4, *self.state) for d in range(4)])
            self.state = [rows[:, :self.cut], rows[:, self.cut:]]
        self.state = [beside(rows, steps[i][0], "seq", steps[i][1], dim)
                      for rows, steps, dim in zip(self.state, self.steps, (1, 1 + i))]

    def cores(self):
        if not self.plain:
            self.state = [beside(rows, self.core, "wshard", [(i, i ^ 1) for i in range(8)], 1)
                          for rows in self.state]

    def tie(self, others):
        others, self.state = lax.optimization_barrier((others, self.state))
        return others

    def whole(self):
        if self.plain:
            return self.state
        first, last = self.state
        c = first.shape[-1]
        keep = self.n - self.cut
        w_ff = jnp.concatenate([first, last[..., :keep, :]], axis=-2).reshape(32 * self.n, c)
        return w_ff, last[..., keep:, :].reshape(32 * self.m, c)


def quarter_sum(rows):
    parts = lax.all_to_all(rows.reshape(4, -1, rows.shape[1]), "seq", split_axis=0, concat_axis=0, tiled=True)
    return jnp.sum(parts.astype(f32), axis=0).astype(bf16)


def join_quarters(rows, me):
    steps = seq_bits(me, "xy")
    rows = beside(rows, *steps[0][:1], "seq", steps[0][1], 0)
    return beside(rows, steps[1][0], "seq", steps[1][1], 0).reshape((4,) + rows.shape[1:])


def sum_prompt(me, partial):
    owner = jnp.array(OWNER_BLOCK, jnp.int32)

    def take(device):
        start = owner[device] * QB
        return lax.dynamic_slice_in_dim(partial, start, QB, 0)

    total = take(me).astype(f32)
    for flip in (1, 2, 3):
        total = total + send(take(me ^ flip), [(i, i ^ flip) for i in range(4)]).astype(f32)
    parts = [block_of(partial, i) for i in range(8)]
    crossed = send(jnp.where(me == 2, parts[7], parts[4]), [(2, 3), (3, 2)])
    zero = jnp.zeros_like(parts[0])
    joined = (jnp.where(me == 2, parts[6], parts[5]).astype(f32) + crossed.astype(f32)).astype(bf16)
    rows = [
        total.astype(bf16),
        pick_by(me, zero, zero, parts[4], joined),
        pick_by(me, zero, parts[4], parts[5], parts[6]),
        pick_by(me, zero, parts[5], joined, parts[7]),
    ]
    return jnp.concatenate(rows, axis=0)


FORWARD_SPLIT = 4
CHUNKS = (4, 2)


def interleave(key_part, value_part):
    r, w = key_part.shape
    both = jnp.stack([key_part.reshape(r, w // TILE, TILE), value_part.reshape(r, w // TILE, TILE)], axis=2)
    return both.reshape(r, 2 * w)


def local(tokens, teacher, lengths, w_query, w_key, w_value, w_out, w_in, w_ff, gain_attn, gain_ff, bias_table):
    me = lax.axis_index("seq")
    own = by_rows(tokens[0])
    inputs = own.astype(f32)
    targets = teacher[0].astype(f32)
    spans = lengths[0]
    width = own.shape[1]
    pairs = width // TILE

    def gather(w):
        return lax.all_gather(w, "wshard", axis=0, tiled=True)

    w_kv = interleave(w_key, w_value)
    gain_columns = jnp.pad(jnp.stack([gain_attn, gain_ff], axis=1), ((0, 0), (0, TILE - 2)))
    first = gather(jnp.concatenate([w_query, w_kv, gain_columns], axis=1))
    full_query, full_kv = first[:, :width], first[:, width:3 * width]
    gains = first[:, 3 * width:3 * width + 2].astype(f32).T
    gain_one, gain_two = gains[0], gains[1]
    gathered = Gathered(me, w_ff, w_out)
    full_in = gather(w_in)
    got = exchange_rows(me, own)
    got, spans, table = lax.optimization_barrier((got, spans, bias_table))
    got = got + exchange_again(me, own, *got)
    prepared = setup(me, spans, table)
    inverse_one = rms(inputs)
    got, prepared, inverse_one = gathered.tie((got, prepared, inverse_one))
    meta, bias, qaug, kaug, far = prepared
    gathered.exchange(0)
    normed_own = by_rows((inputs * inverse_one * gain_one).astype(bf16))
    normed_seen = by_rows(normed_rows(by_rows(seen_rows(me, own, got)), gain_one))
    queries = jnp.dot(normed_own, full_query, preferred_element_type=f32).astype(bf16)
    keys_values = jnp.dot(normed_seen, full_kv, preferred_element_type=f32).astype(bf16)
    meta, queries, keys_values = gathered.tie((meta, queries, keys_values))
    gathered.exchange(1)
    parts = [attention_forward(meta, queries, keys_values, qaug, kaug, bias, 0, FORWARD_SPLIT)]
    meta, parts = gathered.tie((meta, parts))
    gathered.cores()
    parts.append(attention_forward(meta, queries, keys_values, qaug, kaug, bias, FORWARD_SPLIT,
                                   pairs - FORWARD_SPLIT))
    parts = gathered.tie(parts)
    context, rest = (jnp.concatenate([part[i] for part in parts], axis=1) for i in range(2))
    lse = jnp.concatenate([part[2] for part in parts], axis=0)
    full_ff, full_out = gathered.whole()
    middle = by_rows(inputs + jnp.dot(context, full_out, preferred_element_type=f32))
    inverse_two = rms(middle)
    normed_two = by_rows((middle * inverse_two * gain_two).astype(bf16))
    hidden_act = jnp.maximum(jnp.dot(normed_two, full_in, preferred_element_type=f32), 0.0).astype(bf16)
    final_rows = middle + jnp.dot(hidden_act, full_ff, preferred_element_type=f32)
    local_rows = inputs.shape[0]
    row_index = me * local_rows + lax.iota(jnp.int32, local_rows)
    slot_index = jnp.maximum(row_index - PLEN, 0)
    owner_match = (slot_index // CLEN)[:, None] == lax.iota(jnp.int32, CONT)[None, :]
    row_limit = jnp.sum(jnp.where(owner_match, spans[None, :], 0), axis=1)
    valid_rows = (row_index < PLEN) | (slot_index % CLEN < row_limit)
    row_count = PLEN + jnp.sum(spans).astype(f32)
    factor = (PLEN + CONT * CLEN) / row_count
    d_final = jnp.where(valid_rows[:, None], factor * (final_rows - targets), 0.0)
    d_final = by_rows(d_final)
    d_branch_two = by_rows(d_final.astype(bf16))

    def owners(g):
        return lax.psum_scatter(g, "wshard", scatter_dimension=0, tiled=True)

    size = gain_attn.shape[0]
    share_ff = owners(by_rows(contract_rows(hidden_act, d_branch_two).astype(bf16)))
    d_pre = jnp.where(hidden_act > 0, dot_nt(d_branch_two, full_ff), 0.0).astype(bf16)
    share_in = owners(by_rows(contract_rows(normed_two, d_pre).astype(bf16)))
    d_normed_two = by_rows(dot_nt(d_pre, full_in))
    scaled_two = middle * inverse_two
    d_scaled_two = d_normed_two * gain_two
    d_middle = d_final + inverse_two * (
        d_scaled_two - scaled_two * jnp.mean(d_scaled_two * scaled_two, axis=1, keepdims=True))
    d_middle = by_rows(d_middle)
    d_branch_one = by_rows(d_middle.astype(bf16))
    grad_out = contract_rows(context, d_branch_one).astype(bf16)
    d_context = dot_nt(d_branch_one, full_out).astype(bf16)
    d_context, grad_out = lax.optimization_barrier((d_context, grad_out))

    starts = [sum(CHUNKS[:i]) for i in range(len(CHUNKS))]
    cuts = [(starts[i] * TILE, (starts[i] + CHUNKS[i]) * TILE) for i in range(len(CHUNKS))]

    def backward(meta, i):
        return attention_backward(meta, queries, keys_values, d_context, context, rest, lse, qaug, kaug, bias, far,
                                  starts[i], CHUNKS[i])

    def weight_grad(d_q, d_kv):
        return [by_rows(contract_rows(normed_own, d_q).astype(bf16)),
                by_rows(contract_rows(normed_seen, d_kv).astype(bf16))]

    def query_rows(i, d_q):
        return by_rows(dot_nt(d_q, full_query[:, cuts[i][0]:cuts[i][1]]))

    def key_rows(i, d_kv):
        return by_rows(dot_nt(d_kv, full_kv[:, 2 * cuts[i][0]:2 * cuts[i][1]]))

    first = backward(meta, 0)
    meta, first, share_ff = lax.optimization_barrier((meta, first, share_ff))
    share_first = owners(jnp.concatenate(weight_grad(*first[:2]) + [grad_out], axis=1))
    f_query = query_rows(0, first[0])
    f_part = by_rows(key_rows(0, first[1]).astype(bf16))
    meta, f_query, f_part = lax.optimization_barrier((meta, f_query, f_part))
    f_first = sum_prompt(me, f_part)
    second = backward(meta, 1)
    second, f_first, share_in = lax.optimization_barrier((second, f_first, share_in))
    heads = bias_table.shape[1]
    near = jnp.sum(jnp.concatenate([first[2], second[2]], axis=0), axis=3).reshape(heads, 8 * TILE)
    bias_local = jnp.dot(near, jnp.asarray(bias_spread()), precision=lax.Precision.HIGHEST).reshape(-1, TILE)
    bias_top = bias_local.astype(bf16)
    bias_rest = (bias_local - bias_top.astype(f32)).astype(bf16)
    n_bias = bias_local.shape[0]
    size = gain_attn.shape[0]
    bias_columns = jnp.pad(jnp.concatenate([bias_top, bias_rest], axis=0), ((0, max(0, size - 2 * n_bias)), (0, 0)))
    bias_rows = bias_columns.shape[0]
    blocks = jnp.concatenate(weight_grad(*second[:2]), axis=1)
    n_last = blocks.shape[1]
    blocks = blocks.reshape(-1, size, n_last)
    if bias_rows > size:
        blocks = jnp.pad(blocks, ((0, 0), (0, bias_rows - size), (0, 0)))
    last = jnp.concatenate([blocks, jnp.broadcast_to(bias_columns[None], (blocks.shape[0],) + bias_columns.shape)],
                           axis=2).reshape(-1, n_last + TILE)
    owned_last = Owned(by_rows(last), me, "yx")
    owned_last.advance()
    f_query = f_query + query_rows(1, second[0])
    d_kv = sum_prompt(me, second[1])
    owned_last.advance()
    x_step, y_step = [(bit, "seq", pairs) for bit, pairs in seq_bits(me, "xy")]

    def flat(*shares):
        return jnp.concatenate([share.reshape(-1, width) for share in shares], axis=0)

    quarter_early = quarter_sum(flat(share_ff, share_in))
    f_total = f_first.astype(f32) + key_rows(1, d_kv)
    f_block = f_total[:QB].astype(bf16)
    owned_last.advance()
    owned_last.advance()
    owned_last.advance()
    quarter_first = quarter_sum(flat(share_first))
    owned_last.rows, quarter_early, quarter_first, f_total = lax.optimization_barrier((owned_last.rows, quarter_early, quarter_first, f_total))
    from_two = send(f_block, [(2, 0)])
    from_three = send(f_block, [(3, 0)])
    f_own = f_query + f_total[QB:] + jnp.concatenate(
        [jnp.where(me < 2, f_block, jnp.zeros_like(f_block)), from_two, from_three], axis=0).astype(f32)
    scaled_one = inputs * inverse_one
    d_scaled_one = f_own * gain_one
    d_tokens = d_middle + inverse_one * (
        d_scaled_one - scaled_one * jnp.mean(d_scaled_one * scaled_one, axis=1, keepdims=True))

    half_early = beside(quarter_early, *x_step, 0)
    early = beside(half_early, *y_step, 0).reshape(-1, width).astype(f32)
    n_ff = share_ff.shape[0]
    share_ff, share_in = early[:n_ff], early[n_ff:].reshape(size, -1)
    late = join_quarters(owned_last.finish(), me).reshape(bias_rows if bias_rows > size else size, -1).astype(f32)
    share_first = join_quarters(quarter_first, me).reshape(size, -1).astype(f32)
    share_out = share_first[:, -width:]
    shares = [share_first[:, :-width], late[:size, :n_last]]
    bias_grad = (late[:n_bias, n_last:] + late[n_bias:2 * n_bias, n_last:]).reshape(heads, NB).T
    share_query = jnp.concatenate(
        [share[:, :count * TILE] for share, count in zip(shares, CHUNKS)], axis=1)
    share_kv = jnp.concatenate(
        [share[:, count * TILE:] for share, count in zip(shares, CHUNKS)], axis=1)
    share_kv = share_kv.reshape(share_kv.shape[0], pairs, 2, TILE)
    share_key = share_kv[:, :, 0].reshape(-1, width)
    share_value = share_kv[:, :, 1].reshape(-1, width)
    gain_grad_one = (jnp.sum(share_query * w_query.astype(f32), axis=1)
                     + jnp.sum(share_key * w_key.astype(f32), axis=1)
                     + jnp.sum(share_value * w_value.astype(f32), axis=1)) / gain_attn.astype(f32)
    gain_grad_two = jnp.sum(share_in * w_in.astype(f32), axis=1) / gain_ff.astype(f32)
    return (
        final_rows.astype(bf16)[None],
        d_tokens[None],
        share_query,
        share_key,
        share_value,
        share_out,
        share_in,
        share_ff,
        gain_grad_one,
        gain_grad_two,
        bias_grad,
    )


def solution(mesh):
    rows = P("wshard", "seq", None)
    weight = P("wshard", None)
    placed = (rows, rows) + (weight,) * 7 + (P("wshard"), P("wshard"), P())
    return jax.shard_map(
        local,
        mesh=mesh,
        in_specs=placed,
        out_specs=(rows, rows) + (weight,) * 6 + (P("wshard"), P("wshard"), P()),
        check_vma=False,
    )
```

```python
import jax
import jax.numpy as jnp
import numpy as np
from jax import lax
from jax.experimental import pallas as pl
from jax.experimental.pallas import tpu as pltpu
from jax.experimental.layout import Layout, with_layout_constraint
from jax.sharding import PartitionSpec as P

DH = 64
NB = 32
PLEN = 1024
CLEN = 512
CONT = 4
QB = 256
NQ = 3
ROWS = QB * NQ
KROWS = PLEN + 2 * CLEN
TILE = 128
NEGATIVE = -1e30
f32 = jnp.float32
bf16 = jnp.bfloat16


def dot_nt(a, b):
    return lax.dot_general(a, b, (((1,), (1,)), ((), ())), preferred_element_type=f32)


def dot_nn(a, b):
    return lax.dot_general(a, b, (((1,), (0,)), ((), ())), preferred_element_type=f32)


def low_lanes(shape):
    return lax.broadcasted_iota(jnp.int32, shape, 1) < DH


def add_bias(s, bias_ref, head, kc, qc):
    rows = []
    for a in range(s.shape[0] // TILE):
        cols = []
        for b in range(s.shape[1] // TILE):
            d = jnp.clip(kc + a - qc[b], -2, 2) + 2
            cols.append(bias_ref[head, pl.ds(pl.multiple_of(d * TILE, TILE), TILE), :])
        rows.append(jnp.concatenate(cols, axis=1))
    return s + jnp.concatenate(rows, axis=0)


def fold_rows(rows):
    return jnp.sum(rows.reshape(rows.shape[0] // 8, 8, rows.shape[1]), axis=0)


def fold_max(rows):
    return jnp.max(rows.reshape(rows.shape[0] // 8, 8, rows.shape[1]), axis=0)


def forward_kernel(meta, q_ref, k_ref, v_ref, qaug_ref, kaug_ref, bias_ref, ctx_ref, rest_ref, lse_ref,
                   q_scr, vt_scr, s_scr, ctx_scr):
    low_q = low_lanes((ROWS, TILE))
    zero = jnp.zeros((ROWS, TILE), bf16)
    q_scr[0, :, :TILE] = jnp.where(low_q, q_ref[...], zero)
    q_scr[1, :, :TILE] = jnp.where(low_q, zero, q_ref[...])
    q_scr[0, :, TILE:] = qaug_ref[...]
    q_scr[1, :, TILE:] = qaug_ref[...]
    vt_scr[...] = v_ref[...].T
    keys = PLEN + CLEN
    chunks = keys // QB

    def place(unit):
        h, qb = unit // NQ, unit % NQ
        slot = pl.multiple_of(PLEN + meta[NQ + qb] * CLEN, CLEN)
        return h, slice(qb * QB, (qb + 1) * QB), meta[qb], slot

    def key_start(slot, c):
        return c * QB if c < PLEN // QB else pl.multiple_of(slot + (c * QB - PLEN), QB)

    def score_chunk(unit, c):
        h, columns, qc, slot = place(unit)
        rows = pl.ds(key_start(slot, c), QB)
        s = dot_nt(jnp.concatenate([k_ref[rows, :], kaug_ref[rows, :]], axis=1), q_scr[h, columns, :])
        s = add_bias(s, bias_ref, h, 2 * c, (qc, qc + 1))
        s_scr[unit % 2, c * QB:(c + 1) * QB, :] = s
        return fold_max(s)

    def weight_chunk(unit, c, m):
        h, columns, qc, slot = place(unit)
        p = jnp.exp(s_scr[unit % 2, c * QB:(c + 1) * QB, :] - m)
        v = vt_scr[h * DH:(h + 1) * DH, pl.ds(key_start(slot, c), QB)]
        return fold_rows(p), dot_nn(v, p.astype(bf16))

    units = 2 * NQ
    m = None
    for unit in range(-1, units):
        if unit >= 0:
            m = jnp.max(top, axis=0, keepdims=True)
        top = total = acc = None
        for c in range(chunks):
            if unit + 1 < units:
                t = score_chunk(unit + 1, c)
                top = t if top is None else jnp.maximum(top, t)
            if unit >= 0:
                l, o = weight_chunk(unit, c, m)
                total = l if total is None else total + l
                acc = o if acc is None else acc + o
        if unit >= 0:
            h, columns, qc, slot = place(unit)
            l = jnp.sum(total, axis=0, keepdims=True)
            ctx_scr[h * DH:(h + 1) * DH, columns] = acc / l
            lse_ref[0, h:h + 1, columns] = m + jnp.log(l)
    ctx = ctx_scr[...].T
    ctx_low = ctx.astype(bf16)
    ctx_ref[...] = ctx_low
    rest_ref[...] = (ctx - ctx_low.astype(f32)).astype(bf16)


def attention_forward(meta, q, kv, qaug, kaug, bias, first, pairs):
    own = pl.BlockSpec((ROWS, TILE), lambda i, meta: (0, first + i))
    out = pl.BlockSpec((ROWS, TILE), lambda i, meta: (0, i))
    keys = pl.BlockSpec((KROWS, TILE), lambda i, meta: (0, 2 * (first + i)))
    values = pl.BlockSpec((KROWS, TILE), lambda i, meta: (0, 2 * (first + i) + 1))
    fixed = lambda rows: pl.BlockSpec((rows, TILE), lambda i, meta: (0, 0))
    return pl.pallas_call(
        forward_kernel,
        grid_spec=pltpu.PrefetchScalarGridSpec(
            num_scalar_prefetch=1,
            grid=(pairs,),
            in_specs=[own, keys, values, fixed(ROWS), fixed(KROWS),
                      pl.BlockSpec((2, 5 * TILE, TILE), lambda i, meta: (first + i, 0, 0))],
            out_specs=[out, out, pl.BlockSpec((1, 2, ROWS), lambda i, meta: (i, 0, 0))],
            scratch_shapes=[
                pltpu.VMEM((2, ROWS, 2 * TILE), bf16),
                pltpu.VMEM((TILE, KROWS), bf16),
                pltpu.VMEM((2, PLEN + CLEN, QB), f32),
                pltpu.VMEM((TILE, ROWS), f32),
            ],
        ),
        out_shape=[jax.ShapeDtypeStruct((ROWS, pairs * TILE), bf16),
                   jax.ShapeDtypeStruct((ROWS, pairs * TILE), bf16),
                   jax.ShapeDtypeStruct((pairs, 2, ROWS), f32)],
        compiler_params=pltpu.CompilerParams(dimension_semantics=("arbitrary",),
                                             vmem_limit_bytes=56 << 20),
        cost_estimate=pl.CostEstimate(flops=pairs * 5_000_000_000, bytes_accessed=pairs * 2_000_000,
                                      transcendentals=pairs * 2 * ROWS * (PLEN + CLEN)),
        name="attention_forward",
    )(meta, q, kv, kv, qaug, kaug, bias)


PAD = TILE


def backward_kernel(meta, q_ref, k_ref, v_ref, do_ref, ctx_ref, rest_ref, lse_ref, qaug_ref, kaug_ref,
                    bias_ref, pick_ref, dq_ref, dkv_ref, near_ref,
                    kt_scr, q_scr, wide_scr, do_scr, delta_scr, ds_scr, p_scr, dks_scr, dvs_scr, far_scr):
    low_q = low_lanes((ROWS, TILE))
    kt_scr[...] = k_ref[...].T
    zero = jnp.zeros((ROWS, TILE), bf16)
    for h in range(2):
        q = q_ref[...]
        aug = qaug_ref[...]
        q_scr[h] = jnp.where(low_q, q, aug) if h == 0 else jnp.where(low_q, aug, q)
        wide_scr[h, :, :TILE] = jnp.where(low_q, q, zero) if h == 0 else jnp.where(low_q, zero, q)
        wide_scr[h, :, TILE:] = aug
        do = jnp.where(low_q, do_ref[...], zero) if h == 0 else jnp.where(low_q, zero, do_ref[...])
        for qb in range(NQ):
            do_scr[qb, h] = do[qb * QB:(qb + 1) * QB]
    prod = do_ref[...].astype(f32) * (ctx_ref[...].astype(f32) + rest_ref[...].astype(f32))
    hi = prod.astype(bf16)
    lo = (prod - hi.astype(f32)).astype(bf16)
    pick_row = lax.broadcasted_iota(jnp.int32, (8, TILE), 0)
    pick_low = low_lanes((8, TILE))
    pick = jnp.where((pick_row == 0) & pick_low | (pick_row == 1) & ~pick_low, 1.0, 0.0).astype(bf16)
    delta_scr[...] = dot_nt(pick, hi) + dot_nt(pick, lo)
    for h in range(2):
        ds_scr[h, 0:PAD, :] = jnp.zeros((PAD, ROWS), bf16)
        ds_scr[h, PAD + PLEN + CLEN:, :] = jnp.zeros((PAD, ROWS), bf16)

    def piece(h, kk, vv, kc, qb):
        cols = slice(qb * QB, (qb + 1) * QB)
        s = dot_nt(kk, wide_scr[h, cols, :])
        qc = meta[qb]
        s = add_bias(s, bias_ref, h, kc, (qc, qc + 1))
        p = jnp.exp(s - lse_ref[0, h:h + 1, cols])
        dp = dot_nt(vv, do_scr[qb, h])
        ds = (p * (dp - delta_scr[h:h + 1, cols])).astype(bf16)
        return p.astype(bf16), ds

    low_c = low_lanes((QB, TILE))

    def prompt_chunk(c, carry):
        start = c * QB
        rows = pl.ds(start, QB)
        kk = jnp.concatenate([k_ref[rows, :], kaug_ref[rows, :]], axis=1)
        vv = v_ref[rows, :]
        buffer = c % 2
        for h in range(2):
            for qb in range(NQ):
                cols = slice(qb * QB, (qb + 1) * QB)
                p, ds = piece(h, kk, vv, 2 * c, qb)
                ds_scr[h, pl.ds(PAD + start, QB), cols] = ds
                p_scr[buffer, :, (2 * qb + h) * QB:(2 * qb + h + 1) * QB] = p
        dv = dot_nn(p_scr[buffer], do_scr[...].reshape(2 * ROWS, TILE))
        dks = [dot_nn(ds_scr[h, pl.ds(PAD + start, QB), :], q_scr[h]) for h in range(2)]
        dkv_ref[rows, TILE:] = dv.astype(bf16)
        dkv_ref[rows, :TILE] = jnp.where(low_c, dks[0], dks[1]).astype(bf16)
        sums = jnp.where(low_c, dks[1], dks[0])
        far_scr[2 * c] = fold_rows(sums[:TILE])
        far_scr[2 * c + 1] = fold_rows(sums[TILE:])
        return carry

    for c in range(PLEN // QB):
        prompt_chunk(c, 0)
    for qb in range(NQ):
        cols = slice(qb * QB, (qb + 1) * QB)
        slot = pl.multiple_of(PLEN + meta[NQ + qb] * CLEN, CLEN)
        for half in range(CLEN // QB):
            rows = pl.ds(pl.multiple_of(slot + half * QB, QB), QB)
            there = slice(half * QB, (half + 1) * QB)
            kk = jnp.concatenate([k_ref[rows, :], kaug_ref[rows, :]], axis=1)
            vv = v_ref[rows, :]
            ps = []
            for h in range(2):
                p, ds = piece(h, kk, vv, 8 + 2 * half, qb)
                ds_scr[h, PAD + PLEN + half * QB:PAD + PLEN + (half + 1) * QB, cols] = ds
                ps.append(p)
                dks_scr[qb, h, there, :] = dot_nn(ds, q_scr[h, cols, :])
            dvs_scr[qb, there, :] = dot_nn(jnp.concatenate(ps, axis=1), do_scr[qb].reshape(2 * QB, TILE))
    for slot in range(2):
        for half in range(CLEN // TILE):
            there = slice(half * TILE, (half + 1) * TILE)
            rows = slice(PLEN + slot * CLEN + half * TILE, PLEN + slot * CLEN + (half + 1) * TILE)
            totals = [None] * 3
            for qb in range(NQ):
                mine = meta[NQ + qb] == slot
                parts = (dvs_scr[qb, there, :], dks_scr[qb, 0, there, :], dks_scr[qb, 1, there, :])
                for i, part in enumerate(parts):
                    part = jnp.where(mine, part, 0.0)
                    totals[i] = part if totals[i] is None else totals[i] + part
            dkv_ref[rows, TILE:] = totals[0].astype(bf16)
            low_t = low_lanes((TILE, TILE))
            dkv_ref[rows, :TILE] = jnp.where(low_t, totals[1], totals[2]).astype(bf16)
            far_scr[8 + slot * (CLEN // TILE) + half] = fold_rows(jnp.where(low_t, totals[2], totals[1]))

    dqt = []
    for h in range(2):
        parts = []
        for qb in range(NQ):
            cols = slice(qb * QB, (qb + 1) * QB)
            slot = pl.multiple_of(PLEN + meta[NQ + qb] * CLEN, CLEN)
            rows = slice(h * DH, (h + 1) * DH)
            keys = jnp.concatenate([kt_scr[rows, 0:PLEN], kt_scr[rows, pl.ds(slot, CLEN)]], axis=1)
            parts.append(dot_nn(keys, ds_scr[h, PAD:PAD + PLEN + CLEN, cols]))
        dqt.append(jnp.concatenate(parts, axis=1))
    dq_ref[...] = jnp.concatenate(dqt, axis=0).T.astype(bf16)

    row_id = lax.broadcasted_iota(jnp.int32, (TILE, TILE), 0)
    lane_id = lax.broadcasted_iota(jnp.int32, (TILE, TILE), 1)
    flip = jnp.where(row_id + lane_id == TILE - 1, 1.0, 0.0).astype(bf16)
    flips = jnp.concatenate([flip, flip], axis=0)
    for h in range(2):
        acc = None
        for qb in range(NQ):
            tiles = [ds_scr[h, pl.ds(pl.multiple_of((meta[qb] + half) * TILE, TILE), 3 * TILE),
                            (2 * qb + half) * TILE:(2 * qb + half + 1) * TILE] for half in range(2)]
            part = dot_nn(jnp.concatenate(tiles, axis=1), flips)
            acc = part if acc is None else acc + part
        sums = []
        for d in range(3):
            rolled = pltpu.roll(acc[d * TILE:(d + 1) * TILE], 0, 1, stride=1, stride_axis=0)
            wrapped = jnp.where(lane_id < row_id, rolled, 0.0)
            sums += [fold_rows(rolled), fold_rows(wrapped)]
        for side in range(2):
            total = None
            for t in range(16):
                term = far_scr[t] * pick_ref[h, side, t]
                total = term if total is None else total + term
            sums.append(total)
        for i, eight in enumerate(sums):
            near_ref[0, h, i] = eight


def attention_backward(meta, q, kv, do, ctx, rest, lse, qaug, kaug, bias, pick, first, pairs):
    own = pl.BlockSpec((ROWS, TILE), lambda i, meta: (0, first + i))
    keys = pl.BlockSpec((KROWS, TILE), lambda i, meta: (0, 2 * (first + i)))
    values = pl.BlockSpec((KROWS, TILE), lambda i, meta: (0, 2 * (first + i) + 1))
    fixed = lambda rows: pl.BlockSpec((rows, TILE), lambda i, meta: (0, 0))
    return pl.pallas_call(
        backward_kernel,
        grid_spec=pltpu.PrefetchScalarGridSpec(
            num_scalar_prefetch=1,
            grid=(pairs,),
            in_specs=[own, keys, values, own, own, own,
                      pl.BlockSpec((1, 2, ROWS), lambda i, meta: (first + i, 0, 0)),
                      fixed(ROWS), fixed(KROWS),
                      pl.BlockSpec((2, 5 * TILE, TILE), lambda i, meta: (first + i, 0, 0)),
                      pl.BlockSpec((2, 2, 16, 8, TILE), lambda i, meta: (0, 0, 0, 0, 0))],
            out_specs=[pl.BlockSpec((ROWS, TILE), lambda i, meta: (0, i)),
                       pl.BlockSpec((KROWS, 2 * TILE), lambda i, meta: (0, i)),
                       pl.BlockSpec((1, 2, 8, 8, TILE), lambda i, meta: (i, 0, 0, 0, 0))],
            scratch_shapes=[
                pltpu.VMEM((TILE, KROWS), bf16),
                pltpu.VMEM((2, ROWS, TILE), bf16),
                pltpu.VMEM((2, ROWS, 2 * TILE), bf16),
                pltpu.VMEM((NQ, 2, QB, TILE), bf16),
                pltpu.VMEM((8, ROWS), f32),
                pltpu.VMEM((2, PLEN + CLEN + 2 * PAD, ROWS), bf16),
                pltpu.VMEM((2, QB, 2 * ROWS), bf16),
                pltpu.VMEM((NQ, 2, CLEN, TILE), f32),
                pltpu.VMEM((NQ, CLEN, TILE), f32),
                pltpu.VMEM((16, 8, TILE), f32),
            ],
        ),
        out_shape=[jax.ShapeDtypeStruct((ROWS, pairs * TILE), bf16),
                   jax.ShapeDtypeStruct((KROWS, 2 * pairs * TILE), bf16),
                   jax.ShapeDtypeStruct((pairs, 2, 8, 8, TILE), f32)],
        compiler_params=pltpu.CompilerParams(dimension_semantics=("arbitrary",),
                                             vmem_limit_bytes=56 << 20),
        cost_estimate=pl.CostEstimate(flops=pairs * 10_000_000_000, bytes_accessed=pairs * 3_000_000,
                                      transcendentals=pairs * 2 * ROWS * (PLEN + CLEN)),
        name="attention_backward",
    )(meta, q, kv, kv, do, ctx, rest, lse, qaug, kaug, bias, pick)


EPSILON = 1e-06
THRESHOLDS = (12, 16, 23, 32, 46, 64, 91)
OWNER_BLOCK = (0, 3, 1, 2)


def python_bucket(offset):
    magnitude = abs(offset)
    base = NB // 2 if offset > 0 else 0
    if magnitude < 8:
        return base + magnitude
    return base + 8 + sum(1 for edge in THRESHOLDS if magnitude >= edge)


def bias_spread():
    spread = np.zeros((8, TILE, NB), np.float32)
    for lane in range(TILE):
        for d in range(3):
            inside = python_bucket(TILE * (d - 1) + lane - (TILE - 1))
            passed = python_bucket(TILE * d + lane - (TILE - 1))
            spread[2 * d, lane, inside] += 1
            spread[2 * d + 1, lane, passed] += 1
            spread[2 * d + 1, lane, inside] -= 1
    spread[6, :, python_bucket(-200)] = 1
    spread[7, :, python_bucket(200)] = 1
    return spread.reshape(8 * TILE, NB)


def setup_kernel(meta, limit, table, bias_ref, qaug_ref, kaug_ref, far_ref):
    head = pl.program_id(0)
    heads = pl.num_programs(0)
    near = (lax.broadcasted_iota(jnp.int32, (TILE, TILE), 0)
            - lax.broadcasted_iota(jnp.int32, (TILE, TILE), 1))
    for d in range(-2, 3):
        first, last = TILE * d - TILE + 1, TILE * d + TILE - 1
        previous = python_bucket(first)
        tile = jnp.full((TILE, TILE), table[previous * heads + head], f32)
        for n in range(first + 1, last + 1):
            current = python_bucket(n)
            if current != previous:
                tile = jnp.where(near >= n - TILE * d, table[current * heads + head], tile)
                previous = current
        bias_ref[0, (d + 2) * TILE:(d + 3) * TILE, :] = tile

    @pl.when(head == 0)
    def _():
        shape = (ROWS, TILE)
        sub = lax.broadcasted_iota(jnp.int32, shape, 1) & (DH - 1)
        qaug_ref[...] = jnp.where(sub == lax.broadcasted_iota(jnp.int32, shape, 0) // TILE, 1.0, 0.0).astype(bf16)
        shape = (KROWS, TILE)
        key = lax.broadcasted_iota(jnp.int32, shape, 0)
        sub = lax.broadcasted_iota(jnp.int32, shape, 1) & (DH - 1)
        kaug = jnp.zeros(shape, f32)
        for q in range(NQ):
            first = PLEN + CLEN * meta[NQ + q]
            hidden = (key >= PLEN) & ((key < first) | (key >= first + limit[q]))
            kaug = jnp.where(((sub == 2 * q) | (sub == 2 * q + 1)) & hidden, NEGATIVE, kaug)
        kaug_ref[...] = kaug.astype(bf16)
        lane = lax.broadcasted_iota(jnp.int32, (8, TILE), 1)
        for h in range(2):
            for row in range(16):
                key_tile = row if row < 8 else 8 + (row - 8) % 4
                for side in range(2):
                    out = jnp.zeros((8, TILE), f32)
                    for q in range(2 * NQ):
                        apart = key_tile - (meta[q // 2] + q % 2)
                        is_far = (apart <= -2) if side == 0 else (apart >= 2)
                        out = jnp.where(lane == q + (DH if h == 0 else 0), jnp.where(is_far, 1.0, 0.0), out)
                    far_ref[h, side, row] = out


def setup(me, spans, table):
    block = NQ * me + jnp.arange(NQ, dtype=jnp.int32)
    prompt = block < PLEN // QB
    cont = jnp.maximum(block - PLEN // QB, 0) // 2
    half = jnp.maximum(block - PLEN // QB, 0) % 2
    tile = jnp.where(prompt, 2 * block, PLEN // TILE + 2 * half)
    slot = jnp.where(prompt, 0, cont - (me - 1))
    chosen = cont[:, None] == jnp.arange(CONT, dtype=jnp.int32)[None, :]
    limit = jnp.where(prompt, 0, jnp.sum(jnp.where(chosen, spans[None, :], 0), axis=1)).astype(jnp.int32)
    meta = jnp.concatenate([tile, slot]).astype(jnp.int32)
    heads = table.shape[1]
    whole = lambda *shape: pl.BlockSpec(shape, lambda i, *_: (0,) * len(shape))
    bias, qaug, kaug, far = pl.pallas_call(
        setup_kernel,
        grid_spec=pltpu.PrefetchScalarGridSpec(
            num_scalar_prefetch=3,
            grid=(heads,),
            in_specs=[],
            out_specs=[pl.BlockSpec((1, 5 * TILE, TILE), lambda i, *_: (i, 0, 0)),
                       whole(ROWS, TILE), whole(KROWS, TILE), whole(2, 2, 16, 8, TILE)],
        ),
        out_shape=[jax.ShapeDtypeStruct((heads, 5 * TILE, TILE), f32),
                   jax.ShapeDtypeStruct((ROWS, TILE), bf16),
                   jax.ShapeDtypeStruct((KROWS, TILE), bf16),
                   jax.ShapeDtypeStruct((2, 2, 16, 8, TILE), f32)],
        compiler_params=pltpu.CompilerParams(dimension_semantics=("arbitrary",)),
        cost_estimate=pl.CostEstimate(flops=30_000_000, bytes_accessed=5_000_000, transcendentals=0),
        name="setup",
    )(meta, limit, table.astype(f32).reshape(-1))
    return meta, bias, qaug, kaug, far


def by_rows(x):
    return with_layout_constraint(x, Layout(tuple(range(x.ndim))))


def rms(rows):
    return lax.rsqrt(jnp.mean(rows * rows, axis=1, keepdims=True) + EPSILON)


def normed_rows(rows, gain):
    rows = rows.astype(f32)
    return (rows * rms(rows) * gain).astype(bf16)


def contract_rows(left, right):
    return lax.dot_general(left, right, (((0,), (0,)), ((), ())), preferred_element_type=f32)


def block_of(rows, i):
    return rows[i * QB:(i + 1) * QB]


def send(rows, pairs):
    return lax.ppermute(rows, "seq", pairs)


def pick_by(me, *choices):
    out = choices[-1]
    for i in range(len(choices) - 2, -1, -1):
        out = jnp.where(me == i, choices[i], out)
    return out


def exchange_rows(me, own):
    low, high = own[:ROWS // 2], own[ROWS // 2:]
    return (send(jnp.where(me == 2, high, low), [(0, 1), (1, 0), (2, 3), (3, 2)]),
            send(jnp.where(me == 0, high, low), [(0, 2), (1, 3)]))


def exchange_again(me, own, across, down):
    low, high = own[:ROWS // 2], own[ROWS // 2:]
    return (send(jnp.where(me == 0, high, down), [(0, 1), (2, 3), (3, 2)]),
            send(jnp.where(me == 0, low, across), [(0, 2), (1, 3)]))


def seen_rows(me, own, got):
    across, down, across_again, down_again = got
    mine = [block_of(own, i) for i in range(NQ)]
    low, high = own[:ROWS // 2], own[ROWS // 2:]
    prompt = [
        pick_by(me, low, across, down_again, down_again),
        pick_by(me, high, across_again, down, across_again),
        pick_by(me, across[:QB], mine[0], across_again[:QB], down[:QB]),
    ]
    slots = [
        pick_by(me, mine[0], mine[1], mine[0], across[ROWS // 2 - QB:]),
        pick_by(me, mine[1], mine[2], mine[1], mine[0]),
        pick_by(me, mine[1], mine[1], mine[2], mine[1]),
        pick_by(me, mine[2], mine[2], across[:QB], mine[2]),
    ]
    return jnp.concatenate(prompt + slots, axis=0)


def halve(rows, bit, axis, pairs):
    n, r, c = rows.shape
    parts = rows.reshape(n, 2, r // 2, c)
    away = lax.dynamic_index_in_dim(parts, 1 - bit, 1, keepdims=False)
    kept = lax.dynamic_index_in_dim(parts, bit, 1, keepdims=False)
    got = lax.ppermute(away, axis, pairs)
    return (kept.astype(f32) + got.astype(f32)).astype(bf16)


def join(rows, bit, axis, pairs):
    got = lax.ppermute(rows, axis, pairs)
    return jnp.concatenate([jnp.where(bit == 0, rows, got), jnp.where(bit == 0, got, rows)], axis=-2)


def seq_bits(me, order):
    steps = {"x": (me % 2, [(i, i ^ 1) for i in range(4)]), "y": (me // 2, [(i, i ^ 2) for i in range(4)])}
    return [steps[name] for name in order]


class Owned:
    def __init__(self, grad, me, order):
        self.step, self.steps = 0, seq_bits(me, order)
        self.rows = grad
        if lax.axis_size("wshard") != 8:
            self.rows = quarter_sum(lax.psum_scatter(grad, "wshard", scatter_dimension=0, tiled=True))
            self.step = 5

    def advance(self):
        place = lax.axis_index("wshard")
        flip = lambda bit: [(i, i ^ bit) for i in range(8)]
        step, rows = self.step, self.rows
        if step == 0:
            rows = halve(rows.reshape(4, -1, rows.shape[1]), place % 2, "wshard", flip(1))
        elif step in (1, 2):
            rows = halve(rows, self.steps[step - 1][0], "seq", self.steps[step - 1][1])
        elif step == 3:
            rows = halve(rows.reshape(1, -1, rows.shape[2]), place // 4, "wshard", flip(4))
        elif step == 4:
            rows = halve(rows, place // 2 % 2, "wshard", flip(2))[0]
        self.step, self.rows = step + 1, rows

    def finish(self):
        while self.step < 5:
            self.advance()
        return self.rows


def beside(rows, bit, axis, pairs, dim):
    got = lax.ppermute(rows, axis, pairs)
    return jnp.stack([jnp.where(bit == 0, rows, got), jnp.where(bit == 0, got, rows)], axis=dim)


class Gathered:
    def __init__(self, me, w_ff, w_out):
        self.plain = lax.axis_size("wshard") != 8
        if self.plain:
            self.state = [lax.all_gather(w, "wshard", axis=0, tiled=True) for w in (w_ff, w_out)]
            return
        place = lax.axis_index("wshard")
        self.core, self.depth = place % 2, place // 2
        self.n, self.m = w_ff.shape[0] // 4, w_out.shape[0] // 4
        self.cut = 2 * self.n // 3
        quarter = jnp.concatenate([lax.dynamic_slice_in_dim(w_ff, me * self.n, self.n, 0),
                                   lax.dynamic_slice_in_dim(w_out, me * self.m, self.m, 0)], axis=0)
        self.state = [quarter] + [
            lax.ppermute(quarter, "wshard", [(i, ((i // 2 + k) % 4) * 2 + i % 2) for i in range(8)])
            for k in range(1, 4)]
        self.steps = [seq_bits(me, "xy"), seq_bits(me, "yx")]

    def exchange(self, i):
        if self.plain:
            return
        if i == 0:
            rows = jnp.stack([pick_by((self.depth - d) % 4, *self.state) for d in range(4)])
            self.state = [rows[:, :self.cut], rows[:, self.cut:]]
        self.state = [beside(rows, steps[i][0], "seq", steps[i][1], dim)
                      for rows, steps, dim in zip(self.state, self.steps, (1, 1 + i))]

    def cores(self):
        if not self.plain:
            self.state = [beside(rows, self.core, "wshard", [(i, i ^ 1) for i in range(8)], 1)
                          for rows in self.state]

    def tie(self, others):
        others, self.state = lax.optimization_barrier((others, self.state))
        return others

    def whole(self):
        if self.plain:
            return self.state
        first, last = self.state
        c = first.shape[-1]
        keep = self.n - self.cut
        w_ff = jnp.concatenate([first, last[..., :keep, :]], axis=-2).reshape(32 * self.n, c)
        return w_ff, last[..., keep:, :].reshape(32 * self.m, c)


def quarter_sum(rows):
    parts = lax.all_to_all(rows.reshape(4, -1, rows.shape[1]), "seq", split_axis=0, concat_axis=0, tiled=True)
    return jnp.sum(parts.astype(f32), axis=0).astype(bf16)


def join_quarters(rows, me):
    steps = seq_bits(me, "xy")
    rows = beside(rows, *steps[0][:1], "seq", steps[0][1], 0)
    return beside(rows, steps[1][0], "seq", steps[1][1], 0).reshape((4,) + rows.shape[1:])


def sum_prompt(me, partial):
    owner = jnp.array(OWNER_BLOCK, jnp.int32)

    def take(device):
        start = owner[device] * QB
        return lax.dynamic_slice_in_dim(partial, start, QB, 0)

    total = take(me).astype(f32)
    for flip in (1, 2, 3):
        total = total + send(take(me ^ flip), [(i, i ^ flip) for i in range(4)]).astype(f32)
    parts = [block_of(partial, i) for i in range(8)]
    crossed = send(jnp.where(me == 2, parts[7], parts[4]), [(2, 3), (3, 2)])
    zero = jnp.zeros_like(parts[0])
    joined = (jnp.where(me == 2, parts[6], parts[5]).astype(f32) + crossed.astype(f32)).astype(bf16)
    rows = [
        total.astype(bf16),
        pick_by(me, zero, zero, parts[4], joined),
        pick_by(me, zero, parts[4], parts[5], parts[6]),
        pick_by(me, zero, parts[5], joined, parts[7]),
    ]
    return jnp.concatenate(rows, axis=0)


CHUNKS = (4, 2)


def interleave(key_part, value_part):
    r, w = key_part.shape
    both = jnp.stack([key_part.reshape(r, w // TILE, TILE), value_part.reshape(r, w // TILE, TILE)], axis=2)
    return both.reshape(r, 2 * w)


def local(tokens, teacher, lengths, w_query, w_key, w_value, w_out, w_in, w_ff, gain_attn, gain_ff, bias_table):
    me = lax.axis_index("seq")
    own = by_rows(tokens[0])
    inputs = own.astype(f32)
    targets = teacher[0].astype(f32)
    spans = lengths[0]
    width = own.shape[1]
    pairs = width // TILE

    def gather(w):
        return lax.all_gather(w, "wshard", axis=0, tiled=True)

    w_kv = interleave(w_key, w_value)
    gain_columns = jnp.pad(jnp.stack([gain_attn, gain_ff], axis=1), ((0, 0), (0, TILE - 2)))
    first = gather(jnp.concatenate([w_query, w_kv, gain_columns], axis=1))
    full_query, full_kv = first[:, :width], first[:, width:3 * width]
    gains = first[:, 3 * width:3 * width + 2].astype(f32).T
    gain_one, gain_two = gains[0], gains[1]
    gathered = Gathered(me, w_ff, w_out)
    full_in = gather(w_in)
    got = exchange_rows(me, own)
    got, spans, table = lax.optimization_barrier((got, spans, bias_table))
    got = got + exchange_again(me, own, *got)
    prepared = setup(me, spans, table)
    inverse_one = rms(inputs)
    got, prepared, inverse_one = gathered.tie((got, prepared, inverse_one))
    meta, bias, qaug, kaug, far = prepared
    gathered.exchange(0)
    normed_own = by_rows((inputs * inverse_one * gain_one).astype(bf16))
    normed_seen = by_rows(normed_rows(by_rows(seen_rows(me, own, got)), gain_one))
    normed_own, normed_seen = gathered.tie((normed_own, normed_seen))
    gathered.exchange(1)
    queries = jnp.dot(normed_own, full_query, preferred_element_type=f32).astype(bf16)
    keys_values = jnp.dot(normed_seen, full_kv, preferred_element_type=f32).astype(bf16)
    meta, queries, keys_values = gathered.tie((meta, queries, keys_values))
    gathered.cores()
    context, rest, lse = gathered.tie(attention_forward(meta, queries, keys_values, qaug, kaug, bias, 0, pairs))
    full_ff, full_out = gathered.whole()
    middle = by_rows(inputs + jnp.dot(context, full_out, preferred_element_type=f32))
    inverse_two = rms(middle)
    normed_two = by_rows((middle * inverse_two * gain_two).astype(bf16))
    hidden_act = jnp.maximum(jnp.dot(normed_two, full_in, preferred_element_type=f32), 0.0).astype(bf16)
    final_rows = middle + jnp.dot(hidden_act, full_ff, preferred_element_type=f32)
    local_rows = inputs.shape[0]
    row_index = me * local_rows + lax.iota(jnp.int32, local_rows)
    slot_index = jnp.maximum(row_index - PLEN, 0)
    owner_match = (slot_index // CLEN)[:, None] == lax.iota(jnp.int32, CONT)[None, :]
    row_limit = jnp.sum(jnp.where(owner_match, spans[None, :], 0), axis=1)
    valid_rows = (row_index < PLEN) | (slot_index % CLEN < row_limit)
    row_count = PLEN + jnp.sum(spans).astype(f32)
    factor = (PLEN + CONT * CLEN) / row_count
    d_final = jnp.where(valid_rows[:, None], factor * (final_rows - targets), 0.0)
    d_final = by_rows(d_final)
    d_branch_two = by_rows(d_final.astype(bf16))

    def owners(g):
        return lax.psum_scatter(g, "wshard", scatter_dimension=0, tiled=True)

    size = gain_attn.shape[0]
    share_ff = owners(by_rows(contract_rows(hidden_act, d_branch_two).astype(bf16)))
    d_pre = jnp.where(hidden_act > 0, dot_nt(d_branch_two, full_ff), 0.0).astype(bf16)
    share_in = owners(by_rows(contract_rows(normed_two, d_pre).astype(bf16)))
    d_normed_two = by_rows(dot_nt(d_pre, full_in))
    scaled_two = middle * inverse_two
    d_scaled_two = d_normed_two * gain_two
    d_middle = d_final + inverse_two * (
        d_scaled_two - scaled_two * jnp.mean(d_scaled_two * scaled_two, axis=1, keepdims=True))
    d_middle = by_rows(d_middle)
    d_branch_one = by_rows(d_middle.astype(bf16))
    grad_out = contract_rows(context, d_branch_one).astype(bf16)
    d_context = dot_nt(d_branch_one, full_out).astype(bf16)
    d_context, grad_out = lax.optimization_barrier((d_context, grad_out))

    starts = [sum(CHUNKS[:i]) for i in range(len(CHUNKS))]
    cuts = [(starts[i] * TILE, (starts[i] + CHUNKS[i]) * TILE) for i in range(len(CHUNKS))]

    def backward(meta, i):
        return attention_backward(meta, queries, keys_values, d_context, context, rest, lse, qaug, kaug, bias, far,
                                  starts[i], CHUNKS[i])

    def weight_grad(d_q, d_kv):
        return [by_rows(contract_rows(normed_own, d_q).astype(bf16)),
                by_rows(contract_rows(normed_seen, d_kv).astype(bf16))]

    def query_rows(i, d_q):
        return by_rows(dot_nt(d_q, full_query[:, cuts[i][0]:cuts[i][1]]))

    def key_rows(i, d_kv):
        return by_rows(dot_nt(d_kv, full_kv[:, 2 * cuts[i][0]:2 * cuts[i][1]]))

    first = backward(meta, 0)
    meta, first, share_ff = lax.optimization_barrier((meta, first, share_ff))
    share_first = owners(jnp.concatenate(weight_grad(*first[:2]) + [grad_out], axis=1))
    f_query = query_rows(0, first[0])
    f_part = by_rows(key_rows(0, first[1]).astype(bf16))
    meta, f_query, f_part = lax.optimization_barrier((meta, f_query, f_part))
    f_first = sum_prompt(me, f_part)
    second = backward(meta, 1)
    second, f_first, share_in = lax.optimization_barrier((second, f_first, share_in))
    heads = bias_table.shape[1]
    near = jnp.sum(jnp.concatenate([first[2], second[2]], axis=0), axis=3).reshape(heads, 8 * TILE)
    bias_local = jnp.dot(near, jnp.asarray(bias_spread()), precision=lax.Precision.HIGHEST).reshape(-1, TILE)
    bias_top = bias_local.astype(bf16)
    bias_rest = (bias_local - bias_top.astype(f32)).astype(bf16)
    n_bias = bias_local.shape[0]
    size = gain_attn.shape[0]
    bias_columns = jnp.pad(jnp.concatenate([bias_top, bias_rest], axis=0), ((0, max(0, size - 2 * n_bias)), (0, 0)))
    bias_rows = bias_columns.shape[0]
    blocks = jnp.concatenate(weight_grad(*second[:2]), axis=1)
    n_last = blocks.shape[1]
    blocks = blocks.reshape(-1, size, n_last)
    if bias_rows > size:
        blocks = jnp.pad(blocks, ((0, 0), (0, bias_rows - size), (0, 0)))
    last = jnp.concatenate([blocks, jnp.broadcast_to(bias_columns[None], (blocks.shape[0],) + bias_columns.shape)],
                           axis=2).reshape(-1, n_last + TILE)
    owned_last = Owned(by_rows(last), me, "yx")
    owned_last.advance()
    f_query = f_query + query_rows(1, second[0])
    d_kv = sum_prompt(me, second[1])
    owned_last.advance()
    x_step, y_step = [(bit, "seq", pairs) for bit, pairs in seq_bits(me, "xy")]

    def flat(*shares):
        return jnp.concatenate([share.reshape(-1, width) for share in shares], axis=0)

    quarter_early = quarter_sum(flat(share_ff, share_in))
    f_total = f_first.astype(f32) + key_rows(1, d_kv)
    f_block = f_total[:QB].astype(bf16)
    owned_last.advance()
    owned_last.advance()
    owned_last.advance()
    quarter_first = quarter_sum(flat(share_first))
    owned_last.rows, quarter_early, quarter_first, f_total = lax.optimization_barrier((owned_last.rows, quarter_early, quarter_first, f_total))
    from_two = send(f_block, [(2, 0)])
    from_three = send(f_block, [(3, 0)])
    f_own = f_query + f_total[QB:] + jnp.concatenate(
        [jnp.where(me < 2, f_block, jnp.zeros_like(f_block)), from_two, from_three], axis=0).astype(f32)
    scaled_one = inputs * inverse_one
    d_scaled_one = f_own * gain_one
    d_tokens = d_middle + inverse_one * (
        d_scaled_one - scaled_one * jnp.mean(d_scaled_one * scaled_one, axis=1, keepdims=True))

    half_early = beside(quarter_early, *x_step, 0)
    early = beside(half_early, *y_step, 0).reshape(-1, width).astype(f32)
    n_ff = share_ff.shape[0]
    share_ff, share_in = early[:n_ff], early[n_ff:].reshape(size, -1)
    late = join_quarters(owned_last.finish(), me).reshape(bias_rows if bias_rows > size else size, -1).astype(f32)
    share_first = join_quarters(quarter_first, me).reshape(size, -1).astype(f32)
    share_out = share_first[:, -width:]
    shares = [share_first[:, :-width], late[:size, :n_last]]
    bias_grad = (late[:n_bias, n_last:] + late[n_bias:2 * n_bias, n_last:]).reshape(heads, NB).T
    share_query = jnp.concatenate(
        [share[:, :count * TILE] for share, count in zip(shares, CHUNKS)], axis=1)
    share_kv = jnp.concatenate(
        [share[:, count * TILE:] for share, count in zip(shares, CHUNKS)], axis=1)
    share_kv = share_kv.reshape(share_kv.shape[0], pairs, 2, TILE)
    share_key = share_kv[:, :, 0].reshape(-1, width)
    share_value = share_kv[:, :, 1].reshape(-1, width)
    gain_grad_one = (jnp.sum(share_query * w_query.astype(f32), axis=1)
                     + jnp.sum(share_key * w_key.astype(f32), axis=1)
                     + jnp.sum(share_value * w_value.astype(f32), axis=1)) / gain_attn.astype(f32)
    gain_grad_two = jnp.sum(share_in * w_in.astype(f32), axis=1) / gain_ff.astype(f32)
    return (
        final_rows.astype(bf16)[None],
        d_tokens[None],
        share_query,
        share_key,
        share_value,
        share_out,
        share_in,
        share_ff,
        gain_grad_one,
        gain_grad_two,
        bias_grad,
    )


def solution(mesh):
    rows = P("wshard", "seq", None)
    weight = P("wshard", None)
    placed = (rows, rows) + (weight,) * 7 + (P("wshard"), P("wshard"), P())
    return jax.shard_map(
        local,
        mesh=mesh,
        in_specs=placed,
        out_specs=(rows, rows) + (weight,) * 6 + (P("wshard"), P("wshard"), P()),
        check_vma=False,
    )
```

```python
import jax
import jax.numpy as jnp
import numpy as np
from jax import lax
from jax.experimental import pallas as pl
from jax.experimental.pallas import tpu as pltpu
from jax.experimental.layout import Layout, with_layout_constraint
from jax.sharding import PartitionSpec as P

DH = 64
NB = 32
PLEN = 1024
CLEN = 512
CONT = 4
QB = 256
NQ = 3
ROWS = QB * NQ
KROWS = PLEN + 2 * CLEN
TILE = 128
NEGATIVE = -1e30
f32 = jnp.float32
bf16 = jnp.bfloat16


def dot_nt(a, b):
    return lax.dot_general(a, b, (((1,), (1,)), ((), ())), preferred_element_type=f32)


def dot_nn(a, b):
    return lax.dot_general(a, b, (((1,), (0,)), ((), ())), preferred_element_type=f32)


def low_lanes(shape):
    return lax.broadcasted_iota(jnp.int32, shape, 1) < DH


def add_bias(s, bias_ref, head, kc, qc):
    rows = []
    for a in range(s.shape[0] // TILE):
        cols = []
        for b in range(s.shape[1] // TILE):
            d = jnp.clip(kc + a - qc[b], -2, 2) + 2
            cols.append(bias_ref[head, pl.ds(pl.multiple_of(d * TILE, TILE), TILE), :])
        rows.append(jnp.concatenate(cols, axis=1))
    return s + jnp.concatenate(rows, axis=0)


def fold_rows(rows):
    return jnp.sum(rows.reshape(rows.shape[0] // 8, 8, rows.shape[1]), axis=0)


def fold_max(rows):
    return jnp.max(rows.reshape(rows.shape[0] // 8, 8, rows.shape[1]), axis=0)


def forward_kernel(meta, q_ref, k_ref, v_ref, qaug_ref, kaug_ref, bias_ref, ctx_ref, rest_ref, lse_ref,
                   q_scr, vt_scr, s_scr, ctx_scr):
    low_q = low_lanes((ROWS, TILE))
    zero = jnp.zeros((ROWS, TILE), bf16)
    q_scr[0, :, :TILE] = jnp.where(low_q, q_ref[...], zero)
    q_scr[1, :, :TILE] = jnp.where(low_q, zero, q_ref[...])
    q_scr[0, :, TILE:] = qaug_ref[...]
    q_scr[1, :, TILE:] = qaug_ref[...]
    vt_scr[...] = v_ref[...].T
    keys = PLEN + CLEN
    chunks = keys // QB

    def place(unit):
        h, qb = unit // NQ, unit % NQ
        slot = pl.multiple_of(PLEN + meta[NQ + qb] * CLEN, CLEN)
        return h, slice(qb * QB, (qb + 1) * QB), meta[qb], slot

    def key_start(slot, c):
        return c * QB if c < PLEN // QB else pl.multiple_of(slot + (c * QB - PLEN), QB)

    def score_chunk(unit, c):
        h, columns, qc, slot = place(unit)
        rows = pl.ds(key_start(slot, c), QB)
        s = dot_nt(jnp.concatenate([k_ref[rows, :], kaug_ref[rows, :]], axis=1), q_scr[h, columns, :])
        s = add_bias(s, bias_ref, h, 2 * c, (qc, qc + 1))
        s_scr[unit % 2, c * QB:(c + 1) * QB, :] = s
        return fold_max(s)

    def weight_chunk(unit, c, m):
        h, columns, qc, slot = place(unit)
        p = jnp.exp(s_scr[unit % 2, c * QB:(c + 1) * QB, :] - m)
        v = vt_scr[h * DH:(h + 1) * DH, pl.ds(key_start(slot, c), QB)]
        return fold_rows(p), dot_nn(v, p.astype(bf16))

    units = 2 * NQ
    m = None
    for unit in range(-1, units):
        if unit >= 0:
            m = jnp.max(top, axis=0, keepdims=True)
        top = total = acc = None
        for c in range(chunks):
            if unit + 1 < units:
                t = score_chunk(unit + 1, c)
                top = t if top is None else jnp.maximum(top, t)
            if unit >= 0:
                l, o = weight_chunk(unit, c, m)
                total = l if total is None else total + l
                acc = o if acc is None else acc + o
        if unit >= 0:
            h, columns, qc, slot = place(unit)
            l = jnp.sum(total, axis=0, keepdims=True)
            ctx_scr[h * DH:(h + 1) * DH, columns] = acc / l
            lse_ref[0, h:h + 1, columns] = m + jnp.log(l)
    ctx = ctx_scr[...].T
    ctx_low = ctx.astype(bf16)
    ctx_ref[...] = ctx_low
    rest_ref[...] = (ctx - ctx_low.astype(f32)).astype(bf16)


def attention_forward(meta, q, kv, qaug, kaug, bias, first, pairs):
    own = pl.BlockSpec((ROWS, TILE), lambda i, meta: (0, first + i))
    out = pl.BlockSpec((ROWS, TILE), lambda i, meta: (0, i))
    keys = pl.BlockSpec((KROWS, TILE), lambda i, meta: (0, 2 * (first + i)))
    values = pl.BlockSpec((KROWS, TILE), lambda i, meta: (0, 2 * (first + i) + 1))
    fixed = lambda rows: pl.BlockSpec((rows, TILE), lambda i, meta: (0, 0))
    return pl.pallas_call(
        forward_kernel,
        grid_spec=pltpu.PrefetchScalarGridSpec(
            num_scalar_prefetch=1,
            grid=(pairs,),
            in_specs=[own, keys, values, fixed(ROWS), fixed(KROWS),
                      pl.BlockSpec((2, 5 * TILE, TILE), lambda i, meta: (first + i, 0, 0))],
            out_specs=[out, out, pl.BlockSpec((1, 2, ROWS), lambda i, meta: (i, 0, 0))],
            scratch_shapes=[
                pltpu.VMEM((2, ROWS, 2 * TILE), bf16),
                pltpu.VMEM((TILE, KROWS), bf16),
                pltpu.VMEM((2, PLEN + CLEN, QB), f32),
                pltpu.VMEM((TILE, ROWS), f32),
            ],
        ),
        out_shape=[jax.ShapeDtypeStruct((ROWS, pairs * TILE), bf16),
                   jax.ShapeDtypeStruct((ROWS, pairs * TILE), bf16),
                   jax.ShapeDtypeStruct((pairs, 2, ROWS), f32)],
        compiler_params=pltpu.CompilerParams(dimension_semantics=("arbitrary",),
                                             vmem_limit_bytes=56 << 20),
        cost_estimate=pl.CostEstimate(flops=pairs * 5_000_000_000, bytes_accessed=pairs * 2_000_000,
                                      transcendentals=pairs * 2 * ROWS * (PLEN + CLEN)),
        name="attention_forward",
    )(meta, q, kv, kv, qaug, kaug, bias)


PAD = TILE


def backward_kernel(meta, q_ref, k_ref, v_ref, do_ref, ctx_ref, rest_ref, lse_ref, qaug_ref, kaug_ref,
                    bias_ref, pick_ref, dq_ref, dkv_ref, near_ref,
                    kt_scr, q_scr, wide_scr, do_scr, delta_scr, ds_scr, p_scr, dks_scr, dvs_scr, far_scr):
    low_q = low_lanes((ROWS, TILE))
    kt_scr[...] = k_ref[...].T
    zero = jnp.zeros((ROWS, TILE), bf16)
    for h in range(2):
        q = q_ref[...]
        aug = qaug_ref[...]
        q_scr[h] = jnp.where(low_q, q, aug) if h == 0 else jnp.where(low_q, aug, q)
        wide_scr[h, :, :TILE] = jnp.where(low_q, q, zero) if h == 0 else jnp.where(low_q, zero, q)
        wide_scr[h, :, TILE:] = aug
        do = jnp.where(low_q, do_ref[...], zero) if h == 0 else jnp.where(low_q, zero, do_ref[...])
        for qb in range(NQ):
            do_scr[qb, h] = do[qb * QB:(qb + 1) * QB]
    prod = do_ref[...].astype(f32) * (ctx_ref[...].astype(f32) + rest_ref[...].astype(f32))
    hi = prod.astype(bf16)
    lo = (prod - hi.astype(f32)).astype(bf16)
    pick_row = lax.broadcasted_iota(jnp.int32, (8, TILE), 0)
    pick_low = low_lanes((8, TILE))
    pick = jnp.where((pick_row == 0) & pick_low | (pick_row == 1) & ~pick_low, 1.0, 0.0).astype(bf16)
    delta_scr[...] = dot_nt(pick, hi) + dot_nt(pick, lo)
    for h in range(2):
        ds_scr[h, 0:PAD, :] = jnp.zeros((PAD, ROWS), bf16)
        ds_scr[h, PAD + PLEN + CLEN:, :] = jnp.zeros((PAD, ROWS), bf16)

    def piece(h, kk, vv, kc, qb):
        cols = slice(qb * QB, (qb + 1) * QB)
        s = dot_nt(kk, wide_scr[h, cols, :])
        qc = meta[qb]
        s = add_bias(s, bias_ref, h, kc, (qc, qc + 1))
        p = jnp.exp(s - lse_ref[0, h:h + 1, cols])
        dp = dot_nt(vv, do_scr[qb, h])
        ds = (p * (dp - delta_scr[h:h + 1, cols])).astype(bf16)
        return p.astype(bf16), ds

    low_c = low_lanes((QB, TILE))

    def prompt_chunk(c, carry):
        start = c * QB
        rows = pl.ds(start, QB)
        kk = jnp.concatenate([k_ref[rows, :], kaug_ref[rows, :]], axis=1)
        vv = v_ref[rows, :]
        buffer = c % 2
        for h in range(2):
            for qb in range(NQ):
                cols = slice(qb * QB, (qb + 1) * QB)
                p, ds = piece(h, kk, vv, 2 * c, qb)
                ds_scr[h, pl.ds(PAD + start, QB), cols] = ds
                p_scr[buffer, :, (2 * qb + h) * QB:(2 * qb + h + 1) * QB] = p
        dv = dot_nn(p_scr[buffer], do_scr[...].reshape(2 * ROWS, TILE))
        dks = [dot_nn(ds_scr[h, pl.ds(PAD + start, QB), :], q_scr[h]) for h in range(2)]
        dkv_ref[rows, TILE:] = dv.astype(bf16)
        dkv_ref[rows, :TILE] = jnp.where(low_c, dks[0], dks[1]).astype(bf16)
        sums = jnp.where(low_c, dks[1], dks[0])
        far_scr[2 * c] = fold_rows(sums[:TILE])
        far_scr[2 * c + 1] = fold_rows(sums[TILE:])
        return carry

    for c in range(PLEN // QB):
        prompt_chunk(c, 0)
    for qb in range(NQ):
        cols = slice(qb * QB, (qb + 1) * QB)
        slot = pl.multiple_of(PLEN + meta[NQ + qb] * CLEN, CLEN)
        for half in range(CLEN // QB):
            rows = pl.ds(pl.multiple_of(slot + half * QB, QB), QB)
            there = slice(half * QB, (half + 1) * QB)
            kk = jnp.concatenate([k_ref[rows, :], kaug_ref[rows, :]], axis=1)
            vv = v_ref[rows, :]
            ps = []
            for h in range(2):
                p, ds = piece(h, kk, vv, 8 + 2 * half, qb)
                ds_scr[h, PAD + PLEN + half * QB:PAD + PLEN + (half + 1) * QB, cols] = ds
                ps.append(p)
                dks_scr[qb, h, there, :] = dot_nn(ds, q_scr[h, cols, :])
            dvs_scr[qb, there, :] = dot_nn(jnp.concatenate(ps, axis=1), do_scr[qb].reshape(2 * QB, TILE))
    for slot in range(2):
        for half in range(CLEN // TILE):
            there = slice(half * TILE, (half + 1) * TILE)
            rows = slice(PLEN + slot * CLEN + half * TILE, PLEN + slot * CLEN + (half + 1) * TILE)
            totals = [None] * 3
            for qb in range(NQ):
                mine = meta[NQ + qb] == slot
                parts = (dvs_scr[qb, there, :], dks_scr[qb, 0, there, :], dks_scr[qb, 1, there, :])
                for i, part in enumerate(parts):
                    part = jnp.where(mine, part, 0.0)
                    totals[i] = part if totals[i] is None else totals[i] + part
            dkv_ref[rows, TILE:] = totals[0].astype(bf16)
            low_t = low_lanes((TILE, TILE))
            dkv_ref[rows, :TILE] = jnp.where(low_t, totals[1], totals[2]).astype(bf16)
            far_scr[8 + slot * (CLEN // TILE) + half] = fold_rows(jnp.where(low_t, totals[2], totals[1]))

    dqt = []
    for h in range(2):
        parts = []
        for qb in range(NQ):
            cols = slice(qb * QB, (qb + 1) * QB)
            slot = pl.multiple_of(PLEN + meta[NQ + qb] * CLEN, CLEN)
            rows = slice(h * DH, (h + 1) * DH)
            keys = jnp.concatenate([kt_scr[rows, 0:PLEN], kt_scr[rows, pl.ds(slot, CLEN)]], axis=1)
            parts.append(dot_nn(keys, ds_scr[h, PAD:PAD + PLEN + CLEN, cols]))
        dqt.append(jnp.concatenate(parts, axis=1))
    dq_ref[...] = jnp.concatenate(dqt, axis=0).T.astype(bf16)

    row_id = lax.broadcasted_iota(jnp.int32, (TILE, TILE), 0)
    lane_id = lax.broadcasted_iota(jnp.int32, (TILE, TILE), 1)
    flip = jnp.where(row_id + lane_id == TILE - 1, 1.0, 0.0).astype(bf16)
    flips = jnp.concatenate([flip, flip], axis=0)
    for h in range(2):
        acc = None
        for qb in range(NQ):
            tiles = [ds_scr[h, pl.ds(pl.multiple_of((meta[qb] + half) * TILE, TILE), 3 * TILE),
                            (2 * qb + half) * TILE:(2 * qb + half + 1) * TILE] for half in range(2)]
            part = dot_nn(jnp.concatenate(tiles, axis=1), flips)
            acc = part if acc is None else acc + part
        sums = []
        for d in range(3):
            rolled = pltpu.roll(acc[d * TILE:(d + 1) * TILE], 0, 1, stride=1, stride_axis=0)
            wrapped = jnp.where(lane_id < row_id, rolled, 0.0)
            sums += [fold_rows(rolled), fold_rows(wrapped)]
        for side in range(2):
            total = None
            for t in range(16):
                term = far_scr[t] * pick_ref[h, side, t]
                total = term if total is None else total + term
            sums.append(total)
        for i, eight in enumerate(sums):
            near_ref[0, h, i] = eight


def attention_backward(meta, q, kv, do, ctx, rest, lse, qaug, kaug, bias, pick, first, pairs):
    own = pl.BlockSpec((ROWS, TILE), lambda i, meta: (0, first + i))
    keys = pl.BlockSpec((KROWS, TILE), lambda i, meta: (0, 2 * (first + i)))
    values = pl.BlockSpec((KROWS, TILE), lambda i, meta: (0, 2 * (first + i) + 1))
    fixed = lambda rows: pl.BlockSpec((rows, TILE), lambda i, meta: (0, 0))
    return pl.pallas_call(
        backward_kernel,
        grid_spec=pltpu.PrefetchScalarGridSpec(
            num_scalar_prefetch=1,
            grid=(pairs,),
            in_specs=[own, keys, values, own, own, own,
                      pl.BlockSpec((1, 2, ROWS), lambda i, meta: (first + i, 0, 0)),
                      fixed(ROWS), fixed(KROWS),
                      pl.BlockSpec((2, 5 * TILE, TILE), lambda i, meta: (first + i, 0, 0)),
                      pl.BlockSpec((2, 2, 16, 8, TILE), lambda i, meta: (0, 0, 0, 0, 0))],
            out_specs=[pl.BlockSpec((ROWS, TILE), lambda i, meta: (0, i)),
                       pl.BlockSpec((KROWS, 2 * TILE), lambda i, meta: (0, i)),
                       pl.BlockSpec((1, 2, 8, 8, TILE), lambda i, meta: (i, 0, 0, 0, 0))],
            scratch_shapes=[
                pltpu.VMEM((TILE, KROWS), bf16),
                pltpu.VMEM((2, ROWS, TILE), bf16),
                pltpu.VMEM((2, ROWS, 2 * TILE), bf16),
                pltpu.VMEM((NQ, 2, QB, TILE), bf16),
                pltpu.VMEM((8, ROWS), f32),
                pltpu.VMEM((2, PLEN + CLEN + 2 * PAD, ROWS), bf16),
                pltpu.VMEM((2, QB, 2 * ROWS), bf16),
                pltpu.VMEM((NQ, 2, CLEN, TILE), f32),
                pltpu.VMEM((NQ, CLEN, TILE), f32),
                pltpu.VMEM((16, 8, TILE), f32),
            ],
        ),
        out_shape=[jax.ShapeDtypeStruct((ROWS, pairs * TILE), bf16),
                   jax.ShapeDtypeStruct((KROWS, 2 * pairs * TILE), bf16),
                   jax.ShapeDtypeStruct((pairs, 2, 8, 8, TILE), f32)],
        compiler_params=pltpu.CompilerParams(dimension_semantics=("arbitrary",),
                                             vmem_limit_bytes=56 << 20),
        cost_estimate=pl.CostEstimate(flops=pairs * 10_000_000_000, bytes_accessed=pairs * 3_000_000,
                                      transcendentals=pairs * 2 * ROWS * (PLEN + CLEN)),
        name="attention_backward",
    )(meta, q, kv, kv, do, ctx, rest, lse, qaug, kaug, bias, pick)


EPSILON = 1e-06
THRESHOLDS = (12, 16, 23, 32, 46, 64, 91)
OWNER_BLOCK = (0, 3, 1, 2)


def python_bucket(offset):
    magnitude = abs(offset)
    base = NB // 2 if offset > 0 else 0
    if magnitude < 8:
        return base + magnitude
    return base + 8 + sum(1 for edge in THRESHOLDS if magnitude >= edge)


def bias_spread():
    spread = np.zeros((8, TILE, NB), np.float32)
    for lane in range(TILE):
        for d in range(3):
            inside = python_bucket(TILE * (d - 1) + lane - (TILE - 1))
            passed = python_bucket(TILE * d + lane - (TILE - 1))
            spread[2 * d, lane, inside] += 1
            spread[2 * d + 1, lane, passed] += 1
            spread[2 * d + 1, lane, inside] -= 1
    spread[6, :, python_bucket(-200)] = 1
    spread[7, :, python_bucket(200)] = 1
    return spread.reshape(8 * TILE, NB)


def setup_kernel(meta, limit, table, bias_ref, qaug_ref, kaug_ref, far_ref):
    head = pl.program_id(0)
    heads = pl.num_programs(0)
    near = (lax.broadcasted_iota(jnp.int32, (TILE, TILE), 0)
            - lax.broadcasted_iota(jnp.int32, (TILE, TILE), 1))
    for d in range(-2, 3):
        first, last = TILE * d - TILE + 1, TILE * d + TILE - 1
        previous = python_bucket(first)
        tile = jnp.full((TILE, TILE), table[previous * heads + head], f32)
        for n in range(first + 1, last + 1):
            current = python_bucket(n)
            if current != previous:
                tile = jnp.where(near >= n - TILE * d, table[current * heads + head], tile)
                previous = current
        bias_ref[0, (d + 2) * TILE:(d + 3) * TILE, :] = tile

    @pl.when(head == 0)
    def _():
        shape = (ROWS, TILE)
        sub = lax.broadcasted_iota(jnp.int32, shape, 1) & (DH - 1)
        qaug_ref[...] = jnp.where(sub == lax.broadcasted_iota(jnp.int32, shape, 0) // TILE, 1.0, 0.0).astype(bf16)
        shape = (KROWS, TILE)
        key = lax.broadcasted_iota(jnp.int32, shape, 0)
        sub = lax.broadcasted_iota(jnp.int32, shape, 1) & (DH - 1)
        kaug = jnp.zeros(shape, f32)
        for q in range(NQ):
            first = PLEN + CLEN * meta[NQ + q]
            hidden = (key >= PLEN) & ((key < first) | (key >= first + limit[q]))
            kaug = jnp.where(((sub == 2 * q) | (sub == 2 * q + 1)) & hidden, NEGATIVE, kaug)
        kaug_ref[...] = kaug.astype(bf16)
        lane = lax.broadcasted_iota(jnp.int32, (8, TILE), 1)
        for h in range(2):
            for row in range(16):
                key_tile = row if row < 8 else 8 + (row - 8) % 4
                for side in range(2):
                    out = jnp.zeros((8, TILE), f32)
                    for q in range(2 * NQ):
                        apart = key_tile - (meta[q // 2] + q % 2)
                        is_far = (apart <= -2) if side == 0 else (apart >= 2)
                        out = jnp.where(lane == q + (DH if h == 0 else 0), jnp.where(is_far, 1.0, 0.0), out)
                    far_ref[h, side, row] = out


def setup(me, spans, table):
    block = NQ * me + jnp.arange(NQ, dtype=jnp.int32)
    prompt = block < PLEN // QB
    cont = jnp.maximum(block - PLEN // QB, 0) // 2
    half = jnp.maximum(block - PLEN // QB, 0) % 2
    tile = jnp.where(prompt, 2 * block, PLEN // TILE + 2 * half)
    slot = jnp.where(prompt, 0, cont - (me - 1))
    chosen = cont[:, None] == jnp.arange(CONT, dtype=jnp.int32)[None, :]
    limit = jnp.where(prompt, 0, jnp.sum(jnp.where(chosen, spans[None, :], 0), axis=1)).astype(jnp.int32)
    meta = jnp.concatenate([tile, slot]).astype(jnp.int32)
    heads = table.shape[1]
    whole = lambda *shape: pl.BlockSpec(shape, lambda i, *_: (0,) * len(shape))
    bias, qaug, kaug, far = pl.pallas_call(
        setup_kernel,
        grid_spec=pltpu.PrefetchScalarGridSpec(
            num_scalar_prefetch=3,
            grid=(heads,),
            in_specs=[],
            out_specs=[pl.BlockSpec((1, 5 * TILE, TILE), lambda i, *_: (i, 0, 0)),
                       whole(ROWS, TILE), whole(KROWS, TILE), whole(2, 2, 16, 8, TILE)],
        ),
        out_shape=[jax.ShapeDtypeStruct((heads, 5 * TILE, TILE), f32),
                   jax.ShapeDtypeStruct((ROWS, TILE), bf16),
                   jax.ShapeDtypeStruct((KROWS, TILE), bf16),
                   jax.ShapeDtypeStruct((2, 2, 16, 8, TILE), f32)],
        compiler_params=pltpu.CompilerParams(dimension_semantics=("arbitrary",)),
        cost_estimate=pl.CostEstimate(flops=30_000_000, bytes_accessed=5_000_000, transcendentals=0),
        name="setup",
    )(meta, limit, table.astype(f32).reshape(-1))
    return meta, bias, qaug, kaug, far


def by_rows(x):
    return with_layout_constraint(x, Layout(tuple(range(x.ndim))))


def rms(rows):
    return lax.rsqrt(jnp.mean(rows * rows, axis=1, keepdims=True) + EPSILON)


def normed_rows(rows, gain):
    rows = rows.astype(f32)
    return (rows * rms(rows) * gain).astype(bf16)


def contract_rows(left, right):
    return lax.dot_general(left, right, (((0,), (0,)), ((), ())), preferred_element_type=f32)


def block_of(rows, i):
    return rows[i * QB:(i + 1) * QB]


def send(rows, pairs):
    return lax.ppermute(rows, "seq", pairs)


def pick_by(me, *choices):
    out = choices[-1]
    for i in range(len(choices) - 2, -1, -1):
        out = jnp.where(me == i, choices[i], out)
    return out


def exchange_rows(me, own):
    low, high = own[:ROWS // 2], own[ROWS // 2:]
    return (send(jnp.where(me == 2, high, low), [(0, 1), (1, 0), (2, 3), (3, 2)]),
            send(jnp.where(me == 0, high, low), [(0, 2), (1, 3)]))


def exchange_again(me, own, across, down):
    low, high = own[:ROWS // 2], own[ROWS // 2:]
    return (send(jnp.where(me == 0, high, down), [(0, 1), (2, 3), (3, 2)]),
            send(jnp.where(me == 0, low, across), [(0, 2), (1, 3)]))


def seen_rows(me, own, got):
    across, down, across_again, down_again = got
    mine = [block_of(own, i) for i in range(NQ)]
    low, high = own[:ROWS // 2], own[ROWS // 2:]
    prompt = [
        pick_by(me, low, across, down_again, down_again),
        pick_by(me, high, across_again, down, across_again),
        pick_by(me, across[:QB], mine[0], across_again[:QB], down[:QB]),
    ]
    slots = [
        pick_by(me, mine[0], mine[1], mine[0], across[ROWS // 2 - QB:]),
        pick_by(me, mine[1], mine[2], mine[1], mine[0]),
        pick_by(me, mine[1], mine[1], mine[2], mine[1]),
        pick_by(me, mine[2], mine[2], across[:QB], mine[2]),
    ]
    return jnp.concatenate(prompt + slots, axis=0)


def halve(rows, bit, axis, pairs):
    n, r, c = rows.shape
    parts = rows.reshape(n, 2, r // 2, c)
    away = lax.dynamic_index_in_dim(parts, 1 - bit, 1, keepdims=False)
    kept = lax.dynamic_index_in_dim(parts, bit, 1, keepdims=False)
    got = lax.ppermute(away, axis, pairs)
    return (kept.astype(f32) + got.astype(f32)).astype(bf16)


def join(rows, bit, axis, pairs):
    got = lax.ppermute(rows, axis, pairs)
    return jnp.concatenate([jnp.where(bit == 0, rows, got), jnp.where(bit == 0, got, rows)], axis=-2)


def seq_bits(me, order):
    steps = {"x": (me % 2, [(i, i ^ 1) for i in range(4)]), "y": (me // 2, [(i, i ^ 2) for i in range(4)])}
    return [steps[name] for name in order]


class Owned:
    def __init__(self, grad, me, order):
        self.step, self.steps = 0, seq_bits(me, order)
        self.rows = grad
        if lax.axis_size("wshard") != 8:
            self.rows = quarter_sum(lax.psum_scatter(grad, "wshard", scatter_dimension=0, tiled=True))
            self.step = 5

    def advance(self):
        place = lax.axis_index("wshard")
        flip = lambda bit: [(i, i ^ bit) for i in range(8)]
        step, rows = self.step, self.rows
        if step == 0:
            rows = halve(rows.reshape(4, -1, rows.shape[1]), place % 2, "wshard", flip(1))
        elif step in (1, 2):
            rows = halve(rows, self.steps[step - 1][0], "seq", self.steps[step - 1][1])
        elif step == 3:
            rows = halve(rows.reshape(1, -1, rows.shape[2]), place // 4, "wshard", flip(4))
        elif step == 4:
            rows = halve(rows, place // 2 % 2, "wshard", flip(2))[0]
        self.step, self.rows = step + 1, rows

    def finish(self):
        while self.step < 5:
            self.advance()
        return self.rows


def beside(rows, bit, axis, pairs, dim):
    got = lax.ppermute(rows, axis, pairs)
    return jnp.stack([jnp.where(bit == 0, rows, got), jnp.where(bit == 0, got, rows)], axis=dim)


class Gathered:
    def __init__(self, me, w_ff, w_out):
        self.plain = lax.axis_size("wshard") != 8
        if self.plain:
            self.state = [lax.all_gather(w, "wshard", axis=0, tiled=True) for w in (w_ff, w_out)]
            return
        place = lax.axis_index("wshard")
        self.core, self.depth = place % 2, place // 2
        self.n, self.m = w_ff.shape[0] // 4, w_out.shape[0] // 4
        self.cut = 2 * self.n // 3
        quarter = jnp.concatenate([lax.dynamic_slice_in_dim(w_ff, me * self.n, self.n, 0),
                                   lax.dynamic_slice_in_dim(w_out, me * self.m, self.m, 0)], axis=0)
        self.state = [quarter] + [
            lax.ppermute(quarter, "wshard", [(i, ((i // 2 + k) % 4) * 2 + i % 2) for i in range(8)])
            for k in range(1, 4)]
        self.steps = [seq_bits(me, "xy"), seq_bits(me, "yx")]

    def exchange(self, i):
        if self.plain:
            return
        if i == 0:
            rows = jnp.stack([pick_by((self.depth - d) % 4, *self.state) for d in range(4)])
            self.state = [rows[:, :self.cut], rows[:, self.cut:]]
        self.state = [beside(rows, steps[i][0], "seq", steps[i][1], dim)
                      for rows, steps, dim in zip(self.state, self.steps, (1, 1 + i))]

    def cores(self):
        if not self.plain:
            rows = jnp.concatenate(self.state, axis=-2)
            self.state = [beside(rows, self.core, "wshard", [(i, i ^ 1) for i in range(8)], 1)]

    def tie(self, others):
        others, self.state = lax.optimization_barrier((others, self.state))
        return others

    def whole(self):
        if self.plain:
            return self.state
        rows = self.state[0]
        c = rows.shape[-1]
        return rows[..., :self.n, :].reshape(32 * self.n, c), rows[..., self.n:, :].reshape(32 * self.m, c)


def quarter_sum(rows):
    parts = lax.all_to_all(rows.reshape(4, -1, rows.shape[1]), "seq", split_axis=0, concat_axis=0, tiled=True)
    return jnp.sum(parts.astype(f32), axis=0).astype(bf16)


def join_quarters(rows, me):
    steps = seq_bits(me, "xy")
    rows = beside(rows, *steps[0][:1], "seq", steps[0][1], 0)
    return beside(rows, steps[1][0], "seq", steps[1][1], 0).reshape((4,) + rows.shape[1:])


def sum_prompt(me, partial):
    owner = jnp.array(OWNER_BLOCK, jnp.int32)

    def take(device):
        start = owner[device] * QB
        return lax.dynamic_slice_in_dim(partial, start, QB, 0)

    total = take(me).astype(f32)
    for flip in (1, 2, 3):
        total = total + send(take(me ^ flip), [(i, i ^ flip) for i in range(4)]).astype(f32)
    parts = [block_of(partial, i) for i in range(8)]
    crossed = send(jnp.where(me == 2, parts[7], parts[4]), [(2, 3), (3, 2)])
    zero = jnp.zeros_like(parts[0])
    joined = (jnp.where(me == 2, parts[6], parts[5]).astype(f32) + crossed.astype(f32)).astype(bf16)
    rows = [
        total.astype(bf16),
        pick_by(me, zero, zero, parts[4], joined),
        pick_by(me, zero, parts[4], parts[5], parts[6]),
        pick_by(me, zero, parts[5], joined, parts[7]),
    ]
    return jnp.concatenate(rows, axis=0)


CHUNKS = (4, 2)


def interleave(key_part, value_part):
    r, w = key_part.shape
    both = jnp.stack([key_part.reshape(r, w // TILE, TILE), value_part.reshape(r, w // TILE, TILE)], axis=2)
    return both.reshape(r, 2 * w)


def local(tokens, teacher, lengths, w_query, w_key, w_value, w_out, w_in, w_ff, gain_attn, gain_ff, bias_table):
    me = lax.axis_index("seq")
    own = by_rows(tokens[0])
    inputs = own.astype(f32)
    targets = teacher[0].astype(f32)
    spans = lengths[0]
    width = own.shape[1]
    pairs = width // TILE

    def gather(w):
        return lax.all_gather(w, "wshard", axis=0, tiled=True)

    w_kv = interleave(w_key, w_value)
    gain_columns = jnp.pad(jnp.stack([gain_attn, gain_ff], axis=1), ((0, 0), (0, TILE - 2)))
    first = gather(jnp.concatenate([w_query, w_kv, gain_columns], axis=1))
    full_query, full_kv = first[:, :width], first[:, width:3 * width]
    gains = first[:, 3 * width:3 * width + 2].astype(f32).T
    gain_one, gain_two = gains[0], gains[1]
    gathered = Gathered(me, w_ff, w_out)
    full_in = gather(w_in)
    got = exchange_rows(me, own)
    got, spans, table = lax.optimization_barrier((got, spans, bias_table))
    got = got + exchange_again(me, own, *got)
    prepared = setup(me, spans, table)
    inverse_one = rms(inputs)
    got, prepared, inverse_one = gathered.tie((got, prepared, inverse_one))
    meta, bias, qaug, kaug, far = prepared
    gathered.exchange(0)
    normed_own = by_rows((inputs * inverse_one * gain_one).astype(bf16))
    seen = gathered.tie(by_rows(seen_rows(me, own, got)))
    gathered.exchange(1)
    normed_seen = by_rows(normed_rows(seen, gain_one))
    queries = jnp.dot(normed_own, full_query, preferred_element_type=f32).astype(bf16)
    keys_values = jnp.dot(normed_seen, full_kv, preferred_element_type=f32).astype(bf16)
    meta, queries, keys_values = gathered.tie((meta, queries, keys_values))
    gathered.cores()
    context, rest, lse = gathered.tie(attention_forward(meta, queries, keys_values, qaug, kaug, bias, 0, pairs))
    full_ff, full_out = gathered.whole()
    middle = by_rows(inputs + jnp.dot(context, full_out, preferred_element_type=f32))
    inverse_two = rms(middle)
    normed_two = by_rows((middle * inverse_two * gain_two).astype(bf16))
    hidden_act = jnp.maximum(jnp.dot(normed_two, full_in, preferred_element_type=f32), 0.0).astype(bf16)
    final_rows = middle + jnp.dot(hidden_act, full_ff, preferred_element_type=f32)
    local_rows = inputs.shape[0]
    row_index = me * local_rows + lax.iota(jnp.int32, local_rows)
    slot_index = jnp.maximum(row_index - PLEN, 0)
    owner_match = (slot_index // CLEN)[:, None] == lax.iota(jnp.int32, CONT)[None, :]
    row_limit = jnp.sum(jnp.where(owner_match, spans[None, :], 0), axis=1)
    valid_rows = (row_index < PLEN) | (slot_index % CLEN < row_limit)
    row_count = PLEN + jnp.sum(spans).astype(f32)
    factor = (PLEN + CONT * CLEN) / row_count
    d_final = jnp.where(valid_rows[:, None], factor * (final_rows - targets), 0.0)
    d_final = by_rows(d_final)
    d_branch_two = by_rows(d_final.astype(bf16))

    def owners(g):
        return lax.psum_scatter(g, "wshard", scatter_dimension=0, tiled=True)

    size = gain_attn.shape[0]
    share_ff = owners(by_rows(contract_rows(hidden_act, d_branch_two).astype(bf16)))
    d_pre = jnp.where(hidden_act > 0, dot_nt(d_branch_two, full_ff), 0.0).astype(bf16)
    share_in = owners(by_rows(contract_rows(normed_two, d_pre).astype(bf16)))
    d_normed_two = by_rows(dot_nt(d_pre, full_in))
    scaled_two = middle * inverse_two
    d_scaled_two = d_normed_two * gain_two
    d_middle = d_final + inverse_two * (
        d_scaled_two - scaled_two * jnp.mean(d_scaled_two * scaled_two, axis=1, keepdims=True))
    d_middle = by_rows(d_middle)
    d_branch_one = by_rows(d_middle.astype(bf16))
    grad_out = contract_rows(context, d_branch_one).astype(bf16)
    d_context = dot_nt(d_branch_one, full_out).astype(bf16)
    d_context, grad_out = lax.optimization_barrier((d_context, grad_out))

    starts = [sum(CHUNKS[:i]) for i in range(len(CHUNKS))]
    cuts = [(starts[i] * TILE, (starts[i] + CHUNKS[i]) * TILE) for i in range(len(CHUNKS))]

    def backward(meta, i):
        return attention_backward(meta, queries, keys_values, d_context, context, rest, lse, qaug, kaug, bias, far,
                                  starts[i], CHUNKS[i])

    def weight_grad(d_q, d_kv):
        return [by_rows(contract_rows(normed_own, d_q).astype(bf16)),
                by_rows(contract_rows(normed_seen, d_kv).astype(bf16))]

    def query_rows(i, d_q):
        return by_rows(dot_nt(d_q, full_query[:, cuts[i][0]:cuts[i][1]]))

    def key_rows(i, d_kv):
        return by_rows(dot_nt(d_kv, full_kv[:, 2 * cuts[i][0]:2 * cuts[i][1]]))

    first = backward(meta, 0)
    meta, first, share_ff = lax.optimization_barrier((meta, first, share_ff))
    share_first = owners(jnp.concatenate(weight_grad(*first[:2]) + [grad_out], axis=1))
    f_query = query_rows(0, first[0])
    f_part = by_rows(key_rows(0, first[1]).astype(bf16))
    meta, f_query, f_part = lax.optimization_barrier((meta, f_query, f_part))
    f_first = sum_prompt(me, f_part)
    second = backward(meta, 1)
    second, f_first, share_in = lax.optimization_barrier((second, f_first, share_in))
    heads = bias_table.shape[1]
    near = jnp.sum(jnp.concatenate([first[2], second[2]], axis=0), axis=3).reshape(heads, 8 * TILE)
    bias_local = jnp.dot(near, jnp.asarray(bias_spread()), precision=lax.Precision.HIGHEST).reshape(-1, TILE)
    bias_top = bias_local.astype(bf16)
    bias_rest = (bias_local - bias_top.astype(f32)).astype(bf16)
    n_bias = bias_local.shape[0]
    size = gain_attn.shape[0]
    bias_columns = jnp.pad(jnp.concatenate([bias_top, bias_rest], axis=0), ((0, max(0, size - 2 * n_bias)), (0, 0)))
    bias_rows = bias_columns.shape[0]
    blocks = jnp.concatenate(weight_grad(*second[:2]), axis=1)
    n_last = blocks.shape[1]
    blocks = blocks.reshape(-1, size, n_last)
    if bias_rows > size:
        blocks = jnp.pad(blocks, ((0, 0), (0, bias_rows - size), (0, 0)))
    last = jnp.concatenate([blocks, jnp.broadcast_to(bias_columns[None], (blocks.shape[0],) + bias_columns.shape)],
                           axis=2).reshape(-1, n_last + TILE)
    owned_last = Owned(by_rows(last), me, "yx")
    owned_last.advance()
    f_query = f_query + query_rows(1, second[0])
    d_kv = sum_prompt(me, second[1])
    owned_last.advance()
    x_step, y_step = [(bit, "seq", pairs) for bit, pairs in seq_bits(me, "xy")]

    def flat(*shares):
        return jnp.concatenate([share.reshape(-1, width) for share in shares], axis=0)

    quarter_early = quarter_sum(flat(share_ff, share_in))
    f_total = f_first.astype(f32) + key_rows(1, d_kv)
    f_block = f_total[:QB].astype(bf16)
    owned_last.advance()
    owned_last.advance()
    owned_last.advance()
    quarter_first = quarter_sum(flat(share_first))
    owned_last.rows, quarter_early, quarter_first, f_total = lax.optimization_barrier((owned_last.rows, quarter_early, quarter_first, f_total))
    from_two = send(f_block, [(2, 0)])
    from_three = send(f_block, [(3, 0)])
    f_own = f_query + f_total[QB:] + jnp.concatenate(
        [jnp.where(me < 2, f_block, jnp.zeros_like(f_block)), from_two, from_three], axis=0).astype(f32)
    scaled_one = inputs * inverse_one
    d_scaled_one = f_own * gain_one
    d_tokens = d_middle + inverse_one * (
        d_scaled_one - scaled_one * jnp.mean(d_scaled_one * scaled_one, axis=1, keepdims=True))

    half_early = beside(quarter_early, *x_step, 0)
    early = beside(half_early, *y_step, 0).reshape(-1, width).astype(f32)
    n_ff = share_ff.shape[0]
    share_ff, share_in = early[:n_ff], early[n_ff:].reshape(size, -1)
    late = join_quarters(owned_last.finish(), me).reshape(bias_rows if bias_rows > size else size, -1).astype(f32)
    share_first = join_quarters(quarter_first, me).reshape(size, -1).astype(f32)
    share_out = share_first[:, -width:]
    shares = [share_first[:, :-width], late[:size, :n_last]]
    bias_grad = (late[:n_bias, n_last:] + late[n_bias:2 * n_bias, n_last:]).reshape(heads, NB).T
    share_query = jnp.concatenate(
        [share[:, :count * TILE] for share, count in zip(shares, CHUNKS)], axis=1)
    share_kv = jnp.concatenate(
        [share[:, count * TILE:] for share, count in zip(shares, CHUNKS)], axis=1)
    share_kv = share_kv.reshape(share_kv.shape[0], pairs, 2, TILE)
    share_key = share_kv[:, :, 0].reshape(-1, width)
    share_value = share_kv[:, :, 1].reshape(-1, width)
    gain_grad_one = (jnp.sum(share_query * w_query.astype(f32), axis=1)
                     + jnp.sum(share_key * w_key.astype(f32), axis=1)
                     + jnp.sum(share_value * w_value.astype(f32), axis=1)) / gain_attn.astype(f32)
    gain_grad_two = jnp.sum(share_in * w_in.astype(f32), axis=1) / gain_ff.astype(f32)
    return (
        final_rows.astype(bf16)[None],
        d_tokens[None],
        share_query,
        share_key,
        share_value,
        share_out,
        share_in,
        share_ff,
        gain_grad_one,
        gain_grad_two,
        bias_grad,
    )


def solution(mesh):
    rows = P("wshard", "seq", None)
    weight = P("wshard", None)
    placed = (rows, rows) + (weight,) * 7 + (P("wshard"), P("wshard"), P())
    return jax.shard_map(
        local,
        mesh=mesh,
        in_specs=placed,
        out_specs=(rows, rows) + (weight,) * 6 + (P("wshard"), P("wshard"), P()),
        check_vma=False,
    )
```

```python
import jax
import jax.numpy as jnp
import numpy as np
from jax import lax
from jax.experimental import pallas as pl
from jax.experimental.pallas import tpu as pltpu
from jax.experimental.layout import Layout, with_layout_constraint
from jax.sharding import PartitionSpec as P

DH = 64
NB = 32
PLEN = 1024
CLEN = 512
CONT = 4
QB = 256
NQ = 3
ROWS = QB * NQ
KROWS = PLEN + 2 * CLEN
TILE = 128
NEGATIVE = -1e30
f32 = jnp.float32
bf16 = jnp.bfloat16


def dot_nt(a, b):
    return lax.dot_general(a, b, (((1,), (1,)), ((), ())), preferred_element_type=f32)


def dot_nn(a, b):
    return lax.dot_general(a, b, (((1,), (0,)), ((), ())), preferred_element_type=f32)


def low_lanes(shape):
    return lax.broadcasted_iota(jnp.int32, shape, 1) < DH


def add_bias(s, bias_ref, head, kc, qc):
    rows = []
    for a in range(s.shape[0] // TILE):
        cols = []
        for b in range(s.shape[1] // TILE):
            d = jnp.clip(kc + a - qc[b], -2, 2) + 2
            cols.append(bias_ref[head, pl.ds(pl.multiple_of(d * TILE, TILE), TILE), :])
        rows.append(jnp.concatenate(cols, axis=1))
    return s + jnp.concatenate(rows, axis=0)


def fold_rows(rows):
    return jnp.sum(rows.reshape(rows.shape[0] // 8, 8, rows.shape[1]), axis=0)


def fold_max(rows):
    return jnp.max(rows.reshape(rows.shape[0] // 8, 8, rows.shape[1]), axis=0)


def forward_kernel(meta, q_ref, k_ref, v_ref, qaug_ref, kaug_ref, bias_ref, ctx_ref, rest_ref, lse_ref,
                   q_scr, vt_scr, s_scr, ctx_scr):
    low_q = low_lanes((ROWS, TILE))
    zero = jnp.zeros((ROWS, TILE), bf16)
    q_scr[0, :, :TILE] = jnp.where(low_q, q_ref[...], zero)
    q_scr[1, :, :TILE] = jnp.where(low_q, zero, q_ref[...])
    q_scr[0, :, TILE:] = qaug_ref[...]
    q_scr[1, :, TILE:] = qaug_ref[...]
    vt_scr[...] = v_ref[...].T
    keys = PLEN + CLEN
    chunks = keys // QB

    def place(unit):
        h, qb = unit // NQ, unit % NQ
        slot = pl.multiple_of(PLEN + meta[NQ + qb] * CLEN, CLEN)
        return h, slice(qb * QB, (qb + 1) * QB), meta[qb], slot

    def key_start(slot, c):
        return c * QB if c < PLEN // QB else pl.multiple_of(slot + (c * QB - PLEN), QB)

    def score_chunk(unit, c):
        h, columns, qc, slot = place(unit)
        rows = pl.ds(key_start(slot, c), QB)
        s = dot_nt(jnp.concatenate([k_ref[rows, :], kaug_ref[rows, :]], axis=1), q_scr[h, columns, :])
        s = add_bias(s, bias_ref, h, 2 * c, (qc, qc + 1))
        s_scr[unit % 2, c * QB:(c + 1) * QB, :] = s
        return fold_max(s)

    def weight_chunk(unit, c, m):
        h, columns, qc, slot = place(unit)
        p = jnp.exp(s_scr[unit % 2, c * QB:(c + 1) * QB, :] - m)
        v = vt_scr[h * DH:(h + 1) * DH, pl.ds(key_start(slot, c), QB)]
        return fold_rows(p), dot_nn(v, p.astype(bf16))

    units = 2 * NQ
    m = None
    for unit in range(-1, units):
        if unit >= 0:
            m = jnp.max(top, axis=0, keepdims=True)
        top = total = acc = None
        for c in range(chunks):
            if unit + 1 < units:
                t = score_chunk(unit + 1, c)
                top = t if top is None else jnp.maximum(top, t)
            if unit >= 0:
                l, o = weight_chunk(unit, c, m)
                total = l if total is None else total + l
                acc = o if acc is None else acc + o
        if unit >= 0:
            h, columns, qc, slot = place(unit)
            l = jnp.sum(total, axis=0, keepdims=True)
            ctx_scr[h * DH:(h + 1) * DH, columns] = acc / l
            lse_ref[0, h:h + 1, columns] = m + jnp.log(l)
    ctx = ctx_scr[...].T
    ctx_low = ctx.astype(bf16)
    ctx_ref[...] = ctx_low
    rest_ref[...] = (ctx - ctx_low.astype(f32)).astype(bf16)


def attention_forward(meta, q, kv, qaug, kaug, bias, first, pairs):
    own = pl.BlockSpec((ROWS, TILE), lambda i, meta: (0, first + i))
    out = pl.BlockSpec((ROWS, TILE), lambda i, meta: (0, i))
    keys = pl.BlockSpec((KROWS, TILE), lambda i, meta: (0, 2 * (first + i)))
    values = pl.BlockSpec((KROWS, TILE), lambda i, meta: (0, 2 * (first + i) + 1))
    fixed = lambda rows: pl.BlockSpec((rows, TILE), lambda i, meta: (0, 0))
    return pl.pallas_call(
        forward_kernel,
        grid_spec=pltpu.PrefetchScalarGridSpec(
            num_scalar_prefetch=1,
            grid=(pairs,),
            in_specs=[own, keys, values, fixed(ROWS), fixed(KROWS),
                      pl.BlockSpec((2, 5 * TILE, TILE), lambda i, meta: (first + i, 0, 0))],
            out_specs=[out, out, pl.BlockSpec((1, 2, ROWS), lambda i, meta: (i, 0, 0))],
            scratch_shapes=[
                pltpu.VMEM((2, ROWS, 2 * TILE), bf16),
                pltpu.VMEM((TILE, KROWS), bf16),
                pltpu.VMEM((2, PLEN + CLEN, QB), f32),
                pltpu.VMEM((TILE, ROWS), f32),
            ],
        ),
        out_shape=[jax.ShapeDtypeStruct((ROWS, pairs * TILE), bf16),
                   jax.ShapeDtypeStruct((ROWS, pairs * TILE), bf16),
                   jax.ShapeDtypeStruct((pairs, 2, ROWS), f32)],
        compiler_params=pltpu.CompilerParams(dimension_semantics=("arbitrary",),
                                             vmem_limit_bytes=56 << 20),
        cost_estimate=pl.CostEstimate(flops=pairs * 5_000_000_000, bytes_accessed=pairs * 2_000_000,
                                      transcendentals=pairs * 2 * ROWS * (PLEN + CLEN)),
        name="attention_forward",
    )(meta, q, kv, kv, qaug, kaug, bias)


PAD = TILE


def backward_kernel(meta, q_ref, k_ref, v_ref, do_ref, ctx_ref, rest_ref, lse_ref, qaug_ref, kaug_ref,
                    bias_ref, pick_ref, dq_ref, dkv_ref, near_ref,
                    kt_scr, q_scr, wide_scr, do_scr, delta_scr, ds_scr, p_scr, dks_scr, dvs_scr, far_scr):
    low_q = low_lanes((ROWS, TILE))
    kt_scr[...] = k_ref[...].T
    zero = jnp.zeros((ROWS, TILE), bf16)
    for h in range(2):
        q = q_ref[...]
        aug = qaug_ref[...]
        q_scr[h] = jnp.where(low_q, q, aug) if h == 0 else jnp.where(low_q, aug, q)
        wide_scr[h, :, :TILE] = jnp.where(low_q, q, zero) if h == 0 else jnp.where(low_q, zero, q)
        wide_scr[h, :, TILE:] = aug
        do = jnp.where(low_q, do_ref[...], zero) if h == 0 else jnp.where(low_q, zero, do_ref[...])
        for qb in range(NQ):
            do_scr[qb, h] = do[qb * QB:(qb + 1) * QB]
    prod = do_ref[...].astype(f32) * (ctx_ref[...].astype(f32) + rest_ref[...].astype(f32))
    hi = prod.astype(bf16)
    lo = (prod - hi.astype(f32)).astype(bf16)
    pick_row = lax.broadcasted_iota(jnp.int32, (8, TILE), 0)
    pick_low = low_lanes((8, TILE))
    pick = jnp.where((pick_row == 0) & pick_low | (pick_row == 1) & ~pick_low, 1.0, 0.0).astype(bf16)
    delta_scr[...] = dot_nt(pick, hi) + dot_nt(pick, lo)
    for h in range(2):
        ds_scr[h, 0:PAD, :] = jnp.zeros((PAD, ROWS), bf16)
        ds_scr[h, PAD + PLEN + CLEN:, :] = jnp.zeros((PAD, ROWS), bf16)

    def piece(h, kk, vv, kc, qb):
        cols = slice(qb * QB, (qb + 1) * QB)
        s = dot_nt(kk, wide_scr[h, cols, :])
        qc = meta[qb]
        s = add_bias(s, bias_ref, h, kc, (qc, qc + 1))
        p = jnp.exp(s - lse_ref[0, h:h + 1, cols])
        dp = dot_nt(vv, do_scr[qb, h])
        ds = (p * (dp - delta_scr[h:h + 1, cols])).astype(bf16)
        return p.astype(bf16), ds

    low_c = low_lanes((QB, TILE))

    def prompt_chunk(c, carry):
        start = c * QB
        rows = pl.ds(start, QB)
        kk = jnp.concatenate([k_ref[rows, :], kaug_ref[rows, :]], axis=1)
        vv = v_ref[rows, :]
        buffer = c % 2
        for h in range(2):
            for qb in range(NQ):
                cols = slice(qb * QB, (qb + 1) * QB)
                p, ds = piece(h, kk, vv, 2 * c, qb)
                ds_scr[h, pl.ds(PAD + start, QB), cols] = ds
                p_scr[buffer, :, (2 * qb + h) * QB:(2 * qb + h + 1) * QB] = p
        dv = dot_nn(p_scr[buffer], do_scr[...].reshape(2 * ROWS, TILE))
        dks = [dot_nn(ds_scr[h, pl.ds(PAD + start, QB), :], q_scr[h]) for h in range(2)]
        dkv_ref[rows, TILE:] = dv.astype(bf16)
        dkv_ref[rows, :TILE] = jnp.where(low_c, dks[0], dks[1]).astype(bf16)
        sums = jnp.where(low_c, dks[1], dks[0])
        far_scr[2 * c] = fold_rows(sums[:TILE])
        far_scr[2 * c + 1] = fold_rows(sums[TILE:])
        return carry

    for c in range(PLEN // QB):
        prompt_chunk(c, 0)
    for qb in range(NQ):
        cols = slice(qb * QB, (qb + 1) * QB)
        slot = pl.multiple_of(PLEN + meta[NQ + qb] * CLEN, CLEN)
        for half in range(CLEN // QB):
            rows = pl.ds(pl.multiple_of(slot + half * QB, QB), QB)
            there = slice(half * QB, (half + 1) * QB)
            kk = jnp.concatenate([k_ref[rows, :], kaug_ref[rows, :]], axis=1)
            vv = v_ref[rows, :]
            ps = []
            for h in range(2):
                p, ds = piece(h, kk, vv, 8 + 2 * half, qb)
                ds_scr[h, PAD + PLEN + half * QB:PAD + PLEN + (half + 1) * QB, cols] = ds
                ps.append(p)
                dks_scr[qb, h, there, :] = dot_nn(ds, q_scr[h, cols, :])
            dvs_scr[qb, there, :] = dot_nn(jnp.concatenate(ps, axis=1), do_scr[qb].reshape(2 * QB, TILE))
    for slot in range(2):
        for half in range(CLEN // TILE):
            there = slice(half * TILE, (half + 1) * TILE)
            rows = slice(PLEN + slot * CLEN + half * TILE, PLEN + slot * CLEN + (half + 1) * TILE)
            totals = [None] * 3
            for qb in range(NQ):
                mine = meta[NQ + qb] == slot
                parts = (dvs_scr[qb, there, :], dks_scr[qb, 0, there, :], dks_scr[qb, 1, there, :])
                for i, part in enumerate(parts):
                    part = jnp.where(mine, part, 0.0)
                    totals[i] = part if totals[i] is None else totals[i] + part
            dkv_ref[rows, TILE:] = totals[0].astype(bf16)
            low_t = low_lanes((TILE, TILE))
            dkv_ref[rows, :TILE] = jnp.where(low_t, totals[1], totals[2]).astype(bf16)
            far_scr[8 + slot * (CLEN // TILE) + half] = fold_rows(jnp.where(low_t, totals[2], totals[1]))

    dqt = []
    for h in range(2):
        parts = []
        for qb in range(NQ):
            cols = slice(qb * QB, (qb + 1) * QB)
            slot = pl.multiple_of(PLEN + meta[NQ + qb] * CLEN, CLEN)
            rows = slice(h * DH, (h + 1) * DH)
            keys = jnp.concatenate([kt_scr[rows, 0:PLEN], kt_scr[rows, pl.ds(slot, CLEN)]], axis=1)
            parts.append(dot_nn(keys, ds_scr[h, PAD:PAD + PLEN + CLEN, cols]))
        dqt.append(jnp.concatenate(parts, axis=1))
    dq_ref[...] = jnp.concatenate(dqt, axis=0).T.astype(bf16)

    row_id = lax.broadcasted_iota(jnp.int32, (TILE, TILE), 0)
    lane_id = lax.broadcasted_iota(jnp.int32, (TILE, TILE), 1)
    flip = jnp.where(row_id + lane_id == TILE - 1, 1.0, 0.0).astype(bf16)
    flips = jnp.concatenate([flip, flip], axis=0)
    for h in range(2):
        acc = None
        for qb in range(NQ):
            tiles = [ds_scr[h, pl.ds(pl.multiple_of((meta[qb] + half) * TILE, TILE), 3 * TILE),
                            (2 * qb + half) * TILE:(2 * qb + half + 1) * TILE] for half in range(2)]
            part = dot_nn(jnp.concatenate(tiles, axis=1), flips)
            acc = part if acc is None else acc + part
        sums = []
        for d in range(3):
            rolled = pltpu.roll(acc[d * TILE:(d + 1) * TILE], 0, 1, stride=1, stride_axis=0)
            wrapped = jnp.where(lane_id < row_id, rolled, 0.0)
            sums += [fold_rows(rolled), fold_rows(wrapped)]
        for side in range(2):
            total = None
            for t in range(16):
                term = far_scr[t] * pick_ref[h, side, t]
                total = term if total is None else total + term
            sums.append(total)
        for i, eight in enumerate(sums):
            near_ref[0, h, i] = eight


def attention_backward(meta, q, kv, do, ctx, rest, lse, qaug, kaug, bias, pick, first, pairs):
    own = pl.BlockSpec((ROWS, TILE), lambda i, meta: (0, first + i))
    keys = pl.BlockSpec((KROWS, TILE), lambda i, meta: (0, 2 * (first + i)))
    values = pl.BlockSpec((KROWS, TILE), lambda i, meta: (0, 2 * (first + i) + 1))
    fixed = lambda rows: pl.BlockSpec((rows, TILE), lambda i, meta: (0, 0))
    return pl.pallas_call(
        backward_kernel,
        grid_spec=pltpu.PrefetchScalarGridSpec(
            num_scalar_prefetch=1,
            grid=(pairs,),
            in_specs=[own, keys, values, own, own, own,
                      pl.BlockSpec((1, 2, ROWS), lambda i, meta: (first + i, 0, 0)),
                      fixed(ROWS), fixed(KROWS),
                      pl.BlockSpec((2, 5 * TILE, TILE), lambda i, meta: (first + i, 0, 0)),
                      pl.BlockSpec((2, 2, 16, 8, TILE), lambda i, meta: (0, 0, 0, 0, 0))],
            out_specs=[pl.BlockSpec((ROWS, TILE), lambda i, meta: (0, i)),
                       pl.BlockSpec((KROWS, 2 * TILE), lambda i, meta: (0, i)),
                       pl.BlockSpec((1, 2, 8, 8, TILE), lambda i, meta: (i, 0, 0, 0, 0))],
            scratch_shapes=[
                pltpu.VMEM((TILE, KROWS), bf16),
                pltpu.VMEM((2, ROWS, TILE), bf16),
                pltpu.VMEM((2, ROWS, 2 * TILE), bf16),
                pltpu.VMEM((NQ, 2, QB, TILE), bf16),
                pltpu.VMEM((8, ROWS), f32),
                pltpu.VMEM((2, PLEN + CLEN + 2 * PAD, ROWS), bf16),
                pltpu.VMEM((2, QB, 2 * ROWS), bf16),
                pltpu.VMEM((NQ, 2, CLEN, TILE), f32),
                pltpu.VMEM((NQ, CLEN, TILE), f32),
                pltpu.VMEM((16, 8, TILE), f32),
            ],
        ),
        out_shape=[jax.ShapeDtypeStruct((ROWS, pairs * TILE), bf16),
                   jax.ShapeDtypeStruct((KROWS, 2 * pairs * TILE), bf16),
                   jax.ShapeDtypeStruct((pairs, 2, 8, 8, TILE), f32)],
        compiler_params=pltpu.CompilerParams(dimension_semantics=("arbitrary",),
                                             vmem_limit_bytes=56 << 20),
        cost_estimate=pl.CostEstimate(flops=pairs * 10_000_000_000, bytes_accessed=pairs * 3_000_000,
                                      transcendentals=pairs * 2 * ROWS * (PLEN + CLEN)),
        name="attention_backward",
    )(meta, q, kv, kv, do, ctx, rest, lse, qaug, kaug, bias, pick)


EPSILON = 1e-06
THRESHOLDS = (12, 16, 23, 32, 46, 64, 91)
OWNER_BLOCK = (0, 3, 1, 2)


def python_bucket(offset):
    magnitude = abs(offset)
    base = NB // 2 if offset > 0 else 0
    if magnitude < 8:
        return base + magnitude
    return base + 8 + sum(1 for edge in THRESHOLDS if magnitude >= edge)


def bias_spread():
    spread = np.zeros((8, TILE, NB), np.float32)
    for lane in range(TILE):
        for d in range(3):
            inside = python_bucket(TILE * (d - 1) + lane - (TILE - 1))
            passed = python_bucket(TILE * d + lane - (TILE - 1))
            spread[2 * d, lane, inside] += 1
            spread[2 * d + 1, lane, passed] += 1
            spread[2 * d + 1, lane, inside] -= 1
    spread[6, :, python_bucket(-200)] = 1
    spread[7, :, python_bucket(200)] = 1
    return spread.reshape(8 * TILE, NB)


def setup_kernel(meta, limit, table, bias_ref, qaug_ref, kaug_ref, far_ref):
    head = pl.program_id(0)
    heads = pl.num_programs(0)
    near = (lax.broadcasted_iota(jnp.int32, (TILE, TILE), 0)
            - lax.broadcasted_iota(jnp.int32, (TILE, TILE), 1))
    for d in range(-2, 3):
        first, last = TILE * d - TILE + 1, TILE * d + TILE - 1
        previous = python_bucket(first)
        tile = jnp.full((TILE, TILE), table[previous * heads + head], f32)
        for n in range(first + 1, last + 1):
            current = python_bucket(n)
            if current != previous:
                tile = jnp.where(near >= n - TILE * d, table[current * heads + head], tile)
                previous = current
        bias_ref[0, (d + 2) * TILE:(d + 3) * TILE, :] = tile

    @pl.when(head == 0)
    def _():
        shape = (ROWS, TILE)
        sub = lax.broadcasted_iota(jnp.int32, shape, 1) & (DH - 1)
        qaug_ref[...] = jnp.where(sub == lax.broadcasted_iota(jnp.int32, shape, 0) // TILE, 1.0, 0.0).astype(bf16)
        shape = (KROWS, TILE)
        key = lax.broadcasted_iota(jnp.int32, shape, 0)
        sub = lax.broadcasted_iota(jnp.int32, shape, 1) & (DH - 1)
        kaug = jnp.zeros(shape, f32)
        for q in range(NQ):
            first = PLEN + CLEN * meta[NQ + q]
            hidden = (key >= PLEN) & ((key < first) | (key >= first + limit[q]))
            kaug = jnp.where(((sub == 2 * q) | (sub == 2 * q + 1)) & hidden, NEGATIVE, kaug)
        kaug_ref[...] = kaug.astype(bf16)
        lane = lax.broadcasted_iota(jnp.int32, (8, TILE), 1)
        for h in range(2):
            for row in range(16):
                key_tile = row if row < 8 else 8 + (row - 8) % 4
                for side in range(2):
                    out = jnp.zeros((8, TILE), f32)
                    for q in range(2 * NQ):
                        apart = key_tile - (meta[q // 2] + q % 2)
                        is_far = (apart <= -2) if side == 0 else (apart >= 2)
                        out = jnp.where(lane == q + (DH if h == 0 else 0), jnp.where(is_far, 1.0, 0.0), out)
                    far_ref[h, side, row] = out


def setup(me, spans, table):
    block = NQ * me + jnp.arange(NQ, dtype=jnp.int32)
    prompt = block < PLEN // QB
    cont = jnp.maximum(block - PLEN // QB, 0) // 2
    half = jnp.maximum(block - PLEN // QB, 0) % 2
    tile = jnp.where(prompt, 2 * block, PLEN // TILE + 2 * half)
    slot = jnp.where(prompt, 0, cont - (me - 1))
    chosen = cont[:, None] == jnp.arange(CONT, dtype=jnp.int32)[None, :]
    limit = jnp.where(prompt, 0, jnp.sum(jnp.where(chosen, spans[None, :], 0), axis=1)).astype(jnp.int32)
    meta = jnp.concatenate([tile, slot]).astype(jnp.int32)
    heads = table.shape[1]
    whole = lambda *shape: pl.BlockSpec(shape, lambda i, *_: (0,) * len(shape))
    bias, qaug, kaug, far = pl.pallas_call(
        setup_kernel,
        grid_spec=pltpu.PrefetchScalarGridSpec(
            num_scalar_prefetch=3,
            grid=(heads,),
            in_specs=[],
            out_specs=[pl.BlockSpec((1, 5 * TILE, TILE), lambda i, *_: (i, 0, 0)),
                       whole(ROWS, TILE), whole(KROWS, TILE), whole(2, 2, 16, 8, TILE)],
        ),
        out_shape=[jax.ShapeDtypeStruct((heads, 5 * TILE, TILE), f32),
                   jax.ShapeDtypeStruct((ROWS, TILE), bf16),
                   jax.ShapeDtypeStruct((KROWS, TILE), bf16),
                   jax.ShapeDtypeStruct((2, 2, 16, 8, TILE), f32)],
        compiler_params=pltpu.CompilerParams(dimension_semantics=("arbitrary",)),
        cost_estimate=pl.CostEstimate(flops=30_000_000, bytes_accessed=5_000_000, transcendentals=0),
        name="setup",
    )(meta, limit, table.astype(f32).reshape(-1))
    return meta, bias, qaug, kaug, far


def by_rows(x):
    return with_layout_constraint(x, Layout(tuple(range(x.ndim))))


def rms(rows):
    return lax.rsqrt(jnp.mean(rows * rows, axis=1, keepdims=True) + EPSILON)


def normed_rows(rows, gain):
    rows = rows.astype(f32)
    return (rows * rms(rows) * gain).astype(bf16)


def contract_rows(left, right):
    return lax.dot_general(left, right, (((0,), (0,)), ((), ())), preferred_element_type=f32)


def block_of(rows, i):
    return rows[i * QB:(i + 1) * QB]


def send(rows, pairs):
    return lax.ppermute(rows, "seq", pairs)


def pick_by(me, *choices):
    out = choices[-1]
    for i in range(len(choices) - 2, -1, -1):
        out = jnp.where(me == i, choices[i], out)
    return out


def exchange_rows(me, own):
    low, high = own[:ROWS // 2], own[ROWS // 2:]
    return (send(jnp.where(me == 2, high, low), [(0, 1), (1, 0), (2, 3), (3, 2)]),
            send(jnp.where(me == 0, high, low), [(0, 2), (1, 3)]))


def exchange_again(me, own, across, down):
    low, high = own[:ROWS // 2], own[ROWS // 2:]
    return (send(jnp.where(me == 0, high, down), [(0, 1), (2, 3), (3, 2)]),
            send(jnp.where(me == 0, low, across), [(0, 2), (1, 3)]))


def seen_rows(me, own, got):
    across, down, across_again, down_again = got
    mine = [block_of(own, i) for i in range(NQ)]
    low, high = own[:ROWS // 2], own[ROWS // 2:]
    prompt = [
        pick_by(me, low, across, down_again, down_again),
        pick_by(me, high, across_again, down, across_again),
        pick_by(me, across[:QB], mine[0], across_again[:QB], down[:QB]),
    ]
    slots = [
        pick_by(me, mine[0], mine[1], mine[0], across[ROWS // 2 - QB:]),
        pick_by(me, mine[1], mine[2], mine[1], mine[0]),
        pick_by(me, mine[1], mine[1], mine[2], mine[1]),
        pick_by(me, mine[2], mine[2], across[:QB], mine[2]),
    ]
    return jnp.concatenate(prompt + slots, axis=0)


def halve(rows, bit, axis, pairs):
    n, r, c = rows.shape
    parts = rows.reshape(n, 2, r // 2, c)
    away = lax.dynamic_index_in_dim(parts, 1 - bit, 1, keepdims=False)
    kept = lax.dynamic_index_in_dim(parts, bit, 1, keepdims=False)
    got = lax.ppermute(away, axis, pairs)
    return (kept.astype(f32) + got.astype(f32)).astype(bf16)


def join(rows, bit, axis, pairs):
    got = lax.ppermute(rows, axis, pairs)
    return jnp.concatenate([jnp.where(bit == 0, rows, got), jnp.where(bit == 0, got, rows)], axis=-2)


def seq_bits(me, order):
    steps = {"x": (me % 2, [(i, i ^ 1) for i in range(4)]), "y": (me // 2, [(i, i ^ 2) for i in range(4)])}
    return [steps[name] for name in order]


class Owned:
    def __init__(self, grad, me, order):
        self.step, self.steps = 0, seq_bits(me, order)
        self.rows = grad
        if lax.axis_size("wshard") != 8:
            self.rows = quarter_sum(lax.psum_scatter(grad, "wshard", scatter_dimension=0, tiled=True))
            self.step = 5

    def advance(self):
        place = lax.axis_index("wshard")
        flip = lambda bit: [(i, i ^ bit) for i in range(8)]
        step, rows = self.step, self.rows
        if step == 0:
            rows = halve(rows.reshape(4, -1, rows.shape[1]), place % 2, "wshard", flip(1))
        elif step in (1, 2):
            rows = halve(rows, self.steps[step - 1][0], "seq", self.steps[step - 1][1])
        elif step == 3:
            rows = halve(rows.reshape(1, -1, rows.shape[2]), place // 4, "wshard", flip(4))
        elif step == 4:
            rows = halve(rows, place // 2 % 2, "wshard", flip(2))[0]
        self.step, self.rows = step + 1, rows

    def finish(self):
        while self.step < 5:
            self.advance()
        return self.rows


def beside(rows, bit, axis, pairs, dim):
    got = lax.ppermute(rows, axis, pairs)
    return jnp.stack([jnp.where(bit == 0, rows, got), jnp.where(bit == 0, got, rows)], axis=dim)


class Gathered:
    def __init__(self, me, w_ff, w_out):
        self.plain = lax.axis_size("wshard") != 8
        if self.plain:
            self.state = [lax.all_gather(w, "wshard", axis=0, tiled=True) for w in (w_ff, w_out)]
            return
        place = lax.axis_index("wshard")
        self.core, self.depth = place % 2, place // 2
        self.n, self.m = w_ff.shape[0] // 4, w_out.shape[0] // 4
        self.cut = 2 * self.n // 3
        quarter = jnp.concatenate([lax.dynamic_slice_in_dim(w_ff, me * self.n, self.n, 0),
                                   lax.dynamic_slice_in_dim(w_out, me * self.m, self.m, 0)], axis=0)
        self.state = [quarter] + [
            lax.ppermute(quarter, "wshard", [(i, ((i // 2 + k) % 4) * 2 + i % 2) for i in range(8)])
            for k in range(1, 4)]
        self.steps = [seq_bits(me, "xy"), seq_bits(me, "yx")]

    def exchange(self, i):
        if self.plain:
            return
        if i == 0:
            rows = jnp.stack([pick_by((self.depth - d) % 4, *self.state) for d in range(4)])
            self.state = [rows[:, :self.cut], rows[:, self.cut:]]
        self.state = [beside(rows, steps[i][0], "seq", steps[i][1], dim)
                      for rows, steps, dim in zip(self.state, self.steps, (1, 1 + i))]

    def cores(self):
        if not self.plain:
            rows = jnp.concatenate(self.state, axis=-2)
            self.state = [beside(rows, self.core, "wshard", [(i, i ^ 1) for i in range(8)], 1)]

    def tie(self, others):
        others, self.state = lax.optimization_barrier((others, self.state))
        return others

    def whole(self):
        if self.plain:
            return self.state
        rows = self.state[0]
        c = rows.shape[-1]
        return rows[..., :self.n, :].reshape(32 * self.n, c), rows[..., self.n:, :].reshape(32 * self.m, c)


def quarter_sum(rows):
    parts = lax.all_to_all(rows.reshape(4, -1, rows.shape[1]), "seq", split_axis=0, concat_axis=0, tiled=True)
    return jnp.sum(parts.astype(f32), axis=0).astype(bf16)


def join_quarters(rows, me):
    steps = seq_bits(me, "xy")
    rows = beside(rows, *steps[0][:1], "seq", steps[0][1], 0)
    return beside(rows, steps[1][0], "seq", steps[1][1], 0).reshape((4,) + rows.shape[1:])


def sum_prompt(me, partial):
    owner = jnp.array(OWNER_BLOCK, jnp.int32)

    def take(device):
        start = owner[device] * QB
        return lax.dynamic_slice_in_dim(partial, start, QB, 0)

    total = take(me).astype(f32)
    for flip in (1, 2, 3):
        total = total + send(take(me ^ flip), [(i, i ^ flip) for i in range(4)]).astype(f32)
    parts = [block_of(partial, i) for i in range(8)]
    crossed = send(jnp.where(me == 2, parts[7], parts[4]), [(2, 3), (3, 2)])
    zero = jnp.zeros_like(parts[0])
    joined = (jnp.where(me == 2, parts[6], parts[5]).astype(f32) + crossed.astype(f32)).astype(bf16)
    rows = [
        total.astype(bf16),
        pick_by(me, zero, zero, parts[4], joined),
        pick_by(me, zero, parts[4], parts[5], parts[6]),
        pick_by(me, zero, parts[5], joined, parts[7]),
    ]
    return jnp.concatenate(rows, axis=0)


CHUNKS = (4, 2)


def interleave(key_part, value_part):
    r, w = key_part.shape
    both = jnp.stack([key_part.reshape(r, w // TILE, TILE), value_part.reshape(r, w // TILE, TILE)], axis=2)
    return both.reshape(r, 2 * w)


def local(tokens, teacher, lengths, w_query, w_key, w_value, w_out, w_in, w_ff, gain_attn, gain_ff, bias_table):
    me = lax.axis_index("seq")
    own = by_rows(tokens[0])
    inputs = own.astype(f32)
    targets = teacher[0].astype(f32)
    spans = lengths[0]
    width = own.shape[1]
    pairs = width // TILE

    def gather(w):
        return lax.all_gather(w, "wshard", axis=0, tiled=True)

    w_kv = interleave(w_key, w_value)
    gain_columns = jnp.pad(jnp.stack([gain_attn, gain_ff], axis=1), ((0, 0), (0, TILE - 2)))
    first = gather(jnp.concatenate([w_query, w_kv, gain_columns], axis=1))
    full_query, full_kv = first[:, :width], first[:, width:3 * width]
    gains = first[:, 3 * width:3 * width + 2].astype(f32).T
    gain_one, gain_two = gains[0], gains[1]
    gathered = Gathered(me, w_ff, w_out)
    full_in = gather(w_in)
    got = exchange_rows(me, own)
    got, spans, table = lax.optimization_barrier((got, spans, bias_table))
    got = got + exchange_again(me, own, *got)
    prepared = setup(me, spans, table)
    inverse_one = rms(inputs)
    got, prepared, inverse_one = gathered.tie((got, prepared, inverse_one))
    meta, bias, qaug, kaug, far = prepared
    gathered.exchange(0)
    normed_own = by_rows((inputs * inverse_one * gain_one).astype(bf16))
    seen = by_rows(seen_rows(me, own, got))
    queries = jnp.dot(normed_own, full_query, preferred_element_type=f32).astype(bf16)
    queries, seen = gathered.tie((queries, seen))
    gathered.exchange(1)
    normed_seen = by_rows(normed_rows(seen, gain_one))
    keys_values = jnp.dot(normed_seen, full_kv, preferred_element_type=f32).astype(bf16)
    meta, queries, keys_values = gathered.tie((meta, queries, keys_values))
    gathered.cores()
    context, rest, lse = gathered.tie(attention_forward(meta, queries, keys_values, qaug, kaug, bias, 0, pairs))
    full_ff, full_out = gathered.whole()
    middle = by_rows(inputs + jnp.dot(context, full_out, preferred_element_type=f32))
    inverse_two = rms(middle)
    normed_two = by_rows((middle * inverse_two * gain_two).astype(bf16))
    hidden_act = jnp.maximum(jnp.dot(normed_two, full_in, preferred_element_type=f32), 0.0).astype(bf16)
    final_rows = middle + jnp.dot(hidden_act, full_ff, preferred_element_type=f32)
    local_rows = inputs.shape[0]
    row_index = me * local_rows + lax.iota(jnp.int32, local_rows)
    slot_index = jnp.maximum(row_index - PLEN, 0)
    owner_match = (slot_index // CLEN)[:, None] == lax.iota(jnp.int32, CONT)[None, :]
    row_limit = jnp.sum(jnp.where(owner_match, spans[None, :], 0), axis=1)
    valid_rows = (row_index < PLEN) | (slot_index % CLEN < row_limit)
    row_count = PLEN + jnp.sum(spans).astype(f32)
    factor = (PLEN + CONT * CLEN) / row_count
    d_final = jnp.where(valid_rows[:, None], factor * (final_rows - targets), 0.0)
    d_final = by_rows(d_final)
    d_branch_two = by_rows(d_final.astype(bf16))

    def owners(g):
        return lax.psum_scatter(g, "wshard", scatter_dimension=0, tiled=True)

    size = gain_attn.shape[0]
    share_ff = owners(by_rows(contract_rows(hidden_act, d_branch_two).astype(bf16)))
    d_pre = jnp.where(hidden_act > 0, dot_nt(d_branch_two, full_ff), 0.0).astype(bf16)
    share_in = owners(by_rows(contract_rows(normed_two, d_pre).astype(bf16)))
    d_normed_two = by_rows(dot_nt(d_pre, full_in))
    scaled_two = middle * inverse_two
    d_scaled_two = d_normed_two * gain_two
    d_middle = d_final + inverse_two * (
        d_scaled_two - scaled_two * jnp.mean(d_scaled_two * scaled_two, axis=1, keepdims=True))
    d_middle = by_rows(d_middle)
    d_branch_one = by_rows(d_middle.astype(bf16))
    grad_out = contract_rows(context, d_branch_one).astype(bf16)
    d_context = dot_nt(d_branch_one, full_out).astype(bf16)
    d_context, grad_out = lax.optimization_barrier((d_context, grad_out))

    starts = [sum(CHUNKS[:i]) for i in range(len(CHUNKS))]
    cuts = [(starts[i] * TILE, (starts[i] + CHUNKS[i]) * TILE) for i in range(len(CHUNKS))]

    def backward(meta, i):
        return attention_backward(meta, queries, keys_values, d_context, context, rest, lse, qaug, kaug, bias, far,
                                  starts[i], CHUNKS[i])

    def weight_grad(d_q, d_kv):
        return [by_rows(contract_rows(normed_own, d_q).astype(bf16)),
                by_rows(contract_rows(normed_seen, d_kv).astype(bf16))]

    def query_rows(i, d_q):
        return by_rows(dot_nt(d_q, full_query[:, cuts[i][0]:cuts[i][1]]))

    def key_rows(i, d_kv):
        return by_rows(dot_nt(d_kv, full_kv[:, 2 * cuts[i][0]:2 * cuts[i][1]]))

    first = backward(meta, 0)
    meta, first, share_ff = lax.optimization_barrier((meta, first, share_ff))
    share_first = owners(jnp.concatenate(weight_grad(*first[:2]) + [grad_out], axis=1))
    f_query = query_rows(0, first[0])
    f_part = by_rows(key_rows(0, first[1]).astype(bf16))
    meta, f_query, f_part = lax.optimization_barrier((meta, f_query, f_part))
    f_first = sum_prompt(me, f_part)
    second = backward(meta, 1)
    second, f_first, share_in = lax.optimization_barrier((second, f_first, share_in))
    heads = bias_table.shape[1]
    near = jnp.sum(jnp.concatenate([first[2], second[2]], axis=0), axis=3).reshape(heads, 8 * TILE)
    bias_local = jnp.dot(near, jnp.asarray(bias_spread()), precision=lax.Precision.HIGHEST).reshape(-1, TILE)
    bias_top = bias_local.astype(bf16)
    bias_rest = (bias_local - bias_top.astype(f32)).astype(bf16)
    n_bias = bias_local.shape[0]
    size = gain_attn.shape[0]
    bias_columns = jnp.pad(jnp.concatenate([bias_top, bias_rest], axis=0), ((0, max(0, size - 2 * n_bias)), (0, 0)))
    bias_rows = bias_columns.shape[0]
    blocks = jnp.concatenate(weight_grad(*second[:2]), axis=1)
    n_last = blocks.shape[1]
    blocks = blocks.reshape(-1, size, n_last)
    if bias_rows > size:
        blocks = jnp.pad(blocks, ((0, 0), (0, bias_rows - size), (0, 0)))
    last = jnp.concatenate([blocks, jnp.broadcast_to(bias_columns[None], (blocks.shape[0],) + bias_columns.shape)],
                           axis=2).reshape(-1, n_last + TILE)
    owned_last = Owned(by_rows(last), me, "yx")
    owned_last.advance()
    f_query = f_query + query_rows(1, second[0])
    d_kv = sum_prompt(me, second[1])
    owned_last.advance()
    x_step, y_step = [(bit, "seq", pairs) for bit, pairs in seq_bits(me, "xy")]

    def flat(*shares):
        return jnp.concatenate([share.reshape(-1, width) for share in shares], axis=0)

    quarter_early = quarter_sum(flat(share_ff, share_in))
    f_total = f_first.astype(f32) + key_rows(1, d_kv)
    f_block = f_total[:QB].astype(bf16)
    owned_last.advance()
    owned_last.advance()
    owned_last.advance()
    quarter_first = quarter_sum(flat(share_first))
    owned_last.rows, quarter_early, quarter_first, f_total = lax.optimization_barrier((owned_last.rows, quarter_early, quarter_first, f_total))
    from_two = send(f_block, [(2, 0)])
    from_three = send(f_block, [(3, 0)])
    f_own = f_query + f_total[QB:] + jnp.concatenate(
        [jnp.where(me < 2, f_block, jnp.zeros_like(f_block)), from_two, from_three], axis=0).astype(f32)
    scaled_one = inputs * inverse_one
    d_scaled_one = f_own * gain_one
    d_tokens = d_middle + inverse_one * (
        d_scaled_one - scaled_one * jnp.mean(d_scaled_one * scaled_one, axis=1, keepdims=True))

    half_early = beside(quarter_early, *x_step, 0)
    early = beside(half_early, *y_step, 0).reshape(-1, width).astype(f32)
    n_ff = share_ff.shape[0]
    share_ff, share_in = early[:n_ff], early[n_ff:].reshape(size, -1)
    late = join_quarters(owned_last.finish(), me).reshape(bias_rows if bias_rows > size else size, -1).astype(f32)
    share_first = join_quarters(quarter_first, me).reshape(size, -1).astype(f32)
    share_out = share_first[:, -width:]
    shares = [share_first[:, :-width], late[:size, :n_last]]
    bias_grad = (late[:n_bias, n_last:] + late[n_bias:2 * n_bias, n_last:]).reshape(heads, NB).T
    share_query = jnp.concatenate(
        [share[:, :count * TILE] for share, count in zip(shares, CHUNKS)], axis=1)
    share_kv = jnp.concatenate(
        [share[:, count * TILE:] for share, count in zip(shares, CHUNKS)], axis=1)
    share_kv = share_kv.reshape(share_kv.shape[0], pairs, 2, TILE)
    share_key = share_kv[:, :, 0].reshape(-1, width)
    share_value = share_kv[:, :, 1].reshape(-1, width)
    gain_grad_one = (jnp.sum(share_query * w_query.astype(f32), axis=1)
                     + jnp.sum(share_key * w_key.astype(f32), axis=1)
                     + jnp.sum(share_value * w_value.astype(f32), axis=1)) / gain_attn.astype(f32)
    gain_grad_two = jnp.sum(share_in * w_in.astype(f32), axis=1) / gain_ff.astype(f32)
    return (
        final_rows.astype(bf16)[None],
        d_tokens[None],
        share_query,
        share_key,
        share_value,
        share_out,
        share_in,
        share_ff,
        gain_grad_one,
        gain_grad_two,
        bias_grad,
    )


def solution(mesh):
    rows = P("wshard", "seq", None)
    weight = P("wshard", None)
    placed = (rows, rows) + (weight,) * 7 + (P("wshard"), P("wshard"), P())
    return jax.shard_map(
        local,
        mesh=mesh,
        in_specs=placed,
        out_specs=(rows, rows) + (weight,) * 6 + (P("wshard"), P("wshard"), P()),
        check_vma=False,
    )
```
